32 devices in a mesh: dp: 8 (over y, x, core), fsdp: 4 (over z).
Axes of the slice: x: 2, y: 2, z: 4, core: 2. Of those that a mesh axis runs over, the one named last changes fastest.
Arguments:
- frames: bfloat16 [2, 16384, 1024], P(None, ('dp', 'fsdp')), may hold values from -6 to 6
- lengths: int32 [2, 32, 16], P(None, ('dp', 'fsdp')), may hold values from 1 to 256, 512 in all within a row
- cotangent: bfloat16 [2, 16384, 1024], P(None, ('dp', 'fsdp')), may hold values from -6 to 6
- first_gain: bfloat16 [1024], P(('dp', 'fsdp')), may hold values from 0.099609375 to 1.8984375
- qkv_weight: bfloat16 [1024, 3072], P(('dp', 'fsdp')), may hold values from -0.1875 to 0.1875
- out_weight: bfloat16 [1024, 1024], P(('dp', 'fsdp')), may hold values from -0.5 to 0.5
- second_gain: bfloat16 [1024], P(('dp', 'fsdp')), may hold values from 0.099609375 to 1.8984375
- up_weight: bfloat16 [1024, 4096], P(('dp', 'fsdp')), may hold values from -0.1875 to 0.1875
- up_bias: bfloat16 [4096], P(('dp', 'fsdp')), may hold values from -3 to 3
- down_weight: bfloat16 [4096, 1024], P(('dp', 'fsdp')), may hold values from -0.09375 to 0.09375
- down_bias: bfloat16 [1024], P(('dp', 'fsdp')), may hold values from -3 to 3
Outputs:
- outputs: bfloat16 [2, 16384, 1024], P(None, ('dp', 'fsdp'))
- frames_grad: float32 [2, 16384, 1024], P(None, ('dp', 'fsdp'))
- first_gain_grad: float32 [1024], P(('dp', 'fsdp'))
- qkv_weight_grad: float32 [1024, 3072], P(('dp', 'fsdp'))
- out_weight_grad: float32 [1024, 1024], P(('dp', 'fsdp'))
- second_gain_grad: float32 [1024], P(('dp', 'fsdp'))
- up_weight_grad: float32 [1024, 4096], P(('dp', 'fsdp'))
- up_bias_grad: float32 [4096], P(('dp', 'fsdp'))
- down_weight_grad: float32 [4096, 1024], P(('dp', 'fsdp'))
- down_bias_grad: float32 [1024], P(('dp', 'fsdp'))
The draws below stay inside these ranges and needn't reach their ends.
Inputs may be any that keep to these rules, and one draw needn't show every extreme that they name: In every row the 16 lengths sum to 512, and the longest is exactly 256; each entry is one item, placed in the row's micro-batch and on the row's device.
All inputs are finite; a program needn't handle non-finite values.
Results may differ from the reference program's by a relative error of at most 0.011.
Values may be sent and summed in bfloat16 or wider, within the bound.
A program may use at most 256 MiB of HBM per device.

```python
import math
import jax
import jax.numpy as jnp
import numpy as np
from jax import lax

D = 1024
HEADS = 16
FF = 4096
HEAD_DIM = 64
CAP = 512
SLOTS = 16
MB = 2
MOST = 256
ROWS = 16384
DEVICES = 32


def block_levels(stream_key, extent, split, least, high):
    def one(dim, parts):
        heights = jax.random.uniform(jax.random.fold_in(jax.random.fold_in(stream_key, 6), dim), (parts,), jnp.float32, least / len(split), high / len(split))
        return jnp.repeat(jnp.exp(heights), extent[dim] // parts).reshape((-1,) + (1,) * (len(extent) - dim - 1))

    loudness = one(*split[0])
    for cut in split[1:]:
        loudness = loudness * one(*cut)
    return loudness


def length_profile(number_of, total, most, skew):
    loads = [(1 << 20) // math.isqrt(rank ** skew) + 1 for rank in range(2, number_of + 1)]
    spare, counts = total - most - (number_of - 1), [1] * (number_of - 1)
    while spare > 0:
        candidates = [i for i in range(number_of - 1) if counts[i] < most]
        pool, remaining = sum([loads[i] for i in candidates]), spare
        for i in candidates:
            extra = min(most - counts[i], max(1, remaining * loads[i] // pool), spare)
            counts[i] = counts[i] + extra
            spare = spare - extra
    return np.array([most] + counts)


def uneven_parts(rng, number_of, total, most, lean):
    if number_of == 2:
        one = jax.random.randint(rng, (), max(1, total - most), min(most, total - 1) + 1)
        return jnp.stack([one, total - one])
    sizes = jnp.asarray(length_profile(number_of, total, most, lean), jnp.int32)
    couples = (number_of - 1) // 2
    giver, receiver = sizes[1:1 + 2 * couples:2], sizes[2:2 + 2 * couples:2]
    margin = jnp.minimum(giver - 1, most - receiver)
    passed = jax.random.randint(jax.random.fold_in(rng, 1), (couples,), 0, 1 << 20) % (margin + 1)
    sizes = sizes.at[1:1 + 2 * couples:2].set(giver - passed).at[2:2 + 2 * couples:2].set(receiver + passed)
    return sizes[jax.random.permutation(jax.random.fold_in(rng, 2), number_of)]


def noise(rng, extent, scale, bound, pieces=(), held_as=jnp.bfloat16):
    result = scale * jax.random.normal(rng, extent, jnp.float32)
    if pieces:
        result = result * block_levels(rng, extent, pieces, -0.22, 0.18)
    return jnp.clip(result, -bound, bound).astype(held_as)


def setup_inputs(seed: int = 0) -> dict:
    splits = jax.random.split(jax.random.key(seed), 12)
    frames = noise(splits[0], (MB, ROWS, D), 1.0, 6.0, ((1, 32),))
    lengths = jax.vmap(lambda own: uneven_parts(own, SLOTS, CAP, MOST, 2))(jax.random.split(splits[1], MB * DEVICES)).reshape((MB, DEVICES, SLOTS)).astype(jnp.int32)
    cotangent = noise(splits[2], (MB, ROWS, D), 1.0, 6.0, ((1, 32),))
    first_gain = jnp.clip(1.0 + 0.18 * jax.random.normal(splits[3], (D,), jnp.float32), 0.099609375, 1.8984375).astype(jnp.bfloat16)
    qkv_weight = noise(splits[4], (D, 3 * D), D ** -0.5, 0.1875, ((0, 32),))
    out_weight = noise(splits[5], (D, D), (D // 8) ** -0.5, 0.5, ((0, 32),))
    second_gain = jnp.clip(1.0 + 0.18 * jax.random.normal(splits[6], (D,), jnp.float32), 0.099609375, 1.8984375).astype(jnp.bfloat16)
    up_weight = noise(splits[7], (D, FF), D ** -0.5, 0.1875, ((0, 32),))
    up_bias = noise(splits[8], (FF,), 0.5, 3.0, ((0, 32),))
    down_weight = noise(splits[9], (FF, D), FF ** -0.5, 0.09375, ((0, 32),))
    down_bias = noise(splits[10], (D,), 0.5, 3.0, ((0, 32),))
    return dict(frames=frames, lengths=lengths, cotangent=cotangent, first_gain=first_gain, qkv_weight=qkv_weight, out_weight=out_weight, second_gain=second_gain, up_weight=up_weight, up_bias=up_bias, down_weight=down_weight, down_bias=down_bias)


EPS = 1e-06

@jax.custom_vjp
def low(v):
    return lax.optimization_barrier(v.astype(jnp.bfloat16)).astype(jnp.float32)

@jax.custom_vjp
def low_back(v):
    return v

def low_keep(v):
    return (low(v), None)

def low_pass(kept, grad):
    return (grad,)

def back_keep(v):
    return (v, None)

def back_low(kept, grad):
    return (low(grad),)
low.defvjp(low_keep, low_pass)
low_back.defvjp(back_keep, back_low)

def build_mask(span):
    ends = jnp.cumsum(span.astype(jnp.int32))
    position = jnp.arange(CAP, dtype=jnp.int32)
    segment = lax.optimization_barrier(jnp.sum((position[:, None] >= ends[None, :]).astype(jnp.int32), axis=1))
    same = segment[:, None] == segment[None, :]
    return jnp.logical_and(same, position[:, None] >= position[None, :])

def layer(x_val, mask, first_gain, qkv_weight, out_weight, second_gain, up_weight, up_bias, down_weight, down_bias):
    highest = lax.Precision.HIGHEST
    count = x_val.shape[0]
    normal_in = x_val * lax.rsqrt(lax.optimization_barrier(jnp.mean(x_val * x_val, axis=-1, keepdims=True)) + EPS)
    entered = low(normal_in * first_gain)
    project = low(low_back(jnp.dot(entered, qkv_weight, precision=highest)))
    queries = project[:, :D].reshape(count, HEADS, HEAD_DIM)
    key_rows = project[:, D:2 * D].reshape(count, HEADS, HEAD_DIM)
    value_rows = project[:, 2 * D:].reshape(count, HEADS, HEAD_DIM)
    scores = low_back(jnp.einsum('qhd,khd->hqk', queries, key_rows, precision=highest) * 0.125)
    scores = jnp.where(mask[None], scores, -1e+30)
    attend = low(jax.nn.softmax(scores, axis=-1))
    attended = jnp.einsum('hqk,khd->qhd', attend, value_rows, precision=highest).reshape(count, D)
    attended = low(low_back(attended))
    branch = low_back(jnp.dot(attended, out_weight, precision=highest))
    middle = x_val + branch
    normal_mid = middle * lax.rsqrt(lax.optimization_barrier(jnp.mean(middle * middle, axis=-1, keepdims=True)) + EPS)
    second = low(normal_mid * second_gain)
    hidden = low_back(jnp.dot(second, up_weight, precision=highest) + up_bias)
    active = low(jax.nn.gelu(hidden, approximate=False))
    final = low_back(jnp.dot(active, down_weight, precision=highest) + down_bias)
    return middle + final

def reference(frames, lengths, cotangent, first_gain, qkv_weight, out_weight, second_gain, up_weight, up_bias, down_weight, down_bias):
    params = (first_gain, qkv_weight, out_weight, second_gain, up_weight, up_bias, down_weight, down_bias)
    params = tuple((piece.astype(jnp.float32) for piece in params))
    buffers = lengths.shape[0] * lengths.shape[1]
    inputs = frames.reshape(buffers, CAP, D)
    cots = cotangent.reshape(buffers, CAP, D)
    spans = lengths.reshape(buffers, SLOTS)

    def step(totals, item):
        x_in, c_in, span = item
        mask = build_mask(span)

        def forward(x_val, gain_a, weight_a, weight_b, gain_b, weight_c, bias_c, weight_d, bias_d):
            return layer(x_val, mask, gain_a, weight_a, weight_b, gain_b, weight_c, bias_c, weight_d, bias_d)
        out_val, pullback = jax.vjp(forward, x_in.astype(jnp.float32), params[0], params[1], params[2], params[3], params[4], params[5], params[6], params[7])
        grads = pullback(c_in.astype(jnp.float32))
        totals = tuple((total + grad for total, grad in zip(totals, grads[1:])))
        return (totals, (out_val.astype(jnp.bfloat16), grads[0]))
    zeros = tuple((jnp.zeros(piece.shape, jnp.float32) for piece in params))
    totals, stacked = lax.scan(step, zeros, (inputs, cots, spans))
    outputs = stacked[0].reshape(frames.shape)
    frames_grad = stacked[1].reshape(frames.shape)
    return (outputs, frames_grad, totals[0], totals[1], totals[2], totals[3], totals[4], totals[5], totals[6], totals[7])
```

```python
import functools
import jax
import jax.numpy as jnp
from jax import lax
from jax.experimental import pallas as pl
from jax.experimental.pallas import tpu as pltpu
from jax.sharding import PartitionSpec as P

AXES = ("dp", "fsdp")
ROWS, WIDE, SKEW = 32, 512, 1


def bit_table(sizes):
    table = []
    for axis in AXES:
        stride = sizes[axis] // 2
        while stride:
            table.append((axis, stride))
            stride //= 2
    return table


def my_bits(table):
    where = {axis: lax.axis_index(axis) for axis in AXES}
    return [(where[axis] // stride) % 2 for axis, stride in table], where


def partner(table, bits, where, k):
    axis, stride = table[k]
    other = dict(where)
    other[axis] = where[axis] + stride * (1 - 2 * bits[k])
    return tuple(other[a] for a in AXES)


def greet(table, bits, where):
    barrier = pltpu.get_barrier_semaphore()
    for k in range(len(table)):
        pl.semaphore_signal(barrier, inc=1, device_id=partner(table, bits, where, k), device_id_type=pl.DeviceIdType.MESH)
    pl.semaphore_wait(barrier, len(table))


def orders(table):
    dp = [k for k, (axis, _) in enumerate(table) if axis == "dp"]
    rest = [k for k, (axis, _) in enumerate(table) if axis != "dp"]
    core, chips = dp[-1:], dp[:-1]
    return [core + chips + rest, core + chips[::-1] + rest]


def units_of(shapes):
    units = []
    for i, (rows, width) in enumerate(shapes):
        high, wide = min(rows, ROWS), min(width, WIDE)
        for r in range(0, rows, high):
            for c in range(0, width, 2 * wide):
                halves = [c] if c + wide >= width else [c, c + wide]
                units.append([(i, slice(r, r + high), slice(b, b + wide)) for b in halves])
    return units


def timetable(units, steps, skew):
    events, piece = [], 0
    for u, unit in enumerate(units):
        for h in range(len(unit)):
            events += [(u + skew * s, s, piece, h) for s in range(steps + 1)]
            piece += 1
    return [(p, s) for _, s, p, _ in sorted(events)]


def gather_kernel(table, n, chunks, times, *refs):
    shards, fulls = refs[:n], refs[n:2 * n]
    local_sem, send_sem, recv_sem = refs[2 * n:]
    bits, where = my_bits(table)
    steps = len(table)
    greet(table, bits, where)

    def view(c, done):
        i, rows, cols, _ = chunks[c]
        index = tuple(slice(None) if k in done else bits[k] for k in range(steps))
        return fulls[i].at[index + (rows, cols)]

    own, copies = [], {}
    for i in range(n):
        index = tuple(bits[k] for k in range(steps))
        copy = pltpu.make_async_copy(shards[i], fulls[i].at[index], local_sem.at[i])
        copy.start()
        own.append(copy)
    arrived = set()
    for c, s in times:
        i, rows, cols, order = chunks[c]
        if s > 0:
            copies[c, s - 1].wait_recv()
            if i not in arrived:
                arrived.add(i)
                own[i].wait()
        if s < steps:
            there = view(c, order[:s])
            copy = pltpu.make_async_remote_copy(
                src_ref=shards[i].at[rows, cols] if s == 0 else there, dst_ref=there,
                send_sem=send_sem.at[c, s], recv_sem=recv_sem.at[c, s],
                device_id=partner(table, bits, where, order[s]), device_id_type=pl.DeviceIdType.MESH)
            copy.start()
            copies[c, s] = copy
    for copy in copies.values():
        copy.wait_send()


def gather(shards, sizes, collective_id):
    table = bit_table(sizes)
    steps = len(table)
    two = [o[::-1] for o in orders(table)]
    units = units_of([a.shape for a in shards])
    chunks = [piece + (two[(h + u) % 2],) for u, unit in enumerate(units) for h, piece in enumerate(unit)]
    out = pl.pallas_call(
        functools.partial(gather_kernel, table, len(shards), chunks, timetable(units, steps, SKEW)),
        out_shape=[jax.ShapeDtypeStruct((2,) * steps + a.shape, a.dtype) for a in shards],
        in_specs=[pl.BlockSpec(memory_space=pl.ANY)] * len(shards),
        out_specs=[pl.BlockSpec(memory_space=pl.ANY)] * len(shards),
        scratch_shapes=[pltpu.SemaphoreType.DMA((len(shards),)), pltpu.SemaphoreType.DMA((len(chunks), steps)), pltpu.SemaphoreType.DMA((len(chunks), steps))],
        compiler_params=pltpu.CompilerParams(collective_id=collective_id, has_side_effects=True),
        name="gather",
    )(*shards)
    return [f.reshape((f.shape[-2] * 2 ** steps,) + f.shape[-1:]) for f in out]


def scatter_kernel(table, plan, *refs):
    n, chunks, times, steps = plan["n"], plan["chunks"], plan["times"], len(table)
    parts, outs = refs[:n], refs[n:2 * n]
    m = len(chunks)
    keep = refs[2 * n:2 * n + m]
    recv = [refs[2 * n + m + c * steps:2 * n + m + (c + 1) * steps] for c in range(m)]
    local_sem, send_sem, recv_sem = refs[2 * n + m + m * steps:]
    bits, where = my_bits(table)
    greet(table, bits, where)
    copies = {}
    loads = {}

    def index(order, s, last):
        out = []
        for k in range(steps):
            if k in order[1:s]:
                out.append(bits[k])
            elif k == order[0]:
                continue
            elif s < steps and k == order[s] and last is not None:
                out.append(last)
            else:
                out.append(slice(None))
        return tuple(out)

    def start(c, s):
        i, rows, cols, order = chunks[c]
        k = order[s]
        other = 1 - bits[k]
        if s == 0:
            full = tuple(other if q == k else slice(None) for q in range(steps))
            src = parts[i].at[full + (rows, cols)]
        else:
            src = keep[c].at[index(order, s, other)]
        copy = pltpu.make_async_remote_copy(
            src_ref=src, dst_ref=recv[c][s], send_sem=send_sem.at[c, s], recv_sem=recv_sem.at[c, s],
            device_id=partner(table, bits, where, k), device_id_type=pl.DeviceIdType.MESH)
        copy.start()
        copies[c, s] = copy

    def add(c, s):
        i, rows, cols, order = chunks[c]
        left = steps - s - 1
        if left == 0:
            own = keep[c][index(order, steps, None)] if steps > 1 else keep[c][...]
            outs[i][rows, cols] = own.astype(jnp.float32) + recv[c][s][...].astype(jnp.float32)
            return
        base = index(order, s, bits[order[s]] if s else None)

        @pl.loop(0, 2 ** left)
        def _(j):
            free, at = [], []
            for b in range(left):
                free.append((j // 2 ** (left - 1 - b)) % 2)
            pos = 0
            for e in base:
                if isinstance(e, slice):
                    at.append(free[pos])
                    pos += 1
                else:
                    at.append(e)
            here = tuple(at)
            got = recv[c][s][tuple(free)]
            keep[c][here] = (keep[c][here].astype(jnp.float32) + got.astype(jnp.float32)).astype(keep[c].dtype)

    for c, s in times:
        i, rows, cols, order = chunks[c]
        if s == 0:
            full = tuple(bits[k] if k == order[0] else slice(None) for k in range(steps))
            loads[c] = pltpu.make_async_copy(parts[i].at[full + (rows, cols)], keep[c], local_sem.at[c])
            loads[c].start()
        else:
            copies[c, s - 1].wait_recv()
            if s == 1:
                loads[c].wait()
            add(c, s - 1)
        if s < steps:
            start(c, s)
    for copy in copies.values():
        copy.wait_send()


def scatter(parts, sizes, collective_id):
    table = bit_table(sizes)
    steps = len(table)
    two = orders(table)
    owners = 2 ** steps
    parts = [a.reshape((2,) * steps + (a.shape[0] // owners, a.shape[1])) for a in parts]
    units = units_of([a.shape[-2:] for a in parts])
    chunks = [piece + (two[(h + u) % 2],) for u, unit in enumerate(units) for h, piece in enumerate(unit)]
    keep, recv = [], []
    for i, rows, cols, order in chunks:
        tail = (rows.stop - rows.start, cols.stop - cols.start)
        keep.append(pltpu.VMEM((2,) * (steps - 1) + tail, parts[i].dtype))
        recv += [pltpu.VMEM((2,) * (steps - 1 - s) + tail, parts[i].dtype) for s in range(steps)]
    plan = {"n": len(parts), "chunks": chunks, "times": timetable(units, steps, SKEW)}
    return pl.pallas_call(
        functools.partial(scatter_kernel, table, plan),
        out_shape=[jax.ShapeDtypeStruct(a.shape[-2:], jnp.float32) for a in parts],
        in_specs=[pl.BlockSpec(memory_space=pl.ANY)] * len(parts),
        out_specs=[pl.BlockSpec(memory_space=pltpu.VMEM)] * len(parts),
        scratch_shapes=keep + recv + [pltpu.SemaphoreType.DMA((len(chunks),)), pltpu.SemaphoreType.DMA((len(chunks), steps)), pltpu.SemaphoreType.DMA((len(chunks), steps))],
        compiler_params=pltpu.CompilerParams(collective_id=collective_id, has_side_effects=True, vmem_limit_bytes=56 * 2 ** 20),
        name="scatter",
    )(*parts)


D = 1024
HEADS = 16
HEAD_DIM = 64


EPS = 1e-06


def build_mask(span, length):
    slots = jnp.arange(span.shape[0], dtype=jnp.int32)
    ends = jnp.sum(jnp.where(slots[:, None] <= slots[None, :], span[:, None], 0), axis=0)
    position = jnp.arange(length, dtype=jnp.int32)
    segment = jnp.sum((position[:, None] >= ends[None, :]).astype(jnp.int32), axis=1)
    same = segment[:, None] == segment[None, :]
    return jnp.logical_and(same, position[:, None] >= position[None, :])


def normalize(x_val):
    factor = lax.rsqrt(jnp.mean(x_val * x_val, axis=-1, keepdims=True) + EPS)
    return (x_val * factor, factor)


def norm_back(normal, factor, gain, grad_out):
    gain_grad = jnp.sum(grad_out * normal, axis=0)
    scaled = grad_out * gain
    inner = jnp.mean(scaled * normal, axis=-1, keepdims=True)
    return (factor * (scaled - normal * inner), gain_grad)


def split_heads(project, count):
    queries = project[:, :D].reshape(count, -1, HEADS, HEAD_DIM)
    key_rows = project[:, D : 2 * D].reshape(count, -1, HEADS, HEAD_DIM)
    value_rows = project[:, 2 * D :].reshape(count, -1, HEADS, HEAD_DIM)
    return (queries, key_rows, value_rows)


def masked_scores(queries, key_rows, mask):
    scores = (
        jnp.einsum("bqhd,bkhd->bhqk", queries, key_rows, preferred_element_type=jnp.float32) * 0.125
    )
    return jnp.where(mask[:, None], scores, -1e30)


def exact_gelu(value):
    return jax.nn.gelu(value, approximate=False)


def forward_pass(x_val, mask, params):
    first_gain, qkv_weight, out_weight, second_gain, up_weight, up_bias, down_weight, down_bias = (
        params
    )
    count = x_val.shape[0]
    normal_in, factor_in = normalize(x_val)
    entered = (normal_in * first_gain.astype(jnp.float32)).astype(jnp.bfloat16)
    project = jnp.dot(entered, qkv_weight, preferred_element_type=jnp.float32).astype(jnp.bfloat16)
    queries, key_rows, value_rows = split_heads(project, mask.shape[0])
    scores = masked_scores(queries, key_rows, mask)
    peak = jnp.max(scores, axis=-1, keepdims=True)
    expo = jnp.exp(scores - peak)
    total = jnp.sum(expo, axis=-1, keepdims=True)
    logsum = peak + jnp.log(total)
    attend = (expo / total).astype(jnp.bfloat16)
    attended = jnp.einsum("bhqk,bkhd->bqhd", attend, value_rows, preferred_element_type=jnp.float32)
    attended = attended.reshape(count, D).astype(jnp.bfloat16)
    middle = x_val + jnp.dot(attended, out_weight, preferred_element_type=jnp.float32)
    normal_mid, factor_mid = normalize(middle)
    second = (normal_mid * second_gain.astype(jnp.float32)).astype(jnp.bfloat16)
    hidden = jnp.dot(second, up_weight, preferred_element_type=jnp.float32) + up_bias.astype(
        jnp.float32
    )
    active = exact_gelu(hidden).astype(jnp.bfloat16)
    final = jnp.dot(active, down_weight, preferred_element_type=jnp.float32) + down_bias.astype(
        jnp.float32
    )
    kept = (
        normal_in,
        factor_in,
        entered,
        project,
        logsum,
        attended,
        normal_mid,
        factor_mid,
        second,
        hidden,
        active,
    )
    return (middle + final, kept)


def backward_pass(grad, mask, params, kept):
    first_gain, qkv_weight, out_weight, second_gain, up_weight, up_bias, down_weight, down_bias = (
        params
    )
    (
        normal_in,
        factor_in,
        entered,
        project,
        logsum,
        attended,
        normal_mid,
        factor_mid,
        second,
        hidden,
        active,
    ) = kept
    count = grad.shape[0]
    grad_final = grad.astype(jnp.bfloat16)
    down_bias_grad = jnp.sum(grad_final.astype(jnp.float32), axis=0)
    down_grad = jnp.einsum("rf,rd->fd", active, grad_final, preferred_element_type=jnp.float32)
    grad_active = jnp.einsum(
        "rd,fd->rf", grad_final, down_weight, preferred_element_type=jnp.float32
    )
    gelu_value, gelu_back = jax.vjp(exact_gelu, hidden)
    grad_hidden = gelu_back(grad_active)[0].astype(jnp.bfloat16)
    up_bias_grad = jnp.sum(grad_hidden.astype(jnp.float32), axis=0)
    up_grad = jnp.einsum("rd,rf->df", second, grad_hidden, preferred_element_type=jnp.float32)
    grad_second = jnp.einsum(
        "rf,df->rd", grad_hidden, up_weight, preferred_element_type=jnp.float32
    )
    grad_norm_mid, second_gain_grad = norm_back(
        normal_mid, factor_mid, second_gain.astype(jnp.float32), grad_second
    )
    grad_middle = grad + grad_norm_mid
    grad_branch = grad_middle.astype(jnp.bfloat16)
    out_grad = jnp.einsum("re,rd->ed", attended, grad_branch, preferred_element_type=jnp.float32)
    grad_attended = jnp.einsum(
        "rd,ed->re", grad_branch, out_weight, preferred_element_type=jnp.float32
    )
    grad_attended = grad_attended.astype(jnp.bfloat16).reshape(mask.shape[0], -1, HEADS, HEAD_DIM)
    queries, key_rows, value_rows = split_heads(project, mask.shape[0])
    scores = masked_scores(queries, key_rows, mask)
    attend_full = jnp.exp(scores - logsum)
    attend = attend_full.astype(jnp.bfloat16)
    value_grad = jnp.einsum(
        "bhqk,bqhd->bkhd", attend, grad_attended, preferred_element_type=jnp.float32
    )
    grad_attend = jnp.einsum(
        "bqhd,bkhd->bhqk", grad_attended, value_rows, preferred_element_type=jnp.float32
    )
    row_total = jnp.sum(attend_full * grad_attend, axis=-1, keepdims=True)
    grad_scores = (attend_full * (grad_attend - row_total)).astype(jnp.bfloat16)
    query_grad = (
        jnp.einsum("bhqk,bkhd->bqhd", grad_scores, key_rows, preferred_element_type=jnp.float32)
        * 0.125
    )
    key_grad = (
        jnp.einsum("bhqk,bqhd->bkhd", grad_scores, queries, preferred_element_type=jnp.float32) * 0.125
    )
    grad_project = jnp.concatenate(
        (query_grad.reshape(count, D), key_grad.reshape(count, D), value_grad.reshape(count, D)),
        axis=1,
    )
    grad_project = grad_project.astype(jnp.bfloat16)
    qkv_grad = jnp.einsum("rd,re->de", entered, grad_project, preferred_element_type=jnp.float32)
    grad_entered = jnp.einsum(
        "re,de->rd", grad_project, qkv_weight, preferred_element_type=jnp.float32
    )
    grad_norm_in, first_gain_grad = norm_back(
        normal_in, factor_in, first_gain.astype(jnp.float32), grad_entered
    )
    frames_grad = grad_middle + grad_norm_in
    grads = (
        first_gain_grad,
        qkv_grad,
        out_grad,
        second_gain_grad,
        up_grad,
        up_bias_grad,
        down_grad,
        down_bias_grad,
    )
    return (frames_grad, grads)


def pack(vectors, owners, rows):
    flat = jnp.concatenate([v.reshape(owners, -1) for v in vectors], axis=1)
    return jnp.pad(flat, ((0, 0), (0, rows * 128 - flat.shape[1]))).reshape(owners * rows, 128)


def unpack(packed, owners, widths):
    flat = packed.reshape(owners, -1)
    out, at = [], 0
    for w in widths:
        out.append(flat[:, at:at + w].reshape(-1))
        at += w
    return out


def fits(sizes, shards):
    return all(s & (s - 1) == 0 for s in sizes.values()) and all(a.shape[0] % 16 == 0 for a in shards)


def body(sizes, frames, lengths, cotangent, *shards):
    owners = sizes["dp"] * sizes["fsdp"]
    weights = [shards[i] for i in (1, 2, 4, 6)]
    vectors = [shards[i] for i in (0, 3, 5, 7)]
    widths = [v.shape[0] for v in vectors]
    own_kernels = fits(sizes, weights)
    if own_kernels:
        packed, qkv, out, up, down = gather([pack(vectors, 1, 16)] + weights, sizes, 1)
        first, second, up_b, down_b = unpack(packed, owners, widths)
    else:
        qkv, out, up, down = [lax.all_gather(w, AXES, axis=0, tiled=True) for w in weights]
        first, second, up_b, down_b = [lax.all_gather(v, AXES, axis=0, tiled=True) for v in vectors]
    params = (first, qkv, out, second, up, up_b, down, down_b)
    batches, rows, width = frames.shape
    mask = jnp.stack([build_mask(lengths[b, 0], rows) for b in range(batches)])
    output, kept = forward_pass(frames.reshape(batches * rows, width).astype(jnp.float32), mask, params)
    frames_grad, grads = backward_pass(cotangent.reshape(batches * rows, width).astype(jnp.float32), mask, params, kept)
    big = [grads[i] for i in (1, 2, 4, 6)]
    small = [grads[i] for i in (0, 3, 5, 7)]
    if own_kernels:
        big = [g.astype(jnp.bfloat16) for g in (big[3], big[2], big[1], big[0])]
        down_g, up_g, out_g, qkv_g, packed = scatter(big + [pack(small, owners, 8)], sizes, 2)
        first_g, second_g, up_b_g, down_b_g = unpack(packed, 1, widths)
    else:
        qkv_g, out_g, up_g, down_g = [lax.psum_scatter(g.astype(jnp.float32), AXES, scatter_dimension=0, tiled=True) for g in big]
        first_g, second_g, up_b_g, down_b_g = [lax.psum_scatter(g, AXES, scatter_dimension=0, tiled=True) for g in small]
    shape = (batches, rows, width)
    return (output.astype(jnp.bfloat16).reshape(shape), frames_grad.reshape(shape), first_g, qkv_g, out_g, second_g, up_g, up_b_g, down_g, down_b_g)


def solution(mesh):
    in_specs = (
        P(None, ("dp", "fsdp"), None),
        P(None, ("dp", "fsdp"), None),
        P(None, ("dp", "fsdp"), None),
        P(("dp", "fsdp")),
        P(("dp", "fsdp"), None),
        P(("dp", "fsdp"), None),
        P(("dp", "fsdp")),
        P(("dp", "fsdp"), None),
        P(("dp", "fsdp")),
        P(("dp", "fsdp"), None),
        P(("dp", "fsdp")),
    )
    out_specs = (
        P(None, ("dp", "fsdp"), None),
        P(None, ("dp", "fsdp"), None),
        P(("dp", "fsdp")),
        P(("dp", "fsdp"), None),
        P(("dp", "fsdp"), None),
        P(("dp", "fsdp")),
        P(("dp", "fsdp"), None),
        P(("dp", "fsdp")),
        P(("dp", "fsdp"), None),
        P(("dp", "fsdp")),
    )
    return jax.shard_map(functools.partial(body, dict(mesh.shape)), mesh=mesh, in_specs=in_specs, out_specs=out_specs, check_vma=False)
```

```python
import functools
import jax
import jax.numpy as jnp
from jax import lax
from jax.experimental import pallas as pl
from jax.experimental.pallas import tpu as pltpu
from jax.sharding import PartitionSpec as P

AXES = ("dp", "fsdp")
ROWS, WIDE, SKEW = 32, 512, 1


def bit_table(sizes):
    table = []
    for axis in AXES:
        stride = sizes[axis] // 2
        while stride:
            table.append((axis, stride))
            stride //= 2
    return table


def my_bits(table):
    where = {axis: lax.axis_index(axis) for axis in AXES}
    return [(where[axis] // stride) % 2 for axis, stride in table], where


def partner(table, bits, where, k):
    axis, stride = table[k]
    other = dict(where)
    other[axis] = where[axis] + stride * (1 - 2 * bits[k])
    return tuple(other[a] for a in AXES)


def greet(table, bits, where):
    barrier = pltpu.get_barrier_semaphore()
    for k in range(len(table)):
        pl.semaphore_signal(barrier, inc=1, device_id=partner(table, bits, where, k), device_id_type=pl.DeviceIdType.MESH)
    pl.semaphore_wait(barrier, len(table))


def orders(table):
    dp = [k for k, (axis, _) in enumerate(table) if axis == "dp"]
    rest = [k for k, (axis, _) in enumerate(table) if axis != "dp"]
    core, chips = dp[-1:], dp[:-1]
    return [core + chips + rest, core + chips[::-1] + rest]


def units_of(shapes):
    units = []
    for i, (rows, width) in enumerate(shapes):
        high, wide = min(rows, ROWS), min(width, WIDE)
        for r in range(0, rows, high):
            for c in range(0, width, 2 * wide):
                halves = [c] if c + wide >= width else [c, c + wide]
                units.append([(i, slice(r, r + high), slice(b, b + wide)) for b in halves])
    return units


def timetable(units, steps, skew):
    events, piece = [], 0
    for u, unit in enumerate(units):
        for h in range(len(unit)):
            events += [(u + skew * s, s, piece, h) for s in range(steps + 1)]
            piece += 1
    return [(p, s) for _, s, p, _ in sorted(events)]


def gather_kernel(table, n, chunks, times, *refs):
    shards, fulls = refs[:n], refs[n:2 * n]
    local_sem, send_sem, recv_sem = refs[2 * n:]
    bits, where = my_bits(table)
    steps = len(table)
    greet(table, bits, where)

    def view(c, done):
        i, rows, cols, _ = chunks[c]
        index = tuple(slice(None) if k in done else bits[k] for k in range(steps))
        return fulls[i].at[index + (rows, cols)]

    own, copies = [], {}
    for i in range(n):
        index = tuple(bits[k] for k in range(steps))
        copy = pltpu.make_async_copy(shards[i], fulls[i].at[index], local_sem.at[i])
        copy.start()
        own.append(copy)
    arrived = set()
    for c, s in times:
        i, rows, cols, order = chunks[c]
        if s > 0:
            copies[c, s - 1].wait_recv()
            if i not in arrived:
                arrived.add(i)
                own[i].wait()
        if s < steps:
            there = view(c, order[:s])
            copy = pltpu.make_async_remote_copy(
                src_ref=shards[i].at[rows, cols] if s == 0 else there, dst_ref=there,
                send_sem=send_sem.at[c, s], recv_sem=recv_sem.at[c, s],
                device_id=partner(table, bits, where, order[s]), device_id_type=pl.DeviceIdType.MESH)
            copy.start()
            copies[c, s] = copy
    for copy in copies.values():
        copy.wait_send()


def gather(shards, sizes, collective_id):
    table = bit_table(sizes)
    steps = len(table)
    two = [o[::-1] for o in orders(table)]
    units = units_of([a.shape for a in shards])
    chunks = [piece + (two[(h + u) % 2],) for u, unit in enumerate(units) for h, piece in enumerate(unit)]
    out = pl.pallas_call(
        functools.partial(gather_kernel, table, len(shards), chunks, timetable(units, steps, SKEW)),
        out_shape=[jax.ShapeDtypeStruct((2,) * steps + a.shape, a.dtype) for a in shards],
        in_specs=[pl.BlockSpec(memory_space=pl.ANY)] * len(shards),
        out_specs=[pl.BlockSpec(memory_space=pl.ANY)] * len(shards),
        scratch_shapes=[pltpu.SemaphoreType.DMA((len(shards),)), pltpu.SemaphoreType.DMA((len(chunks), steps)), pltpu.SemaphoreType.DMA((len(chunks), steps))],
        compiler_params=pltpu.CompilerParams(collective_id=collective_id, has_side_effects=True),
        name="gather",
    )(*shards)
    return [f.reshape((f.shape[-2] * 2 ** steps,) + f.shape[-1:]) for f in out]


def scatter_kernel(table, plan, *refs):
    n, chunks, times, steps = plan["n"], plan["chunks"], plan["times"], len(table)
    parts, outs = refs[:n], refs[n:2 * n]
    m = len(chunks)
    keep = refs[2 * n:2 * n + m]
    recv = [refs[2 * n + m + c * steps:2 * n + m + (c + 1) * steps] for c in range(m)]
    local_sem, send_sem, recv_sem = refs[2 * n + m + m * steps:]
    bits, where = my_bits(table)
    greet(table, bits, where)
    copies = {}
    loads = {}

    def index(order, s, last):
        out = []
        for k in range(steps):
            if k in order[1:s]:
                out.append(bits[k])
            elif k == order[0]:
                continue
            elif s < steps and k == order[s] and last is not None:
                out.append(last)
            else:
                out.append(slice(None))
        return tuple(out)

    def start(c, s):
        i, rows, cols, order = chunks[c]
        k = order[s]
        other = 1 - bits[k]
        if s == 0:
            full = tuple(other if q == k else slice(None) for q in range(steps))
            src = parts[i].at[full + (rows, cols)]
        else:
            src = keep[c].at[index(order, s, other)]
        copy = pltpu.make_async_remote_copy(
            src_ref=src, dst_ref=recv[c][s], send_sem=send_sem.at[c, s], recv_sem=recv_sem.at[c, s],
            device_id=partner(table, bits, where, k), device_id_type=pl.DeviceIdType.MESH)
        copy.start()
        copies[c, s] = copy

    def add(c, s):
        i, rows, cols, order = chunks[c]
        left = steps - s - 1
        if left == 0:
            own = keep[c][index(order, steps, None)] if steps > 1 else keep[c][...]
            outs[i][rows, cols] = own.astype(jnp.float32) + recv[c][s][...].astype(jnp.float32)
            return
        base = index(order, s, bits[order[s]] if s else None)

        @pl.loop(0, 2 ** left)
        def _(j):
            free, at = [], []
            for b in range(left):
                free.append((j // 2 ** (left - 1 - b)) % 2)
            pos = 0
            for e in base:
                if isinstance(e, slice):
                    at.append(free[pos])
                    pos += 1
                else:
                    at.append(e)
            here = tuple(at)
            got = recv[c][s][tuple(free)]
            keep[c][here] = (keep[c][here].astype(jnp.float32) + got.astype(jnp.float32)).astype(keep[c].dtype)

    for c, s in times:
        i, rows, cols, order = chunks[c]
        if s == 0:
            full = tuple(bits[k] if k == order[0] else slice(None) for k in range(steps))
            loads[c] = pltpu.make_async_copy(parts[i].at[full + (rows, cols)], keep[c], local_sem.at[c])
            loads[c].start()
        else:
            copies[c, s - 1].wait_recv()
            if s == 1:
                loads[c].wait()
            add(c, s - 1)
        if s < steps:
            start(c, s)
    for copy in copies.values():
        copy.wait_send()


def scatter(parts, sizes, collective_id):
    table = bit_table(sizes)
    steps = len(table)
    two = orders(table)
    owners = 2 ** steps
    parts = [a.reshape((2,) * steps + (a.shape[0] // owners, a.shape[1])) for a in parts]
    units = units_of([a.shape[-2:] for a in parts])
    chunks = [piece + (two[(h + u) % 2],) for u, unit in enumerate(units) for h, piece in enumerate(unit)]
    keep, recv = [], []
    for i, rows, cols, order in chunks:
        tail = (rows.stop - rows.start, cols.stop - cols.start)
        keep.append(pltpu.VMEM((2,) * (steps - 1) + tail, parts[i].dtype))
        recv += [pltpu.VMEM((2,) * (steps - 1 - s) + tail, parts[i].dtype) for s in range(steps)]
    plan = {"n": len(parts), "chunks": chunks, "times": timetable(units, steps, SKEW)}
    return pl.pallas_call(
        functools.partial(scatter_kernel, table, plan),
        out_shape=[jax.ShapeDtypeStruct(a.shape[-2:], jnp.float32) for a in parts],
        in_specs=[pl.BlockSpec(memory_space=pl.ANY)] * len(parts),
        out_specs=[pl.BlockSpec(memory_space=pltpu.VMEM)] * len(parts),
        scratch_shapes=keep + recv + [pltpu.SemaphoreType.DMA((len(chunks),)), pltpu.SemaphoreType.DMA((len(chunks), steps)), pltpu.SemaphoreType.DMA((len(chunks), steps))],
        compiler_params=pltpu.CompilerParams(collective_id=collective_id, has_side_effects=True, vmem_limit_bytes=56 * 2 ** 20),
        name="scatter",
    )(*parts)


EPS = 1e-06
BLOCK = 1024
TALL = 256
NT = (((1,), (1,)), ((), ()))
TN = (((0,), (0,)), ((), ()))
NN = (((1,), (0,)), ((), ()))
F32, BF16 = jnp.float32, jnp.bfloat16


def mul(a, b, dims=NN):
    return lax.dot_general(a, b, dims, preferred_element_type=F32)


def mlp_kernel(middle, cot, gain, up, up_b, down, down_b, out, grad_middle, grad_branch, up_g, down_g, up_b_g, gain_g, down_b_g,
               second, total, back, active, grad_hidden):
    step, last = pl.program_id(0), pl.num_programs(0) - 1
    rows, width = middle.shape
    part = 128

    @pl.when(step == 0)
    def _():
        @pl.loop(0, rows // part)
        def _(i):
            at = pl.ds(pl.multiple_of(i * part, part), part)
            x = middle[at, :]
            normal = x * lax.rsqrt(jnp.mean(x * x, axis=-1, keepdims=True) + EPS)
            second[at, :] = (normal * gain[...]).astype(BF16)

    bias = up_b[...]
    up_b_g[...] = jnp.zeros_like(up_b_g)

    @pl.loop(0, rows // TALL)
    def _(i):
        at = pl.ds(pl.multiple_of(i * TALL, TALL), TALL)
        hidden = mul(second[at, :], up[...]) + bias
        grad = mul(cot[at, :], down[...], NT)
        half = 0.5 + 0.5 * lax.erf(hidden * (0.5 ** 0.5))
        slope = half + hidden * (jnp.exp(hidden * hidden * -0.5) * 0.3989422804014327)
        active[at, :] = (hidden * half).astype(BF16)
        low = (grad * slope).astype(BF16)
        grad_hidden[at, :] = low
        up_b_g[...] += jnp.sum(low.astype(F32), axis=0, keepdims=True)

    @pl.loop(0, rows // TALL)
    def _(i):
        at = pl.ds(pl.multiple_of(i * TALL, TALL), TALL)
        more, less = mul(active[at, :], down[...]), mul(grad_hidden[at, :], up[...], NT)

        @pl.when(step == 0)
        def _():
            total[at, :] = more
            back[at, :] = less

        @pl.when(step > 0)
        def _():
            total[at, :] += more
            back[at, :] += less

    @pl.loop(0, BLOCK // TALL)
    def _(i):
        at = pl.ds(pl.multiple_of(i * TALL, TALL), TALL)
        down_g[at, :] = mul(active[:, at], cot[...], TN).astype(down_g.dtype)

    @pl.loop(0, width // TALL)
    def _(i):
        at = pl.ds(pl.multiple_of(i * TALL, TALL), TALL)
        up_g[at, :] = mul(second[:, at], grad_hidden[...], TN).astype(up_g.dtype)

    @pl.when(step == last)
    def _():
        gain_g[...] = jnp.zeros_like(gain_g)
        down_b_g[...] = jnp.zeros_like(down_b_g)

        @pl.loop(0, rows // part)
        def _(i):
            at = pl.ds(pl.multiple_of(i * part, part), part)
            x = middle[at, :]
            factor = lax.rsqrt(jnp.mean(x * x, axis=-1, keepdims=True) + EPS)
            normal = x * factor
            out[at, :] = (x + (total[at, :] + down_b[...])).astype(BF16)
            g = cot[at, :].astype(F32)
            grad = back[at, :]
            gain_g[...] += jnp.sum(grad * normal, axis=0, keepdims=True)
            down_b_g[...] += jnp.sum(g, axis=0, keepdims=True)
            n = grad * gain[...]
            result = g + factor * (n - normal * jnp.mean(n * normal, axis=-1, keepdims=True))
            grad_middle[at, :] = result
            grad_branch[at, :] = result.astype(BF16)


def mlp(middle, cot, gain, up, up_b, down, down_b, sum_type=BF16):
    rows, width = middle.shape
    ff = up.shape[1]
    whole = lambda *s: pl.BlockSpec(s, lambda j: (0,) * len(s), pipeline_mode=pl.Buffered(1))
    row = whole(1, width)
    return pl.pallas_call(
        mlp_kernel,
        grid=(ff // BLOCK,),
        in_specs=[whole(rows, width), whole(rows, width), row, pl.BlockSpec((width, BLOCK), lambda j: (0, j)),
                  pl.BlockSpec((1, BLOCK), lambda j: (0, j)), pl.BlockSpec((BLOCK, width), lambda j: (j, 0)), row],
        out_specs=[whole(rows, width), whole(rows, width), whole(rows, width), pl.BlockSpec((width, BLOCK), lambda j: (0, j)),
                   pl.BlockSpec((BLOCK, width), lambda j: (j, 0)), pl.BlockSpec((1, BLOCK), lambda j: (0, j)), row, row],
        out_shape=[jax.ShapeDtypeStruct(s, d) for s, d in (
            ((rows, width), BF16), ((rows, width), F32), ((rows, width), BF16), ((width, ff), sum_type), ((ff, width), sum_type),
            ((1, ff), F32), ((1, width), F32), ((1, width), F32))],
        scratch_shapes=[pltpu.VMEM((rows, width), BF16), pltpu.VMEM((rows, width), F32), pltpu.VMEM((rows, width), F32),
                        pltpu.VMEM((rows, BLOCK), BF16), pltpu.VMEM((rows, BLOCK), BF16)],
        compiler_params=pltpu.CompilerParams(vmem_limit_bytes=56 * 2 ** 20, dimension_semantics=("arbitrary",)),
        name="mlp",
    )(middle, cot, gain.reshape(1, -1).astype(F32), up, up_b.reshape(1, -1).astype(F32), down, down_b.reshape(1, -1).astype(F32))


PIECE = 128
REACH = 256


def spans(rows):
    return [(max(0, i * PIECE - REACH), i * PIECE, (i + 1) * PIECE) for i in range(rows // PIECE)]


def side_by_side(x, lanes):
    zero = jnp.zeros_like(x)
    return jnp.concatenate([jnp.where(lanes, x, zero), jnp.where(lanes, zero, x)], axis=0)


def fill_bias(bias, start, rows):
    at = 0
    for low, q, high in spans(rows):
        n = high - low
        key = low + lax.broadcasted_iota(jnp.int32, (n, PIECE), 0)
        query = q + lax.broadcasted_iota(jnp.int32, (n, PIECE), 1)
        seen = jnp.logical_and(key <= query, key >= start[:, q:high])
        b = jnp.where(seen, 0.0, -1e30)
        bias[at:at + n, :] = jnp.concatenate([b, b], axis=1)
        at += n


def attend_kernel(q_ref, k_ref, v_ref, start, out, logsum, bias):
    rows, wide = q_ref.shape

    @pl.when(pl.program_id(1) == 0)
    def _():
        fill_bias(bias, start[0], rows)

    lanes = lax.broadcasted_iota(jnp.int32, (PIECE, wide), 1) < wide // 2
    at = 0
    for i, (low, q, high) in enumerate(spans(rows)):
        n = high - low
        queries = side_by_side(q_ref[q:high, :] * 0.125, lanes)
        scores = mul(k_ref[low:high, :], queries, NT) + bias[at:at + n, :]
        peak = jnp.max(scores, axis=0, keepdims=True)
        expo = jnp.exp(scores - peak)
        total = jnp.sum(expo, axis=0, keepdims=True)
        logsum[0, 0, i:i + 1, :] = peak + jnp.log(total)
        attend = (expo * (1.0 / total)).astype(BF16)
        both = mul(attend, v_ref[low:high, :], TN)
        out[q:high, :] = jnp.where(lanes, both[:PIECE], both[PIECE:]).astype(BF16)
        at += n


def attend_specs(rows, pairs):
    block = lambda off: pl.BlockSpec((rows, 128), lambda b, h: (b, off * pairs + h))
    start = pl.BlockSpec((1, 1, rows), lambda b, h: (b, 0, 0))
    logsum = pl.BlockSpec((1, 1, rows // PIECE, 2 * PIECE), lambda b, h: (b, h, 0, 0))
    return block, start, logsum


def attend(project, start):
    batches, rows = start.shape[0], start.shape[2]
    width = project.shape[1] // 3
    pairs = width // 128
    block, start_spec, logsum = attend_specs(rows, pairs)
    return pl.pallas_call(
        attend_kernel,
        grid=(batches, pairs),
        in_specs=[block(0), block(1), block(2), start_spec],
        out_specs=[block(0), logsum],
        out_shape=[jax.ShapeDtypeStruct((batches * rows, width), BF16),
                   jax.ShapeDtypeStruct((batches, pairs, rows // PIECE, 2 * PIECE), F32)],
        scratch_shapes=[pltpu.VMEM((sum(h - l for l, _, h in spans(rows)), 2 * PIECE), F32)],
        compiler_params=pltpu.CompilerParams(vmem_limit_bytes=40 * 2 ** 20, dimension_semantics=("arbitrary", "arbitrary")),
        name="attend",
    )(project, project, project, start)


def attend_back_kernel(q_ref, k_ref, v_ref, g_ref, start, logsum, out, bias, k_sum, v_sum):
    rows, wide = q_ref.shape

    @pl.when(pl.program_id(1) == 0)
    def _():
        fill_bias(bias, start[0], rows)

    lanes = lax.broadcasted_iota(jnp.int32, (PIECE, wide), 1) < wide // 2
    at = 0
    k_sum[...] = jnp.zeros_like(k_sum)
    v_sum[...] = jnp.zeros_like(v_sum)
    for i, (low, q, high) in enumerate(spans(rows)):
        n = high - low
        queries = side_by_side(q_ref[q:high, :] * 0.125, lanes)
        grads = side_by_side(g_ref[q:high, :], lanes)
        keys, values = k_ref[low:high, :], v_ref[low:high, :]
        scores = mul(keys, queries, NT) + bias[at:at + n, :]
        full = jnp.exp(scores - logsum[0, 0, i:i + 1, :])
        grad = mul(values, grads, NT)
        v_sum[low:high, :] += mul(full.astype(BF16), grads)
        total = jnp.sum(full * grad, axis=0, keepdims=True)
        grad_scores = (full * (grad - total)).astype(BF16)
        k_sum[low:high, :] += mul(grad_scores, queries)
        both = mul(grad_scores, keys, TN) * 0.125
        out[0, q:high, :] = jnp.where(lanes, both[:PIECE], both[PIECE:]).astype(BF16)
        at += n
    out[1] = k_sum[...].astype(BF16)
    out[2] = v_sum[...].astype(BF16)


def attend_back(project, grad, start, logsum):
    batches, rows = start.shape[0], start.shape[2]
    width = project.shape[1] // 3
    pairs = width // 128
    block, start_spec, logsum_spec = attend_specs(rows, pairs)
    return pl.pallas_call(
        attend_back_kernel,
        grid=(batches, pairs),
        in_specs=[block(0), block(1), block(2), block(0), start_spec, logsum_spec],
        out_specs=pl.BlockSpec((3, rows, 128), lambda b, h: (0, b, h)),
        out_shape=jax.ShapeDtypeStruct((3, batches * rows, width), BF16),
        scratch_shapes=[pltpu.VMEM((sum(h - l for l, _, h in spans(rows)), 2 * PIECE), F32),
                        pltpu.VMEM((rows, 128), F32), pltpu.VMEM((rows, 128), F32)],
        compiler_params=pltpu.CompilerParams(vmem_limit_bytes=40 * 2 ** 20, dimension_semantics=("arbitrary", "arbitrary")),
        name="attend_back",
    )(project, project, project, grad, start, logsum)


def pack(vectors, owners, rows):
    flat = jnp.concatenate([v.reshape(owners, -1) for v in vectors], axis=1)
    return jnp.pad(flat, ((0, 0), (0, rows * 128 - flat.shape[1]))).reshape(owners * rows, 128)


def unpack(packed, owners, widths):
    flat = packed.reshape(owners, -1)
    out, at = [], 0
    for w in widths:
        out.append(flat[:, at:at + w].reshape(-1))
        at += w
    return out


def fits(sizes, shards):
    return all(s & (s - 1) == 0 for s in sizes.values()) and all(a.shape[0] % 16 == 0 for a in shards)


def item_ends(lengths):
    slots = jnp.arange(lengths.shape[1], dtype=jnp.int32)
    ends = jnp.sum(jnp.where(slots[None, :, None] <= slots[None, None, :], lengths[:, :, None], 0), axis=1)
    return ends


def normalize(x_val):
    factor = lax.rsqrt(jnp.mean(x_val * x_val, axis=-1, keepdims=True) + EPS)
    return (x_val * factor, factor)


def norm_back(normal, factor, gain, grad_out):
    gain_grad = jnp.sum(grad_out * normal, axis=0)
    scaled = grad_out * gain
    inner = jnp.mean(scaled * normal, axis=-1, keepdims=True)
    return (factor * (scaled - normal * inner), gain_grad)


def block_pass(frames, lengths, cotangent, params, sum_type):
    first, qkv, out, second, up, up_b, down, down_b = params
    batches, rows, width = frames.shape
    x_val = frames.reshape(batches * rows, width).astype(F32)
    cot = cotangent.reshape(batches * rows, width)
    ends = item_ends(lengths)
    position = jnp.arange(rows, dtype=jnp.int32)[None, None, :]
    start = jnp.max(jnp.where(ends[:, :, None] <= position, ends[:, :, None], 0), axis=1, keepdims=True)
    normal, factor = normalize(x_val)
    gain = first.astype(F32)
    entered = (normal * gain).astype(BF16)
    project = mul(entered, qkv).astype(BF16)
    attended, logsum = attend(project, start)
    middle = x_val + mul(attended, out)
    output, grad_middle, grad_branch, up_g, down_g, up_b_g, second_g, down_b_g = mlp(middle, cot, second, up, up_b, down, down_b, sum_type)
    out_g = mul(attended, grad_branch, TN)
    grad_attended = mul(grad_branch, out, NT).astype(BF16)
    grads = attend_back(project, grad_attended, start, logsum)
    qkv_g = [mul(entered, grads[j], TN) for j in range(3)]
    grad_entered = sum(mul(grads[j], qkv[:, j * width:(j + 1) * width], NT) for j in range(3))
    back, first_g = norm_back(normal, factor, gain, grad_entered)
    shape = frames.shape
    return (output.reshape(shape), (grad_middle + back).reshape(shape), (down_g, up_g, out_g, *qkv_g),
            (first_g, second_g.reshape(-1), up_b_g.reshape(-1), down_b_g.reshape(-1)))


def body(sizes, frames, lengths, cotangent, *shards):
    owners = sizes["dp"] * sizes["fsdp"]
    weights = [shards[i] for i in (1, 2, 4, 6)]
    vectors = [shards[i] for i in (0, 3, 5, 7)]
    widths = [v.shape[0] for v in vectors]
    own_kernels = fits(sizes, weights)
    if own_kernels:
        packed, qkv, out, up, down = gather([pack(vectors, 1, 16)] + weights, sizes, 1)
        first, second, up_b, down_b = unpack(packed, owners, widths)
    else:
        qkv, out, up, down = [lax.all_gather(w, AXES, axis=0, tiled=True) for w in weights]
        first, second, up_b, down_b = [lax.all_gather(v, AXES, axis=0, tiled=True) for v in vectors]
    params = (first, qkv, out, second, up, up_b, down, down_b)
    output, frames_grad, big, small = block_pass(frames, lengths[:, 0], cotangent, params, BF16 if own_kernels else F32)
    if own_kernels:
        down_g, up_g, out_g, *qkv_g, packed = scatter([g.astype(BF16) for g in big] + [pack(small, owners, 8)], sizes, 2)
        first_g, second_g, up_b_g, down_b_g = unpack(packed, 1, widths)
    else:
        down_g, up_g, out_g, *qkv_g = [lax.psum_scatter(g.astype(F32), AXES, scatter_dimension=0, tiled=True) for g in big]
        first_g, second_g, up_b_g, down_b_g = [lax.psum_scatter(g, AXES, scatter_dimension=0, tiled=True) for g in small]
    return (output, frames_grad, first_g, jnp.concatenate(qkv_g, axis=1), out_g, second_g, up_g, up_b_g, down_g, down_b_g)


def solution(mesh):
    in_specs = (
        P(None, ("dp", "fsdp"), None),
        P(None, ("dp", "fsdp"), None),
        P(None, ("dp", "fsdp"), None),
        P(("dp", "fsdp")),
        P(("dp", "fsdp"), None),
        P(("dp", "fsdp"), None),
        P(("dp", "fsdp")),
        P(("dp", "fsdp"), None),
        P(("dp", "fsdp")),
        P(("dp", "fsdp"), None),
        P(("dp", "fsdp")),
    )
    out_specs = (
        P(None, ("dp", "fsdp"), None),
        P(None, ("dp", "fsdp"), None),
        P(("dp", "fsdp")),
        P(("dp", "fsdp"), None),
        P(("dp", "fsdp"), None),
        P(("dp", "fsdp")),
        P(("dp", "fsdp"), None),
        P(("dp", "fsdp")),
        P(("dp", "fsdp"), None),
        P(("dp", "fsdp")),
    )
    return jax.shard_map(functools.partial(body, dict(mesh.shape)), mesh=mesh, in_specs=in_specs, out_specs=out_specs, check_vma=False)
```

```python
import functools
import jax
import jax.numpy as jnp
from jax import lax
from jax.experimental import pallas as pl
from jax.experimental.pallas import tpu as pltpu
from jax.sharding import PartitionSpec as P

AXES = ("dp", "fsdp")
ROWS, WIDE, SKEW = 32, 512, 1


def bit_table(sizes):
    table = []
    for axis in AXES:
        stride = sizes[axis] // 2
        while stride:
            table.append((axis, stride))
            stride //= 2
    return table


def my_bits(table):
    where = {axis: lax.axis_index(axis) for axis in AXES}
    return [(where[axis] // stride) % 2 for axis, stride in table], where


def partner(table, bits, where, k):
    axis, stride = table[k]
    other = dict(where)
    other[axis] = where[axis] + stride * (1 - 2 * bits[k])
    return tuple(other[a] for a in AXES)


def greet(table, bits, where):
    barrier = pltpu.get_barrier_semaphore()
    for k in range(len(table)):
        pl.semaphore_signal(barrier, inc=1, device_id=partner(table, bits, where, k), device_id_type=pl.DeviceIdType.MESH)
    pl.semaphore_wait(barrier, len(table))


def orders(table):
    dp = [k for k, (axis, _) in enumerate(table) if axis == "dp"]
    rest = [k for k, (axis, _) in enumerate(table) if axis != "dp"]
    core, chips = dp[-1:], dp[:-1]
    return [core + chips + rest, core + chips[::-1] + rest]


def units_of(shapes):
    units = []
    for i, (rows, width) in enumerate(shapes):
        high, wide = min(rows, ROWS), min(width, WIDE)
        for r in range(0, rows, high):
            for c in range(0, width, 2 * wide):
                halves = [c] if c + wide >= width else [c, c + wide]
                units.append([(i, slice(r, r + high), slice(b, b + wide)) for b in halves])
    return units


def timetable(units, steps, skew):
    events, piece = [], 0
    for u, unit in enumerate(units):
        for h in range(len(unit)):
            events += [(u + skew * s, s, piece, h) for s in range(steps + 1)]
            piece += 1
    return [(p, s) for _, s, p, _ in sorted(events)]


EPS = 1e-06
BLOCK = 1024
TALL = 256
NT = (((1,), (1,)), ((), ()))
TN = (((0,), (0,)), ((), ()))
NN = (((1,), (0,)), ((), ()))
F32, BF16 = jnp.float32, jnp.bfloat16


def mul(a, b, dims=NN):
    return lax.dot_general(a, b, dims, preferred_element_type=F32)


def mlp_kernel(middle, cot, gain, up, up_b, down, down_b, out, grad_middle, grad_branch, up_g, down_g, up_b_g, gain_g, down_b_g,
               second, total, back, active, grad_hidden):
    step, last = pl.program_id(0), pl.num_programs(0) - 1
    rows, width = middle.shape
    part = 128

    @pl.when(step == 0)
    def _():
        @pl.loop(0, rows // part)
        def _(i):
            at = pl.ds(pl.multiple_of(i * part, part), part)
            x = middle[at, :]
            normal = x * lax.rsqrt(jnp.mean(x * x, axis=-1, keepdims=True) + EPS)
            second[at, :] = (normal * gain[...]).astype(BF16)

    bias = up_b[...]
    up_b_g[...] = jnp.zeros_like(up_b_g)

    @pl.loop(0, rows // TALL)
    def _(i):
        at = pl.ds(pl.multiple_of(i * TALL, TALL), TALL)
        hidden = mul(second[at, :], up[...]) + bias
        grad = mul(cot[at, :], down[...], NT)
        half = 0.5 + 0.5 * lax.erf(hidden * (0.5 ** 0.5))
        slope = half + hidden * (jnp.exp(hidden * hidden * -0.5) * 0.3989422804014327)
        active[at, :] = (hidden * half).astype(BF16)
        low = (grad * slope).astype(BF16)
        grad_hidden[at, :] = low
        up_b_g[...] += jnp.sum(low.astype(F32), axis=0, keepdims=True)

    @pl.loop(0, rows // TALL)
    def _(i):
        at = pl.ds(pl.multiple_of(i * TALL, TALL), TALL)
        more, less = mul(active[at, :], down[...]), mul(grad_hidden[at, :], up[...], NT)

        @pl.when(step == 0)
        def _():
            total[at, :] = more
            back[at, :] = less

        @pl.when(step > 0)
        def _():
            total[at, :] += more
            back[at, :] += less

    @pl.loop(0, BLOCK // TALL)
    def _(i):
        at = pl.ds(pl.multiple_of(i * TALL, TALL), TALL)
        down_g[at, :] = mul(active[:, at], cot[...], TN).astype(down_g.dtype)

    @pl.loop(0, width // TALL)
    def _(i):
        at = pl.ds(pl.multiple_of(i * TALL, TALL), TALL)
        up_g[at, :] = mul(second[:, at], grad_hidden[...], TN).astype(up_g.dtype)

    @pl.when(step == last)
    def _():
        gain_g[...] = jnp.zeros_like(gain_g)
        down_b_g[...] = jnp.zeros_like(down_b_g)

        @pl.loop(0, rows // part)
        def _(i):
            at = pl.ds(pl.multiple_of(i * part, part), part)
            x = middle[at, :]
            factor = lax.rsqrt(jnp.mean(x * x, axis=-1, keepdims=True) + EPS)
            normal = x * factor
            out[at, :] = (x + (total[at, :] + down_b[...])).astype(BF16)
            g = cot[at, :].astype(F32)
            grad = back[at, :]
            gain_g[...] += jnp.sum(grad * normal, axis=0, keepdims=True)
            down_b_g[...] += jnp.sum(g, axis=0, keepdims=True)
            n = grad * gain[...]
            result = g + factor * (n - normal * jnp.mean(n * normal, axis=-1, keepdims=True))
            grad_middle[at, :] = result
            grad_branch[at, :] = result.astype(BF16)


def mlp(middle, cot, gain, up, up_b, down, down_b, sum_type=BF16):
    rows, width = middle.shape
    ff = up.shape[1]
    whole = lambda *s: pl.BlockSpec(s, lambda j: (0,) * len(s), pipeline_mode=pl.Buffered(1))
    row = whole(1, width)
    return pl.pallas_call(
        mlp_kernel,
        grid=(ff // BLOCK,),
        in_specs=[whole(rows, width), whole(rows, width), row, pl.BlockSpec((width, BLOCK), lambda j: (0, j)),
                  pl.BlockSpec((1, BLOCK), lambda j: (0, j)), pl.BlockSpec((BLOCK, width), lambda j: (j, 0)), row],
        out_specs=[whole(rows, width), whole(rows, width), whole(rows, width), pl.BlockSpec((width, BLOCK), lambda j: (0, j)),
                   pl.BlockSpec((BLOCK, width), lambda j: (j, 0)), pl.BlockSpec((1, BLOCK), lambda j: (0, j)), row, row],
        out_shape=[jax.ShapeDtypeStruct(s, d) for s, d in (
            ((rows, width), BF16), ((rows, width), F32), ((rows, width), BF16), ((width, ff), sum_type), ((ff, width), sum_type),
            ((1, ff), F32), ((1, width), F32), ((1, width), F32))],
        scratch_shapes=[pltpu.VMEM((rows, width), BF16), pltpu.VMEM((rows, width), F32), pltpu.VMEM((rows, width), F32),
                        pltpu.VMEM((rows, BLOCK), BF16), pltpu.VMEM((rows, BLOCK), BF16)],
        compiler_params=pltpu.CompilerParams(vmem_limit_bytes=56 * 2 ** 20, dimension_semantics=("arbitrary",)),
        name="mlp",
    )(middle, cot, gain.reshape(1, -1).astype(F32), up, up_b.reshape(1, -1).astype(F32), down, down_b.reshape(1, -1).astype(F32))


PIECE = 128
REACH = 256


def spans(rows):
    return [(max(0, i * PIECE - REACH), i * PIECE, (i + 1) * PIECE) for i in range(rows // PIECE)]


def side_by_side(x, lanes):
    zero = jnp.zeros_like(x)
    return jnp.concatenate([jnp.where(lanes, x, zero), jnp.where(lanes, zero, x)], axis=0)


def fill_bias(bias, start, rows):
    at = 0
    for low, q, high in spans(rows):
        n = high - low
        key = low + lax.broadcasted_iota(jnp.int32, (n, PIECE), 0)
        query = q + lax.broadcasted_iota(jnp.int32, (n, PIECE), 1)
        seen = jnp.logical_and(key <= query, key >= start[:, q:high])
        b = jnp.where(seen, 0.0, -1e30)
        bias[at:at + n, :] = jnp.concatenate([b, b], axis=1)
        at += n


def attend_kernel(q_ref, k_ref, v_ref, start, out, logsum, bias):
    rows, wide = q_ref.shape

    @pl.when(pl.program_id(1) == 0)
    def _():
        fill_bias(bias, start[0], rows)

    lanes = lax.broadcasted_iota(jnp.int32, (PIECE, wide), 1) < wide // 2
    at = 0
    for i, (low, q, high) in enumerate(spans(rows)):
        n = high - low
        queries = side_by_side(q_ref[q:high, :] * 0.125, lanes)
        scores = mul(k_ref[low:high, :], queries, NT) + bias[at:at + n, :]
        peak = jnp.max(scores, axis=0, keepdims=True)
        expo = jnp.exp(scores - peak)
        total = jnp.sum(expo, axis=0, keepdims=True)
        logsum[0, 0, i:i + 1, :] = peak + jnp.log(total)
        attend = (expo * (1.0 / total)).astype(BF16)
        both = mul(attend, v_ref[low:high, :], TN)
        out[q:high, :] = jnp.where(lanes, both[:PIECE], both[PIECE:]).astype(BF16)
        at += n


def attend_specs(rows, pairs):
    block = lambda off: pl.BlockSpec((rows, 128), lambda b, h: (b, off * pairs + h))
    start = pl.BlockSpec((1, 1, rows), lambda b, h: (b, 0, 0))
    logsum = pl.BlockSpec((1, 1, rows // PIECE, 2 * PIECE), lambda b, h: (b, h, 0, 0))
    return block, start, logsum


def attend(project, start):
    batches, rows = start.shape[0], start.shape[2]
    width = project.shape[1] // 3
    pairs = width // 128
    block, start_spec, logsum = attend_specs(rows, pairs)
    return pl.pallas_call(
        attend_kernel,
        grid=(batches, pairs),
        in_specs=[block(0), block(1), block(2), start_spec],
        out_specs=[block(0), logsum],
        out_shape=[jax.ShapeDtypeStruct((batches * rows, width), BF16),
                   jax.ShapeDtypeStruct((batches, pairs, rows // PIECE, 2 * PIECE), F32)],
        scratch_shapes=[pltpu.VMEM((sum(h - l for l, _, h in spans(rows)), 2 * PIECE), F32)],
        compiler_params=pltpu.CompilerParams(vmem_limit_bytes=40 * 2 ** 20, dimension_semantics=("arbitrary", "arbitrary")),
        name="attend",
    )(project, project, project, start)


def attend_back_kernel(q_ref, k_ref, v_ref, g_ref, start, logsum, out, bias, k_sum, v_sum):
    rows, wide = q_ref.shape

    @pl.when(pl.program_id(1) == 0)
    def _():
        fill_bias(bias, start[0], rows)

    lanes = lax.broadcasted_iota(jnp.int32, (PIECE, wide), 1) < wide // 2
    at = 0
    k_sum[...] = jnp.zeros_like(k_sum)
    v_sum[...] = jnp.zeros_like(v_sum)
    for i, (low, q, high) in enumerate(spans(rows)):
        n = high - low
        queries = side_by_side(q_ref[q:high, :] * 0.125, lanes)
        grads = side_by_side(g_ref[q:high, :], lanes)
        keys, values = k_ref[low:high, :], v_ref[low:high, :]
        scores = mul(keys, queries, NT) + bias[at:at + n, :]
        full = jnp.exp(scores - logsum[0, 0, i:i + 1, :])
        grad = mul(values, grads, NT)
        v_sum[low:high, :] += mul(full.astype(BF16), grads)
        total = jnp.sum(full * grad, axis=0, keepdims=True)
        grad_scores = (full * (grad - total)).astype(BF16)
        k_sum[low:high, :] += mul(grad_scores, queries)
        both = mul(grad_scores, keys, TN) * 0.125
        out[0, q:high, :] = jnp.where(lanes, both[:PIECE], both[PIECE:]).astype(BF16)
        at += n
    out[1] = k_sum[...].astype(BF16)
    out[2] = v_sum[...].astype(BF16)


def attend_back(project, grad, start, logsum):
    batches, rows = start.shape[0], start.shape[2]
    width = project.shape[1] // 3
    pairs = width // 128
    block, start_spec, logsum_spec = attend_specs(rows, pairs)
    return pl.pallas_call(
        attend_back_kernel,
        grid=(batches, pairs),
        in_specs=[block(0), block(1), block(2), block(0), start_spec, logsum_spec],
        out_specs=pl.BlockSpec((3, rows, 128), lambda b, h: (0, b, h)),
        out_shape=jax.ShapeDtypeStruct((3, batches * rows, width), BF16),
        scratch_shapes=[pltpu.VMEM((sum(h - l for l, _, h in spans(rows)), 2 * PIECE), F32),
                        pltpu.VMEM((rows, 128), F32), pltpu.VMEM((rows, 128), F32)],
        compiler_params=pltpu.CompilerParams(vmem_limit_bytes=40 * 2 ** 20, dimension_semantics=("arbitrary", "arbitrary")),
        name="attend_back",
    )(project, project, project, grad, start, logsum)


class Gather:
    def __init__(self, table, bits, where, shards, fulls, local_sem, send_sem, recv_sem):
        self.table, self.bits, self.steps = table, bits, len(table)
        self.partners = [partner(table, bits, where, k) for k in range(len(table))]
        self.shards, self.fulls = shards, fulls
        self.local_sem, self.send_sem, self.recv_sem = local_sem, send_sem, recv_sem
        two = [o[::-1] for o in orders(table)]
        self.units = units_of([s.shape for s in shards])
        self.chunks = [piece + (two[(h + u) % 2],) for u, unit in enumerate(self.units) for h, piece in enumerate(unit)]
        self.events = timetable(self.units, self.steps, SKEW)
        self.at = 0
        pieces = {i: [e for e in self.events if self.chunks[e[0]][0] == i and e[1] == 1] for i in range(len(shards))}
        self.first = {found[0] for found in pieces.values()}

    def own(self, i):
        return pltpu.make_async_copy(self.shards[i], self.fulls[i].at[tuple(self.bits)], self.local_sem.at[i])

    def copy(self, c, s):
        i, rows, cols, order = self.chunks[c]
        index = tuple(slice(None) if k in order[:s] else self.bits[k] for k in range(self.steps))
        there = self.fulls[i].at[index + (rows, cols)]
        return pltpu.make_async_remote_copy(
            src_ref=self.shards[i].at[rows, cols] if s == 0 else there, dst_ref=there,
            send_sem=self.send_sem.at[c, s], recv_sem=self.recv_sem.at[c, s],
            device_id=self.partners[order[s]], device_id_type=pl.DeviceIdType.MESH)

    def event(self, c, s):
        i = self.chunks[c][0]
        if s > 0:
            self.copy(c, s - 1).wait_recv()
            if (c, s) in self.first:
                self.own(i).wait()
        if s < self.steps:
            self.copy(c, s).start()

    def run(self, count):
        for c, s in self.events[self.at:self.at + count]:
            self.event(c, s)
        self.at = min(self.at + count, len(self.events))

    def needed(self, array, unit):
        piece, last = 0, 0
        seen = -1
        for u in self.units:
            seen += u[0][0] == array
            if u[0][0] == array and seen <= unit:
                ends = [self.events.index((piece + h, self.steps)) for h in range(len(u))]
                last = max(last, max(ends) + 1)
            piece += len(u)
        return max(0, last - self.at)

    def until(self, array, unit):
        self.run(self.needed(array, unit))

    def finish(self):
        self.run(len(self.events))
        for c in range(len(self.chunks)):
            for s in range(self.steps):
                self.copy(c, s).wait_send()


def spread(index, slots, engine, count):
    done = 0
    for slot in range(slots):
        upto = count * (slot + 1) // slots
        if upto > done:
            pl.when(index == slot)(functools.partial(engine.run, upto - done))
            done = upto


def row_of(table, offset, width, total):
    owners = table.shape[0]
    lane = lax.broadcasted_iota(jnp.int32, (128, total), 0)
    col = lax.broadcasted_iota(jnp.int32, (128, total), 1)
    pick = jnp.where(lane == offset + col % width, 1.0, 0.0).astype(BF16)
    owner = lax.broadcasted_iota(jnp.int32, (owners, total), 0)
    mine = owner == lax.broadcasted_iota(jnp.int32, (owners, total), 1) // width
    return jnp.sum(jnp.where(mine, mul(table, pick), 0.0), axis=0, keepdims=True)


def rows_at(i, size):
    return pl.ds(pl.multiple_of(i * size, size), size)


def norm_rows(x):
    factor = lax.rsqrt(jnp.mean(x * x, axis=-1, keepdims=True) + EPS)
    return x * factor, factor


def attend_pair(q_ref, k_ref, v_ref, bias, out, logsum):
    rows, wide = q_ref.shape
    lanes = lax.broadcasted_iota(jnp.int32, (PIECE, wide), 1) < wide // 2
    at = 0
    for i, (low, q, high) in enumerate(spans(rows)):
        n = high - low
        queries = side_by_side(q_ref[q:high, :] * 0.125, lanes)
        scores = mul(k_ref[low:high, :], queries, NT) + bias[at:at + n, :]
        peak = jnp.max(scores, axis=0, keepdims=True)
        expo = jnp.exp(scores - peak)
        total = jnp.sum(expo, axis=0, keepdims=True)
        logsum[i:i + 1, :] = peak + jnp.log(total)
        attend_low = (expo * (1.0 / total)).astype(BF16)
        both = mul(attend_low, v_ref[low:high, :], TN)
        out[q:high, :] = jnp.where(lanes, both[:PIECE], both[PIECE:]).astype(BF16)
        at += n


def forward_kernel(table, x_ref, cot_hbm, start, small_s, qkv_s, out_s, down_s, up_s,
                   small, qkv, out_w, down, up, project_o, attended_o, entered_o, output_o, middle_o, branch_o, up_g, down_g,
                   logsum, first_row, up_b_g, gain_g, down_b_g,
                   cot, entered, project, attended, middle, total, back, active, grad_hidden, up_v, down_v, up_gv, down_gv, small_v, rows_v, bias_v, bias,
                   local_sem, send_sem, recv_sem, sems):
    bits, where = my_bits(table)
    steps, owners = len(table), 2 ** len(table)
    rows, width = x_ref.shape
    ff = up_s.shape[1]
    length = start.shape[2]
    pairs = width // 128
    g = Gather(table, bits, where, [small_s, qkv_s, out_s, down_s, up_s], [small, qkv, out_w, down, up], local_sem, send_sem, recv_sem)
    SMALL, QKV, OUT, DOWN, UP = range(5)
    greet(table, bits, where)
    for i in range(5):
        g.own(i).start()

    def move(src, dst, k):
        return pltpu.make_async_copy(src, dst, sems.at[k])

    move(cot_hbm, cot, 0).start()
    g.until(SMALL, 0)
    move(small, small_v, 1).start()
    move(small, small_v, 1).wait()
    held = small_v[...].reshape(owners, small_s.shape[0], 128)
    first_row[...] = row_of(held[:, 1], 0, width // owners, width)
    rows_v[0:1, :] = row_of(held[:, 1], width // owners, width // owners, width)
    rows_v[1:2, :] = row_of(held[:, 1], 2 * (width // owners), width // owners, width)
    bias_v[...] = row_of(held[:, 0], 0, ff // owners, ff)
    part = 128

    @pl.loop(0, rows // part)
    def _(i):
        at = rows_at(i, part)
        normal, _ = norm_rows(x_ref[at, :].astype(F32))
        entered[at, :] = (normal * first_row[...]).astype(BF16)
    move(entered, entered_o, 2).start()

    for u in range(3):
        g.until(QKV, u)
        fetch = move(qkv.at[(slice(None),) * (steps + 1) + (slice(u * width, (u + 1) * width),)], up_v.at[u % 2], 3)
        fetch.start()
        fetch.wait()

        @pl.loop(0, rows // TALL)
        def _(i):
            at = rows_at(i, TALL)
            project[at, u * width:(u + 1) * width] = mul(entered[at, :], up_v[u % 2].reshape(width, width)).astype(BF16)
            spread_fixed(i, rows // TALL, g, 8)
        g.at += 8
    move(project, project_o, 4).start()
    loops = rows // length * pairs
    slot_events = 64

    @pl.loop(0, loops)
    def _(i):
        b, h = i // pairs, i % pairs

        @pl.when(h == 0)
        def _():
            fill_bias(bias, start[b], length)
        at = rows_at(b, length)
        lanes = [pl.ds(pl.multiple_of(k * width + h * 128, 128), 128) for k in range(3)]
        q_ref, k_ref, v_ref = [project.at[at, lane] for lane in lanes]
        attend_pair(q_ref, k_ref, v_ref, bias, attended.at[at, lanes[0]], logsum.at[b, h])
        spread_fixed(i, loops, g, slot_events)
    g.at += slot_events
    move(attended, attended_o, 5).start()
    g.until(OUT, 0)
    fetch = move(out_w, up_v.at[1], 3)
    fetch.start()
    fetch.wait()
    move(entered, entered_o, 2).wait()
    second = entered

    @pl.loop(0, rows // TALL)
    def _(i):
        at = rows_at(i, TALL)
        x = x_ref[at, :].astype(F32) + mul(attended[at, :], up_v[1].reshape(width, width))
        middle[at, :] = x
        normal, _ = norm_rows(x)
        second[at, :] = (normal * rows_v[0:1, :]).astype(BF16)
        spread_fixed(i, rows // TALL, g, 8)
    g.at += 8
    g.until(UP, 0)
    move(cot_hbm, cot, 0).wait()
    blocks = ff // BLOCK
    lead = blocks.bit_length() - 1

    def fetches(j, slot):
        top = tuple((j // 2 ** (lead - 1 - k)) % 2 for k in range(lead))
        return [move(up.at[(slice(None),) * (steps + 1) + (rows_at(j, BLOCK),)], up_v.at[slot], 6 + slot),
                move(down.at[top], down_v.at[slot], 8 + slot)]

    def stores(j, slot):
        return [move(up_gv.at[slot], up_g.at[:, rows_at(j, BLOCK)], 10 + slot), move(down_gv.at[slot], down_g.at[rows_at(j, BLOCK), :], 12 + slot)]

    for f in fetches(0, 0):
        f.start()
    left = len(g.events) - g.at
    per = rows // TALL

    @pl.loop(0, blocks)
    def _(j):
        slot = j % 2
        for f in fetches(j, slot):
            f.wait()

        @pl.when(j >= 2)
        def _():
            for f in stores(j, slot):
                f.wait()
        lane = rows_at(j, BLOCK)
        bias_row = bias_v[:, lane]
        up_b_g[:, lane] = jnp.zeros((1, BLOCK), F32)

        @pl.loop(0, per)
        def _(i):
            at = rows_at(i, TALL)
            hidden = mul(second[at, :], up_v[slot].reshape(width, BLOCK)) + bias_row
            grad = mul(cot[at, :], down_v[slot].reshape(BLOCK, width), NT)
            half = 0.5 + 0.5 * lax.erf(hidden * (0.5 ** 0.5))
            slope = half + hidden * (jnp.exp(hidden * hidden * -0.5) * 0.3989422804014327)
            active[at, :] = (hidden * half).astype(BF16)
            low = (grad * slope).astype(BF16)
            grad_hidden[at, :] = low
            up_b_g[:, lane] += jnp.sum(low.astype(F32), axis=0, keepdims=True)
            pl.when(j == 0)(lambda: spread_fixed(i, per, g, left // 2))
        mark = g.at
        g.at += left // 2

        @pl.loop(0, per)
        def _(i):
            at = rows_at(i, TALL)
            more, less = mul(active[at, :], down_v[slot].reshape(BLOCK, width)), mul(grad_hidden[at, :], up_v[slot].reshape(width, BLOCK), NT)

            @pl.when(j == 0)
            def _():
                total[at, :] = more
                back[at, :] = less
                spread_fixed(i, per, g, left - left // 2)

            @pl.when(j > 0)
            def _():
                total[at, :] += more
                back[at, :] += less
        g.at = mark

        @pl.when(j + 1 < blocks)
        def _():
            for f in fetches(j + 1, 1 - slot):
                f.start()

        @pl.loop(0, BLOCK // TALL)
        def _(i):
            at = rows_at(i, TALL)
            down_gv[slot, at, :] = mul(active[:, at], cot[...], TN).astype(BF16)

        @pl.loop(0, width // TALL)
        def _(i):
            at = rows_at(i, TALL)
            up_gv[slot, at, :] = mul(second[:, at], grad_hidden[...], TN).astype(BF16)
        for f in stores(j, slot):
            f.start()
    g.at += left
    move(attended, attended_o, 5).wait()
    output, branch = entered, attended
    gain_g[...] = jnp.zeros_like(gain_g)
    down_b_g[...] = jnp.zeros_like(down_b_g)

    @pl.loop(0, rows // part)
    def _(i):
        at = rows_at(i, part)
        x = middle[at, :]
        normal, factor = norm_rows(x)
        output[at, :] = (x + (total[at, :] + rows_v[1:2, :])).astype(BF16)
        c = cot[at, :].astype(F32)
        grad = back[at, :]
        gain_g[...] += jnp.sum(grad * normal, axis=0, keepdims=True)
        down_b_g[...] += jnp.sum(c, axis=0, keepdims=True)
        n = grad * rows_v[0:1, :]
        result = c + factor * (n - normal * jnp.mean(n * normal, axis=-1, keepdims=True))
        back[at, :] = result
        branch[at, :] = result.astype(BF16)
    last = [move(output, output_o, 2), move(back, middle_o, 3), move(branch, branch_o, 5)]
    for f in last:
        f.start()
    for f in last + [move(project, project_o, 4)] + stores(blocks - 2, blocks % 2) + stores(blocks - 1, (blocks - 1) % 2):
        f.wait()
    g.finish()


def spread_fixed(index, slots, engine, count):
    begin = engine.at
    spread(index, slots, engine, count)
    engine.at = begin


def forward(frames, cot, start, packed, qkv, out, down, up, sizes, collective_id):
    table = bit_table(sizes)
    steps, owners = len(table), 2 ** len(table)
    rows, width = frames.shape
    ff = up.shape[1]
    batches, length = start.shape[0], start.shape[2]
    pairs = width // 128
    two = (2,) * steps
    shards = [packed, qkv, out, down, up]
    pieces = sum(len(u) for u in units_of([a.shape for a in shards]))
    anywhere, vmem = pl.BlockSpec(memory_space=pl.ANY), pl.BlockSpec(memory_space=pltpu.VMEM)
    hbm_out = [(two + a.shape, BF16) for a in shards] + [((rows, 3 * width), BF16), ((rows, width), BF16), ((rows, width), BF16),
               ((rows, width), BF16), ((rows, width), F32), ((rows, width), BF16), ((width, ff), BF16), ((ff, width), BF16)]
    vmem_out = [((batches, pairs, length // PIECE, 2 * PIECE), F32), ((1, width), F32), ((1, ff), F32), ((1, width), F32), ((1, width), F32)]
    lead = (ff // BLOCK).bit_length() - 1
    V = pltpu.VMEM
    return pl.pallas_call(
        functools.partial(forward_kernel, table),
        out_shape=[jax.ShapeDtypeStruct(s, d) for s, d in hbm_out + vmem_out],
        in_specs=[vmem, anywhere, vmem] + [anywhere] * 5,
        out_specs=[anywhere] * len(hbm_out) + [vmem] * len(vmem_out),
        scratch_shapes=[V((rows, width), BF16), V((rows, width), BF16), V((rows, 3 * width), BF16), V((rows, width), BF16), V((rows, width), F32),
                        V((rows, width), F32), V((rows, width), F32), V((rows, BLOCK), BF16), V((rows, BLOCK), BF16),
                        V((2,) + two + (width // owners, BLOCK), BF16), V((2,) + two[lead:] + (ff // owners, width), BF16),
                        V((2, width, BLOCK), BF16), V((2, BLOCK, width), BF16), V(two + packed.shape, BF16), V((2, width), F32), V((1, ff), F32),
                        V((sum(h - l for l, _, h in spans(length)), 2 * PIECE), F32),
                        pltpu.SemaphoreType.DMA((5,)), pltpu.SemaphoreType.DMA((pieces, steps)), pltpu.SemaphoreType.DMA((pieces, steps)),
                        pltpu.SemaphoreType.DMA((14,))],
        compiler_params=pltpu.CompilerParams(collective_id=collective_id, has_side_effects=True, vmem_limit_bytes=58 * 2 ** 20),
        name="forward",
    )(frames, cot, start, *shards)


class Scatter:
    def __init__(self, table, bits, where, parts, outs, recv, stage, small, local_sem, send_sem, recv_sem):
        self.table, self.bits, self.steps = table, bits, len(table)
        self.partners = [partner(table, bits, where, k) for k in range(len(table))]
        self.parts, self.outs, self.recv, self.stage = parts, outs, recv, stage
        self.local_sem, self.send_sem, self.recv_sem = local_sem, send_sem, recv_sem
        self.small_recv = small
        self.units, self.chunks = scatter_chunks(table, [p.shape[-2:] for p in parts])
        self.events = timetable(self.units, self.steps, SKEW)
        self.at = 0

    def into(self, c, s):
        if self.chunks[c][0] == len(self.parts) - 1:
            return self.small_recv[s]
        return self.recv[s].at[c]

    def half(self, c, bit):
        i, rows, cols, order = self.chunks[c]
        index = tuple(bit if k == order[0] else slice(None) for k in range(self.steps))
        return self.parts[i].at[index + (rows, cols)]

    def load(self, c):
        return pltpu.make_async_copy(self.half(c, self.bits[self.chunks[c][3][0]]), self.stage.at[c % 4], self.local_sem.at[c % 4])

    def left(self, c, s, last):
        order, out = self.chunks[c][3], []
        for k in range(self.steps):
            if k == order[0]:
                continue
            if k in order[1:s]:
                out.append(self.bits[k])
            elif s < self.steps and k == order[s] and last is not None:
                out.append(last)
            else:
                out.append(slice(None))
        return tuple(out)

    def copy(self, c, s):
        k = self.chunks[c][3][s]
        other = 1 - self.bits[k]
        return pltpu.make_async_remote_copy(
            src_ref=self.half(c, other) if s == 0 else self.into(c, 0).at[self.left(c, s, other)], dst_ref=self.into(c, s),
            send_sem=self.send_sem.at[c, s], recv_sem=self.recv_sem.at[c, s],
            device_id=self.partners[k], device_id_type=pl.DeviceIdType.MESH)

    def add(self, c, s):
        i, rows, cols, order = self.chunks[c]
        small = i == len(self.parts) - 1
        total, got = self.into(c, 0), self.into(c, s)
        free = self.steps - s - 1
        if free == 0:
            own = total[self.left(c, self.steps, None)]
            self.outs[i][rows, cols] = own.astype(F32) + got[...].astype(F32)
            return
        base = self.left(c, s, self.bits[order[s]]) if s else (slice(None),) * free
        mine = self.half(c, self.bits[order[0]]) if small else self.stage.at[c % 4]

        @pl.loop(0, 2 ** free)
        def _(j):
            spot = [(j // 2 ** (free - 1 - b)) % 2 for b in range(free)]
            rest = iter(spot)
            here = tuple(next(rest) if isinstance(e, slice) else e for e in base)
            more = mine[tuple(spot)] if s == 0 else got[tuple(spot)]
            total[here] = (total[here].astype(F32) + more.astype(F32)).astype(total.dtype)

    def event(self, c, s):
        small = self.chunks[c][0] == len(self.parts) - 1
        if s == 0:
            self.copy(c, 0).start()
            if not small:
                self.load(c).start()
            return
        self.copy(c, s - 1).wait_recv()
        if s == 1 and not small:
            self.load(c).wait()
        self.add(c, s - 1)
        if s < self.steps:
            self.copy(c, s).start()

    def run(self, count):
        for c, s in self.events[self.at:self.at + count]:
            self.event(c, s)
        self.at = min(self.at + count, len(self.events))

    def before(self, part):
        return next(n for n, (c, s) in enumerate(self.events) if self.chunks[c][0] == part)

    def finish(self):
        self.run(len(self.events))
        for c in range(len(self.chunks)):
            for s in range(self.steps):
                self.copy(c, s).wait_send()


def scatter_chunks(table, tails):
    two = orders(table)
    units = units_of(tails)
    return units, [piece + (two[(h + u) % 2],) for u, unit in enumerate(units) for h, piece in enumerate(unit)]


def attend_back_pair(q_ref, k_ref, v_ref, g_ref, bias, logsum, k_sum, v_sum):
    rows, wide = q_ref.shape
    lanes = lax.broadcasted_iota(jnp.int32, (PIECE, wide), 1) < wide // 2
    at = 0
    k_sum[...] = jnp.zeros_like(k_sum)
    v_sum[...] = jnp.zeros_like(v_sum)
    for i, (low, q, high) in enumerate(spans(rows)):
        n = high - low
        queries = side_by_side(q_ref[q:high, :] * 0.125, lanes)
        grads = side_by_side(g_ref[q:high, :], lanes)
        keys, values = k_ref[low:high, :], v_ref[low:high, :]
        scores = mul(keys, queries, NT) + bias[at:at + n, :]
        full = jnp.exp(scores - logsum[i:i + 1, :])
        grad = mul(values, grads, NT)
        v_sum[low:high, :] += mul(full.astype(BF16), grads)
        total = jnp.sum(full * grad, axis=0, keepdims=True)
        grad_scores = (full * (grad - total)).astype(BF16)
        k_sum[low:high, :] += mul(grad_scores, queries)
        both = mul(grad_scores, keys, TN) * 0.125
        q_ref[q:high, :] = jnp.where(lanes, both[:PIECE], both[PIECE:]).astype(BF16)
        at += n
    k_ref[...] = k_sum[...].astype(BF16)
    v_ref[...] = v_sum[...].astype(BF16)


def by_owner(row, offset, owners):
    total = row.shape[1]
    width = total // owners
    lane = lax.broadcasted_iota(jnp.int32, (128, total), 0)
    col = lax.broadcasted_iota(jnp.int32, (128, total), 1)
    pick = jnp.where(lane == offset + col % width, 1.0, 0.0)
    owner = lax.broadcasted_iota(jnp.int32, (owners, total), 0)
    mine = owner == lax.broadcasted_iota(jnp.int32, (owners, total), 1) // width
    return lax.dot_general(jnp.where(mine, row, 0.0), pick, NT, precision=lax.Precision.HIGHEST, preferred_element_type=F32)


def backward_kernel(table, x_hbm, start, project_hbm, attended_hbm, entered_hbm, middle_hbm, branch_hbm, qkv, out_w, up_g, down_g,
                    logsum, first_row, up_b_g, gain_g, down_b_g,
                    grad_o, out_g, q_g, k_g, v_g, up_r, down_r, out_r, q_r, k_r, v_r, small_r,
                    project, attended, branch, entered, weight, held, back, old, bias, k_sum, v_sum, small, stage,
                    r0, r1, r2, r3, r4, s0, s1, s2, s3, s4, local_sem, send_sem, recv_sem, sems):
    bits, where = my_bits(table)
    steps, owners = len(table), 2 ** len(table)
    rows, width = attended.shape
    length = start.shape[2]
    pairs = width // 128
    e = Scatter(table, bits, where, [up_g, down_g, out_g, q_g, k_g, v_g, small], [up_r, down_r, out_r, q_r, k_r, v_r, small_r],
                [r0, r1, r2, r3, r4], stage, [s0, s1, s2, s3, s4], local_sem, send_sem, recv_sem)

    def move(src, dst, k):
        return pltpu.make_async_copy(src, dst, sems.at[k])

    for args in ((attended_hbm, attended, 0), (branch_hbm, branch, 1), (out_w, weight.at[0], 2), (project_hbm, project, 3), (entered_hbm, entered, 4)):
        move(*args).start()
    greet(table, bits, where)
    first_q = e.before(3)
    e.run(2)
    move(attended_hbm, attended, 0).wait()
    move(branch_hbm, branch, 1).wait()
    per = rows // TALL
    deep = (width // TALL).bit_length() - 1

    def place(slot, i):
        return held.at[(slot,) + tuple((i // 2 ** (deep - 1 - k)) % 2 for k in range(deep))]

    def put(slot, i, value):
        ref = place(slot, i)
        ref[...] = value.reshape(ref.shape).astype(BF16)

    @pl.loop(0, width // TALL)
    def _(i):
        put(0, i, mul(attended[:, rows_at(i, TALL)], branch[...], TN))
        spread_fixed(i, width // TALL, e, 4)
    e.at += 4
    move(held.at[0], out_g, 5).start()
    move(out_w, weight.at[0], 2).wait()

    @pl.loop(0, per)
    def _(i):
        at = rows_at(i, TALL)
        branch[at, :] = mul(branch[at, :], weight[0].reshape(width, width), NT).astype(BF16)
        spread_fixed(i, per, e, 4)
    e.at += 4
    move(x_hbm, attended, 0).start()
    move(project_hbm, project, 3).wait()
    move(held.at[0], out_g, 5).wait()
    loops = rows // length * pairs
    count = first_q - e.at - 12

    @pl.loop(0, loops)
    def _(i):
        b, h = i // pairs, i % pairs

        @pl.when(h == 0)
        def _():
            fill_bias(bias, start[b], length)
        at = rows_at(b, length)
        lanes = [pl.ds(pl.multiple_of(k * width + h * 128, 128), 128) for k in range(3)]
        q_ref, k_ref, v_ref = [project.at[at, lane] for lane in lanes]
        attend_back_pair(q_ref, k_ref, v_ref, branch.at[at, lanes[0]], bias, logsum.at[b, h], k_sum, v_sum)
        spread_fixed(i, loops, e, count)
    e.at += count
    move(entered_hbm, entered, 4).wait()

    def fetch(u):
        return move(qkv.at[(slice(None),) * (steps + 1) + (slice(u * width, (u + 1) * width),)], weight.at[(u + 1) % 2], 6 + u % 2)

    fetch(0).start()
    fetch(1).start()
    for u, part in enumerate((q_g, k_g, v_g)):
        slot = (u + 1) % 2
        if u == 2:
            move(held.at[slot], q_g, 8).wait()

        @pl.loop(0, width // TALL)
        def _(i):
            put(slot, i, mul(entered[:, rows_at(i, TALL)], project[:, u * width:(u + 1) * width], TN))
            spread_fixed(i, width // TALL, e, 4)
        e.at += 4
        move(held.at[slot], part, 8 + u).start()
    for u, part in enumerate((q_g, k_g, v_g)):
        if u:
            move(held.at[(u + 1) % 2], part, 8 + u).wait()
    mark = e.before(6)
    each = (mark - e.at) // 3
    for u in range(3):
        fetch(u).wait()

        @pl.loop(0, per)
        def _(i):
            at = rows_at(i, TALL)
            more = mul(project[at, u * width:(u + 1) * width], weight[(u + 1) % 2].reshape(width, width), NT)
            if u == 0:
                back[at, :] = more
            else:
                back[at, :] += more
            spread_fixed(i, per, e, each)
        e.at += each
        if u == 0:
            fetch(2).start()
    move(x_hbm, attended, 0).wait()
    part = old.shape[1]
    first_g = jnp.zeros((1, width), F32)

    def older(i):
        return move(middle_hbm.at[rows_at(i, part), :], old.at[i % 2], 11 + i % 2)

    older(0).start()

    @pl.loop(0, rows // part, init_carry=first_g)
    def first_g(i, first_g):
        @pl.when(i + 1 < rows // part)
        def _():
            older(i + 1).start()
        older(i).wait()
        at = rows_at(i, part)
        normal, factor = norm_rows(attended[at, :].astype(F32))
        grad = back[at, :]
        n = grad * first_row[...]
        back[at, :] = old[i % 2] + factor * (n - normal * jnp.mean(n * normal, axis=-1, keepdims=True))
        return first_g + jnp.sum(grad * normal, axis=0, keepdims=True)
    move(back, grad_o, 13).start()
    share = width // owners
    zero = jnp.zeros((owners, 6, 128), F32)
    vectors = by_owner(first_g, 0, owners) + by_owner(gain_g[...], share, owners) + by_owner(down_b_g[...], 2 * share, owners)
    packed = jnp.concatenate([by_owner(up_b_g[...], 0, owners)[:, None], vectors[:, None], zero], axis=1)
    small[...] = packed.reshape(small.shape)
    e.finish()
    move(back, grad_o, 13).wait()


def backward(frames, start, project, attended, entered, middle, branch, qkv, out_w, up_g, down_g, logsum, first_row, up_b_g, gain_g, down_b_g,
             sizes, collective_id):
    table = bit_table(sizes)
    steps, owners = len(table), 2 ** len(table)
    rows, width = frames.shape
    length = start.shape[2]
    two = (2,) * steps
    share = width // owners
    up_g = up_g.reshape(two + (share, up_g.shape[1]))
    down_g = down_g.reshape(two + (down_g.shape[0] // owners, width))
    small = (8, 128)
    tails = [up_g.shape[-2:], down_g.shape[-2:]] + [(share, width)] * 4 + [small]
    units, chunks = scatter_chunks(table, tails)
    m = len(chunks)
    piece = (min(ROWS, share), WIDE)
    anywhere, vmem = pl.BlockSpec(memory_space=pl.ANY), pl.BlockSpec(memory_space=pltpu.VMEM)
    V = pltpu.VMEM
    out_shape = [((rows, width), F32)] + [(two + (share, width), BF16)] * 4 + [(t, F32) for t in tails]
    return pl.pallas_call(
        functools.partial(backward_kernel, table),
        out_shape=[jax.ShapeDtypeStruct(s, d) for s, d in out_shape],
        in_specs=[anywhere, vmem] + [anywhere] * 9 + [vmem] * 5,
        out_specs=[anywhere] * 5 + [vmem] * 7,
        scratch_shapes=[V((rows, 3 * width), BF16), V((rows, width), BF16), V((rows, width), BF16), V((rows, width), BF16),
                        V((2,) + two + (share, width), BF16), V((2,) + two + (share, width), BF16), V((rows, width), F32), V((2, 128, width), F32),
                        V((sum(h - l for l, _, h in spans(length)), 2 * PIECE), F32), V((length, 128), F32), V((length, 128), F32),
                        V(two + small, F32), V((4,) + two[1:] + piece, BF16)]
        + [V((m - 1,) + two[s + 1:] + piece, BF16) for s in range(steps)] + [V(two[s + 1:] + small, F32) for s in range(steps)]
        + [pltpu.SemaphoreType.DMA((4,)), pltpu.SemaphoreType.DMA((m, steps)), pltpu.SemaphoreType.DMA((m, steps)), pltpu.SemaphoreType.DMA((14,))],
        compiler_params=pltpu.CompilerParams(collective_id=collective_id, has_side_effects=True, vmem_limit_bytes=60 * 2 ** 20),
        name="backward",
    )(frames, start, project, attended, entered, middle, branch, qkv, out_w, up_g, down_g, logsum, first_row, up_b_g, gain_g, down_b_g)


def pack(first, second, up_b, down_b):
    rest = jnp.concatenate([first, second, down_b])
    rest = jnp.pad(rest, (0, 128 - rest.shape[0]))
    return jnp.pad(jnp.stack([jnp.pad(up_b, (0, 128 - up_b.shape[0])), rest]), ((0, 14), (0, 0)))


def fits(sizes, shards):
    return all(s & (s - 1) == 0 for s in sizes.values()) and all(a.shape[0] % ROWS == 0 for a in shards)


def item_starts(lengths, rows):
    slots = jnp.arange(lengths.shape[1], dtype=jnp.int32)
    ends = jnp.sum(jnp.where(slots[None, :, None] <= slots[None, None, :], lengths[:, :, None], 0), axis=1)
    position = jnp.arange(rows, dtype=jnp.int32)[None, None, :]
    return jnp.max(jnp.where(ends[:, :, None] <= position, ends[:, :, None], 0), axis=1, keepdims=True)


def normalize(x_val):
    factor = lax.rsqrt(jnp.mean(x_val * x_val, axis=-1, keepdims=True) + EPS)
    return (x_val * factor, factor)


def norm_back(normal, factor, gain, grad_out):
    gain_grad = jnp.sum(grad_out * normal, axis=0)
    scaled = grad_out * gain
    inner = jnp.mean(scaled * normal, axis=-1, keepdims=True)
    return (factor * (scaled - normal * inner), gain_grad)


def block_pass(frames, lengths, cotangent, params, sum_type):
    first, qkv, out, second, up, up_b, down, down_b = params
    batches, rows, width = frames.shape
    x_val = frames.reshape(batches * rows, width).astype(F32)
    cot = cotangent.reshape(batches * rows, width)
    start = item_starts(lengths, rows)
    normal, factor = normalize(x_val)
    gain = first.astype(F32)
    entered = (normal * gain).astype(BF16)
    project = mul(entered, qkv).astype(BF16)
    attended, logsum = attend(project, start)
    middle = x_val + mul(attended, out)
    output, grad_middle, grad_branch, up_g, down_g, up_b_g, second_g, down_b_g = mlp(middle, cot, second, up, up_b, down, down_b, sum_type)
    out_g = mul(attended, grad_branch, TN)
    grad_attended = mul(grad_branch, out, NT).astype(BF16)
    grads = attend_back(project, grad_attended, start, logsum)
    qkv_g = [mul(entered, grads[j], TN) for j in range(3)]
    grad_entered = sum(mul(grads[j], qkv[:, j * width:(j + 1) * width], NT) for j in range(3))
    back, first_g = norm_back(normal, factor, gain, grad_entered)
    shape = frames.shape
    return (output.reshape(shape), (grad_middle + back).reshape(shape), (down_g, up_g, out_g, *qkv_g),
            (first_g, second_g.reshape(-1), up_b_g.reshape(-1), down_b_g.reshape(-1)))


def body(sizes, frames, lengths, cotangent, *shards):
    weights = [shards[i] for i in (1, 2, 4, 6)]
    vectors = [shards[i] for i in (0, 3, 5, 7)]
    shape = frames.shape
    if fits(sizes, weights):
        qkv_s, out_s, up_s, down_s = weights
        flat = (shape[0] * shape[1], shape[2])
        x_val, cot = frames.reshape(flat), cotangent.reshape(flat)
        start = item_starts(lengths[:, 0], shape[1])
        (_, qkv, out, _, _, project, attended, entered, output, middle, branch, up_g, down_g, logsum, first, up_b_g, second_g, down_b_g) = forward(
            x_val, cot, start, pack(*vectors), qkv_s, out_s, down_s, up_s, sizes, 1)
        frames_grad, _, _, _, _, up_g, down_g, out_g, q_g, k_g, v_g, small = backward(
            x_val, start, project, attended, entered, middle, branch, qkv, out, up_g, down_g, logsum, first, up_b_g, second_g, down_b_g, sizes, 2)
        output, frames_grad = output.reshape(shape), frames_grad.reshape(shape)
        share = vectors[0].shape[0]
        first_g, second_g, down_b_g = [small[1, k * share:(k + 1) * share] for k in range(3)]
        up_b_g, qkv_g = small[0, :vectors[2].shape[0]], [q_g, k_g, v_g]
    else:
        qkv, out, up, down = [lax.all_gather(w, AXES, axis=0, tiled=True) for w in weights]
        first, second, up_b, down_b = [lax.all_gather(v, AXES, axis=0, tiled=True) for v in vectors]
        params = (first, qkv, out, second, up, up_b, down, down_b)
        output, frames_grad, big, small = block_pass(frames, lengths[:, 0], cotangent, params, F32)
        down_g, up_g, out_g, *qkv_g = [lax.psum_scatter(g, AXES, scatter_dimension=0, tiled=True) for g in big]
        first_g, second_g, up_b_g, down_b_g = [lax.psum_scatter(g, AXES, scatter_dimension=0, tiled=True) for g in small]
    return (output, frames_grad, first_g, jnp.concatenate(qkv_g, axis=1), out_g, second_g, up_g, up_b_g, down_g, down_b_g)


def solution(mesh):
    in_specs = (
        P(None, ("dp", "fsdp"), None),
        P(None, ("dp", "fsdp"), None),
        P(None, ("dp", "fsdp"), None),
        P(("dp", "fsdp")),
        P(("dp", "fsdp"), None),
        P(("dp", "fsdp"), None),
        P(("dp", "fsdp")),
        P(("dp", "fsdp"), None),
        P(("dp", "fsdp")),
        P(("dp", "fsdp"), None),
        P(("dp", "fsdp")),
    )
    out_specs = (
        P(None, ("dp", "fsdp"), None),
        P(None, ("dp", "fsdp"), None),
        P(("dp", "fsdp")),
        P(("dp", "fsdp"), None),
        P(("dp", "fsdp"), None),
        P(("dp", "fsdp")),
        P(("dp", "fsdp"), None),
        P(("dp", "fsdp")),
        P(("dp", "fsdp"), None),
        P(("dp", "fsdp")),
    )
    return jax.shard_map(functools.partial(body, dict(mesh.shape)), mesh=mesh, in_specs=in_specs, out_specs=out_specs, check_vma=False)
```

```python
import functools
import jax
import jax.numpy as jnp
from jax import lax
from jax.experimental import pallas as pl
from jax.experimental.pallas import tpu as pltpu
from jax.sharding import PartitionSpec as P

AXES = ("dp", "fsdp")
ROWS, WIDE, SKEW = 32, 512, 1


def bit_table(sizes):
    table = []
    for axis in AXES:
        stride = sizes[axis] // 2
        while stride:
            table.append((axis, stride))
            stride //= 2
    return table


def my_bits(table):
    where = {axis: lax.axis_index(axis) for axis in AXES}
    return [(where[axis] // stride) % 2 for axis, stride in table], where


def partner(table, bits, where, k):
    axis, stride = table[k]
    other = dict(where)
    other[axis] = where[axis] + stride * (1 - 2 * bits[k])
    return tuple(other[a] for a in AXES)


def greet(table, bits, where):
    barrier = pltpu.get_barrier_semaphore()
    for k in range(len(table)):
        pl.semaphore_signal(barrier, inc=1, device_id=partner(table, bits, where, k), device_id_type=pl.DeviceIdType.MESH)
    pl.semaphore_wait(barrier, len(table))


def orders(table):
    dp = [k for k, (axis, _) in enumerate(table) if axis == "dp"]
    rest = [k for k, (axis, _) in enumerate(table) if axis != "dp"]
    core, chips = dp[-1:], dp[:-1]
    return [core + chips + rest, core + chips[::-1] + rest]


def units_of(shapes):
    units = []
    for i, (rows, width) in enumerate(shapes):
        high, wide = min(rows, ROWS), min(width, WIDE)
        for r in range(0, rows, high):
            for c in range(0, width, 2 * wide):
                halves = [c] if c + wide >= width else [c, c + wide]
                units.append([(i, slice(r, r + high), slice(b, b + wide)) for b in halves])
    return units


def timetable(units, steps, skew):
    events, piece = [], 0
    for u, unit in enumerate(units):
        for h in range(len(unit)):
            events += [(u + skew * s, s, piece, h) for s in range(steps + 1)]
            piece += 1
    return [(p, s) for _, s, p, _ in sorted(events)]


EPS = 1e-06
BLOCK = 1024
TALL = 256
NT = (((1,), (1,)), ((), ()))
TN = (((0,), (0,)), ((), ()))
NN = (((1,), (0,)), ((), ()))
F32, BF16 = jnp.float32, jnp.bfloat16


def mul(a, b, dims=NN):
    return lax.dot_general(a, b, dims, preferred_element_type=F32)


def mlp_kernel(middle, cot, gain, up, up_b, down, down_b, out, grad_middle, grad_branch, up_g, down_g, up_b_g, gain_g, down_b_g,
               second, total, back, active, grad_hidden):
    step, last = pl.program_id(0), pl.num_programs(0) - 1
    rows, width = middle.shape
    part = 128

    @pl.when(step == 0)
    def _():
        @pl.loop(0, rows // part)
        def _(i):
            at = pl.ds(pl.multiple_of(i * part, part), part)
            x = middle[at, :]
            normal = x * lax.rsqrt(jnp.mean(x * x, axis=-1, keepdims=True) + EPS)
            second[at, :] = (normal * gain[...]).astype(BF16)

    bias = up_b[...]
    up_b_g[...] = jnp.zeros_like(up_b_g)

    @pl.loop(0, rows // TALL)
    def _(i):
        at = pl.ds(pl.multiple_of(i * TALL, TALL), TALL)
        hidden = mul(second[at, :], up[...]) + bias
        grad = mul(cot[at, :], down[...], NT)
        half = 0.5 + 0.5 * lax.erf(hidden * (0.5 ** 0.5))
        slope = half + hidden * (jnp.exp(hidden * hidden * -0.5) * 0.3989422804014327)
        active[at, :] = (hidden * half).astype(BF16)
        low = (grad * slope).astype(BF16)
        grad_hidden[at, :] = low
        up_b_g[...] += jnp.sum(low.astype(F32), axis=0, keepdims=True)

    @pl.loop(0, rows // TALL)
    def _(i):
        at = pl.ds(pl.multiple_of(i * TALL, TALL), TALL)
        more, less = mul(active[at, :], down[...]), mul(grad_hidden[at, :], up[...], NT)

        @pl.when(step == 0)
        def _():
            total[at, :] = more
            back[at, :] = less

        @pl.when(step > 0)
        def _():
            total[at, :] += more
            back[at, :] += less

    @pl.loop(0, BLOCK // TALL)
    def _(i):
        at = pl.ds(pl.multiple_of(i * TALL, TALL), TALL)
        down_g[at, :] = mul(active[:, at], cot[...], TN).astype(down_g.dtype)

    @pl.loop(0, width // TALL)
    def _(i):
        at = pl.ds(pl.multiple_of(i * TALL, TALL), TALL)
        up_g[at, :] = mul(second[:, at], grad_hidden[...], TN).astype(up_g.dtype)

    @pl.when(step == last)
    def _():
        gain_g[...] = jnp.zeros_like(gain_g)
        down_b_g[...] = jnp.zeros_like(down_b_g)

        @pl.loop(0, rows // part)
        def _(i):
            at = pl.ds(pl.multiple_of(i * part, part), part)
            x = middle[at, :]
            factor = lax.rsqrt(jnp.mean(x * x, axis=-1, keepdims=True) + EPS)
            normal = x * factor
            out[at, :] = (x + (total[at, :] + down_b[...])).astype(BF16)
            g = cot[at, :].astype(F32)
            grad = back[at, :]
            gain_g[...] += jnp.sum(grad * normal, axis=0, keepdims=True)
            down_b_g[...] += jnp.sum(g, axis=0, keepdims=True)
            n = grad * gain[...]
            result = g + factor * (n - normal * jnp.mean(n * normal, axis=-1, keepdims=True))
            grad_middle[at, :] = result
            grad_branch[at, :] = result.astype(BF16)


def mlp(middle, cot, gain, up, up_b, down, down_b, sum_type=BF16):
    rows, width = middle.shape
    ff = up.shape[1]
    whole = lambda *s: pl.BlockSpec(s, lambda j: (0,) * len(s), pipeline_mode=pl.Buffered(1))
    row = whole(1, width)
    return pl.pallas_call(
        mlp_kernel,
        grid=(ff // BLOCK,),
        in_specs=[whole(rows, width), whole(rows, width), row, pl.BlockSpec((width, BLOCK), lambda j: (0, j)),
                  pl.BlockSpec((1, BLOCK), lambda j: (0, j)), pl.BlockSpec((BLOCK, width), lambda j: (j, 0)), row],
        out_specs=[whole(rows, width), whole(rows, width), whole(rows, width), pl.BlockSpec((width, BLOCK), lambda j: (0, j)),
                   pl.BlockSpec((BLOCK, width), lambda j: (j, 0)), pl.BlockSpec((1, BLOCK), lambda j: (0, j)), row, row],
        out_shape=[jax.ShapeDtypeStruct(s, d) for s, d in (
            ((rows, width), BF16), ((rows, width), F32), ((rows, width), BF16), ((width, ff), sum_type), ((ff, width), sum_type),
            ((1, ff), F32), ((1, width), F32), ((1, width), F32))],
        scratch_shapes=[pltpu.VMEM((rows, width), BF16), pltpu.VMEM((rows, width), F32), pltpu.VMEM((rows, width), F32),
                        pltpu.VMEM((rows, BLOCK), BF16), pltpu.VMEM((rows, BLOCK), BF16)],
        compiler_params=pltpu.CompilerParams(vmem_limit_bytes=56 * 2 ** 20, dimension_semantics=("arbitrary",)),
        name="mlp",
    )(middle, cot, gain.reshape(1, -1).astype(F32), up, up_b.reshape(1, -1).astype(F32), down, down_b.reshape(1, -1).astype(F32))


PIECE = 128
REACH = 256


def spans(rows):
    return [(max(0, i * PIECE - REACH), i * PIECE, (i + 1) * PIECE) for i in range(rows // PIECE)]


def side_by_side(x, lanes):
    zero = jnp.zeros_like(x)
    return jnp.concatenate([jnp.where(lanes, x, zero), jnp.where(lanes, zero, x)], axis=0)


def fill_bias(bias, start, rows):
    at = 0
    for low, q, high in spans(rows):
        n = high - low
        key = low + lax.broadcasted_iota(jnp.int32, (n, PIECE), 0)
        query = q + lax.broadcasted_iota(jnp.int32, (n, PIECE), 1)
        seen = jnp.logical_and(key <= query, key >= start[:, q:high])
        b = jnp.where(seen, 0.0, -1e30)
        bias[at:at + n, :] = jnp.concatenate([b, b], axis=1)
        at += n


def attend_kernel(q_ref, k_ref, v_ref, start, out, logsum, bias):
    rows, wide = q_ref.shape

    @pl.when(pl.program_id(1) == 0)
    def _():
        fill_bias(bias, start[0], rows)

    lanes = lax.broadcasted_iota(jnp.int32, (PIECE, wide), 1) < wide // 2
    at = 0
    for i, (low, q, high) in enumerate(spans(rows)):
        n = high - low
        queries = side_by_side(q_ref[q:high, :] * 0.125, lanes)
        scores = mul(k_ref[low:high, :], queries, NT) + bias[at:at + n, :]
        peak = jnp.max(scores, axis=0, keepdims=True)
        expo = jnp.exp(scores - peak)
        total = jnp.sum(expo, axis=0, keepdims=True)
        logsum[0, 0, i:i + 1, :] = peak + jnp.log(total)
        attend = (expo * (1.0 / total)).astype(BF16)
        both = mul(attend, v_ref[low:high, :], TN)
        out[q:high, :] = jnp.where(lanes, both[:PIECE], both[PIECE:]).astype(BF16)
        at += n


def attend_specs(rows, pairs):
    block = lambda off: pl.BlockSpec((rows, 128), lambda b, h: (b, off * pairs + h))
    start = pl.BlockSpec((1, 1, rows), lambda b, h: (b, 0, 0))
    logsum = pl.BlockSpec((1, 1, rows // PIECE, 2 * PIECE), lambda b, h: (b, h, 0, 0))
    return block, start, logsum


def attend(project, start):
    batches, rows = start.shape[0], start.shape[2]
    width = project.shape[1] // 3
    pairs = width // 128
    block, start_spec, logsum = attend_specs(rows, pairs)
    return pl.pallas_call(
        attend_kernel,
        grid=(batches, pairs),
        in_specs=[block(0), block(1), block(2), start_spec],
        out_specs=[block(0), logsum],
        out_shape=[jax.ShapeDtypeStruct((batches * rows, width), BF16),
                   jax.ShapeDtypeStruct((batches, pairs, rows // PIECE, 2 * PIECE), F32)],
        scratch_shapes=[pltpu.VMEM((sum(h - l for l, _, h in spans(rows)), 2 * PIECE), F32)],
        compiler_params=pltpu.CompilerParams(vmem_limit_bytes=40 * 2 ** 20, dimension_semantics=("arbitrary", "arbitrary")),
        name="attend",
    )(project, project, project, start)


def attend_back_kernel(q_ref, k_ref, v_ref, g_ref, start, logsum, out, bias, k_sum, v_sum):
    rows, wide = q_ref.shape

    @pl.when(pl.program_id(1) == 0)
    def _():
        fill_bias(bias, start[0], rows)

    lanes = lax.broadcasted_iota(jnp.int32, (PIECE, wide), 1) < wide // 2
    at = 0
    k_sum[...] = jnp.zeros_like(k_sum)
    v_sum[...] = jnp.zeros_like(v_sum)
    for i, (low, q, high) in enumerate(spans(rows)):
        n = high - low
        queries = side_by_side(q_ref[q:high, :] * 0.125, lanes)
        grads = side_by_side(g_ref[q:high, :], lanes)
        keys, values = k_ref[low:high, :], v_ref[low:high, :]
        scores = mul(keys, queries, NT) + bias[at:at + n, :]
        full = jnp.exp(scores - logsum[0, 0, i:i + 1, :])
        grad = mul(values, grads, NT)
        v_sum[low:high, :] += mul(full.astype(BF16), grads)
        total = jnp.sum(full * grad, axis=0, keepdims=True)
        grad_scores = (full * (grad - total)).astype(BF16)
        k_sum[low:high, :] += mul(grad_scores, queries)
        both = mul(grad_scores, keys, TN) * 0.125
        out[0, q:high, :] = jnp.where(lanes, both[:PIECE], both[PIECE:]).astype(BF16)
        at += n
    out[1] = k_sum[...].astype(BF16)
    out[2] = v_sum[...].astype(BF16)


def attend_back(project, grad, start, logsum):
    batches, rows = start.shape[0], start.shape[2]
    width = project.shape[1] // 3
    pairs = width // 128
    block, start_spec, logsum_spec = attend_specs(rows, pairs)
    return pl.pallas_call(
        attend_back_kernel,
        grid=(batches, pairs),
        in_specs=[block(0), block(1), block(2), block(0), start_spec, logsum_spec],
        out_specs=pl.BlockSpec((3, rows, 128), lambda b, h: (0, b, h)),
        out_shape=jax.ShapeDtypeStruct((3, batches * rows, width), BF16),
        scratch_shapes=[pltpu.VMEM((sum(h - l for l, _, h in spans(rows)), 2 * PIECE), F32),
                        pltpu.VMEM((rows, 128), F32), pltpu.VMEM((rows, 128), F32)],
        compiler_params=pltpu.CompilerParams(vmem_limit_bytes=40 * 2 ** 20, dimension_semantics=("arbitrary", "arbitrary")),
        name="attend_back",
    )(project, project, project, grad, start, logsum)


class Gather:
    def __init__(self, table, bits, where, shards, fulls, local_sem, send_sem, recv_sem):
        self.table, self.bits, self.steps = table, bits, len(table)
        self.partners = [partner(table, bits, where, k) for k in range(len(table))]
        self.shards, self.fulls = shards, fulls
        self.local_sem, self.send_sem, self.recv_sem = local_sem, send_sem, recv_sem
        two = [o[::-1] for o in orders(table)]
        self.units = in_turn(units_of([s.shape for s in shards]), len(shards) - 2)
        self.chunks = [piece + (two[(h + u) % 2],) for u, unit in enumerate(self.units) for h, piece in enumerate(unit)]
        self.events = timetable(self.units, self.steps, SKEW)
        self.at = 0
        pieces = {i: [e for e in self.events if self.chunks[e[0]][0] == i and e[1] == 1] for i in range(len(shards))}
        self.first = {found[0] for found in pieces.values()}

    def own(self, i):
        return pltpu.make_async_copy(self.shards[i], self.fulls[i].at[tuple(self.bits)], self.local_sem.at[i])

    def copy(self, c, s):
        i, rows, cols, order = self.chunks[c]
        index = tuple(slice(None) if k in order[:s] else self.bits[k] for k in range(self.steps))
        there = self.fulls[i].at[index + (rows, cols)]
        return pltpu.make_async_remote_copy(
            src_ref=self.shards[i].at[rows, cols] if s == 0 else there, dst_ref=there,
            send_sem=self.send_sem.at[c, s], recv_sem=self.recv_sem.at[c, s],
            device_id=self.partners[order[s]], device_id_type=pl.DeviceIdType.MESH)

    def event(self, c, s):
        i = self.chunks[c][0]
        if s > 0:
            self.copy(c, s - 1).wait_recv()
            if (c, s) in self.first:
                self.own(i).wait()
        if s < self.steps:
            self.copy(c, s).start()

    def run(self, count):
        self.some(self.at, self.at + count)
        self.at = min(self.at + count, len(self.events))

    def some(self, low, high):
        for c, s in self.events[low:high]:
            self.event(c, s)

    def needed(self, array, unit):
        piece, last = 0, 0
        seen = -1
        for u in self.units:
            seen += u[0][0] == array
            if u[0][0] == array and seen <= unit:
                ends = [self.events.index((piece + h, self.steps)) for h in range(len(u))]
                last = max(last, max(ends) + 1)
            piece += len(u)
        return max(0, last - self.at)

    def until(self, array, unit):
        self.run(self.needed(array, unit))

    def finish(self):
        self.run(len(self.events))
        for c in range(len(self.chunks)):
            for s in range(self.steps):
                self.copy(c, s).wait_send()


def in_turn(units, first):
    one, two = [u for u in units if u[0][0] == first], [u for u in units if u[0][0] == first + 1]
    return [u for u in units if u[0][0] < first] + [u for pair in zip(one, two) for u in pair] + [u for u in units if u[0][0] > first + 1]


def regroup(src, dst, inward):
    width = src.shape[1]
    groups = 128 // ROWS
    part = lax.broadcasted_iota(jnp.int32, (src.shape[0], 128), 1) // ROWS
    tiles = width // 128 // groups
    for k in range(tiles):
        near = [slice((groups * k + m) * 128, (groups * k + m + 1) * 128) for m in range(groups)]
        far = [slice((m * tiles + k) * 128, (m * tiles + k + 1) * 128) for m in range(groups)]
        source, target = (near, far) if inward else (far, near)
        loaded = [src[:, c].astype(F32) for c in source]
        for a in range(groups):
            tile = loaded[a]
            for b in range(groups):
                turned = loaded[b] if a == b else pltpu.roll(loaded[b], (b - a) * ROWS % 128, 1)
                tile = jnp.where(part == b, turned, tile)
            dst[:, target[a]] = tile.astype(dst.dtype)


def spread(index, slots, engine, count):
    done = 0
    for slot in range(slots):
        upto = count * (slot + 1) // slots
        if upto > done:
            pl.when(index == slot)(functools.partial(engine.run, upto - done))
            done = upto


def row_of(table, offset, width, total):
    owners = table.shape[0]
    lane = lax.broadcasted_iota(jnp.int32, (128, total), 0)
    col = lax.broadcasted_iota(jnp.int32, (128, total), 1)
    pick = jnp.where(lane == offset + col % width, 1.0, 0.0).astype(BF16)
    owner = lax.broadcasted_iota(jnp.int32, (owners, total), 0)
    mine = owner == lax.broadcasted_iota(jnp.int32, (owners, total), 1) // width
    return jnp.sum(jnp.where(mine, mul(table, pick), 0.0), axis=0, keepdims=True)


def rows_at(i, size):
    return pl.ds(pl.multiple_of(i * size, size), size)


def norm_rows(x):
    factor = lax.rsqrt(jnp.mean(x * x, axis=-1, keepdims=True) + EPS)
    return x * factor, factor


def attend_pair(q_ref, k_ref, v_ref, bias, out, logsum):
    rows, wide = q_ref.shape
    lanes = lax.broadcasted_iota(jnp.int32, (PIECE, wide), 1) < wide // 2
    at = 0
    for i, (low, q, high) in enumerate(spans(rows)):
        n = high - low
        queries = side_by_side(q_ref[q:high, :] * 0.125, lanes)
        scores = mul(k_ref[low:high, :], queries, NT) + bias[at:at + n, :]
        peak = jnp.max(scores, axis=0, keepdims=True)
        expo = jnp.exp(scores - peak)
        total = jnp.sum(expo, axis=0, keepdims=True)
        logsum[i:i + 1, :] = peak + jnp.log(total)
        attend_low = (expo * (1.0 / total)).astype(BF16)
        both = mul(attend_low, v_ref[low:high, :], TN)
        out[q:high, :] = jnp.where(lanes, both[:PIECE], both[PIECE:]).astype(BF16)
        at += n


def forward_kernel(table, x_ref, cot_hbm, start, small_s, qkv_s, out_s, down_s, up_as_is,
                   small, qkv, out_w, down, up, project_o, attended_o, entered_o, output_o, middle_o, branch_o, up_g, down_g,
                   logsum, first_row, up_b_g, gain_g, down_b_g,
                   up_s, cot, entered, project, attended, middle, total, back, active, grad_hidden, up_v, down_v, up_gv, down_gv, small_v, rows_v, bias_v, bias,
                   local_sem, send_sem, recv_sem, sems):
    bits, where = my_bits(table)
    steps, owners = len(table), 2 ** len(table)
    rows, width = x_ref.shape
    ff = up_s.shape[1]
    regroup(up_as_is, up_s, True)
    length = start.shape[2]
    pairs = width // 128
    g = Gather(table, bits, where, [small_s, qkv_s, out_s, down_s, up_s], [small, qkv, out_w, down, up], local_sem, send_sem, recv_sem)
    SMALL, QKV, OUT, DOWN, UP = range(5)
    greet(table, bits, where)
    for i in range(5):
        g.own(i).start()

    def move(src, dst, k):
        return pltpu.make_async_copy(src, dst, sems.at[k])

    move(cot_hbm, cot, 0).start()
    g.until(SMALL, 0)
    move(small, small_v, 1).start()
    move(small, small_v, 1).wait()
    held = small_v[...].reshape(owners, small_s.shape[0], 128)
    first_row[...] = row_of(held[:, 1], 0, width // owners, width)
    rows_v[0:1, :] = row_of(held[:, 1], width // owners, width // owners, width)
    rows_v[1:2, :] = row_of(held[:, 1], 2 * (width // owners), width // owners, width)
    blocks = ff // BLOCK
    for j in range(blocks):
        bias_v[:, j * BLOCK:(j + 1) * BLOCK] = row_of(held[:, 0], j * ROWS, ROWS, BLOCK)
    part = 128

    @pl.loop(0, rows // part)
    def _(i):
        at = rows_at(i, part)
        normal, _ = norm_rows(x_ref[at, :].astype(F32))
        entered[at, :] = (normal * first_row[...]).astype(BF16)
    move(entered, entered_o, 2).start()

    for u in range(3):
        g.until(QKV, u)
        fetch = move(qkv.at[(slice(None),) * (steps + 1) + (slice(u * width, (u + 1) * width),)], up_v.at[u % 2], 3)
        fetch.start()
        fetch.wait()

        @pl.loop(0, rows // TALL)
        def _(i):
            at = rows_at(i, TALL)
            project[at, u * width:(u + 1) * width] = mul(entered[at, :], up_v[u % 2].reshape(width, width)).astype(BF16)
            spread_fixed(i, rows // TALL, g, 8)
        g.at += 8
    move(project, project_o, 4).start()
    loops = rows // length * pairs
    slot_events = max(0, g.needed(UP, 0) - 8)

    @pl.loop(0, loops)
    def _(i):
        b, h = i // pairs, i % pairs

        @pl.when(h == 0)
        def _():
            fill_bias(bias, start[b], length)
        at = rows_at(b, length)
        lanes = [pl.ds(pl.multiple_of(k * width + h * 128, 128), 128) for k in range(3)]
        q_ref, k_ref, v_ref = [project.at[at, lane] for lane in lanes]
        attend_pair(q_ref, k_ref, v_ref, bias, attended.at[at, lanes[0]], logsum.at[b, h])
        spread_fixed(i, loops, g, slot_events)
    g.at += slot_events
    move(attended, attended_o, 5).start()
    g.until(OUT, 0)
    fetch = move(out_w, up_v.at[1], 3)
    fetch.start()
    fetch.wait()
    move(entered, entered_o, 2).wait()
    second = entered

    @pl.loop(0, rows // TALL)
    def _(i):
        at = rows_at(i, TALL)
        x = x_ref[at, :].astype(F32) + mul(attended[at, :], up_v[1].reshape(width, width))
        middle[at, :] = x
        normal, _ = norm_rows(x)
        second[at, :] = (normal * rows_v[0:1, :]).astype(BF16)
        spread_fixed(i, rows // TALL, g, 8)
    g.at += 8
    g.until(UP, 0)
    move(cot_hbm, cot, 0).wait()

    def block(up_ref, down_ref, j):
        every = (slice(None),) * steps
        return up_ref.at[every + (slice(None), rows_at(j, BLOCK))], down_ref.at[every + (rows_at(j, ROWS),)]

    def fetches(j, slot):
        one, other = block(up, down, j)
        return [move(one, up_v.at[slot], 6 + slot), move(other, down_v.at[slot], 8 + slot)]

    def stores(j, slot):
        one, other = block(up_g, down_g, j)
        return [move(up_gv.at[slot], one, 10 + slot), move(down_gv.at[slot], other, 12 + slot)]

    deep = (BLOCK // TALL).bit_length() - 1

    def put(ref, slot, i, value):
        there = ref.at[(slot,) + tuple((i // 2 ** (deep - 1 - k)) % 2 for k in range(deep))]
        there[...] = value.reshape(there.shape).astype(BF16)

    for f in fetches(0, 0):
        f.start()
    per = rows // TALL
    marks = [g.at] + [g.at + g.needed(UP, j + 1) for j in range(blocks - 1)]

    def between(j, i, loop, loops):
        for k in range(blocks - 1):
            for n in range(per):
                cut = [marks[k] + (marks[k + 1] - marks[k]) * (loop * per + n + e) // (loops * per) for e in (0, 1)]
                if cut[1] > cut[0]:
                    pl.when(jnp.logical_and(j == k, i == n))(functools.partial(g.some, *cut))

    @pl.loop(0, blocks)
    def _(j):
        slot = j % 2
        for f in fetches(j, slot):
            f.wait()

        @pl.when(j >= 2)
        def _():
            for f in stores(j, slot):
                f.wait()
        lane = rows_at(j, BLOCK)
        bias_row = bias_v[:, lane]
        up_b_g[:, lane] = jnp.zeros((1, BLOCK), F32)

        @pl.loop(0, per)
        def _(i):
            at = rows_at(i, TALL)
            hidden = mul(second[at, :], up_v[slot].reshape(width, BLOCK)) + bias_row
            grad = mul(cot[at, :], down_v[slot].reshape(BLOCK, width), NT)
            half = 0.5 + 0.5 * lax.erf(hidden * (0.5 ** 0.5))
            slope = half + hidden * (jnp.exp(hidden * hidden * -0.5) * 0.3989422804014327)
            active[at, :] = (hidden * half).astype(BF16)
            low = (grad * slope).astype(BF16)
            grad_hidden[at, :] = low
            up_b_g[:, lane] += jnp.sum(low.astype(F32), axis=0, keepdims=True)
            between(j, i, 0, 3)

        @pl.loop(0, per)
        def _(i):
            at = rows_at(i, TALL)
            more, less = mul(active[at, :], down_v[slot].reshape(BLOCK, width)), mul(grad_hidden[at, :], up_v[slot].reshape(width, BLOCK), NT)

            @pl.when(j == 0)
            def _():
                total[at, :] = more
                back[at, :] = less

            @pl.when(j > 0)
            def _():
                total[at, :] += more
                back[at, :] += less
            between(j, i, 1, 3)

        @pl.loop(0, BLOCK // TALL)
        def _(i):
            at = rows_at(i, TALL)
            put(down_gv, slot, i, mul(active[:, at], cot[...], TN))
            between(j, i, 2, 3)

        @pl.when(j + 1 < blocks)
        def _():
            for f in fetches(j + 1, 1 - slot):
                f.start()

        @pl.loop(0, width // TALL)
        def _(i):
            at = rows_at(i, TALL)
            put(up_gv, slot, i, mul(second[:, at], grad_hidden[...], TN))
        for f in stores(j, slot):
            f.start()
    g.at = marks[-1]
    move(attended, attended_o, 5).wait()
    output, branch = entered, attended
    gain_g[...] = jnp.zeros_like(gain_g)
    down_b_g[...] = jnp.zeros_like(down_b_g)

    @pl.loop(0, rows // part)
    def _(i):
        at = rows_at(i, part)
        x = middle[at, :]
        normal, factor = norm_rows(x)
        output[at, :] = (x + (total[at, :] + rows_v[1:2, :])).astype(BF16)
        c = cot[at, :].astype(F32)
        grad = back[at, :]
        gain_g[...] += jnp.sum(grad * normal, axis=0, keepdims=True)
        down_b_g[...] += jnp.sum(c, axis=0, keepdims=True)
        n = grad * rows_v[0:1, :]
        result = c + factor * (n - normal * jnp.mean(n * normal, axis=-1, keepdims=True))
        back[at, :] = result
        branch[at, :] = result.astype(BF16)
    last = [move(output, output_o, 2), move(back, middle_o, 3), move(branch, branch_o, 5)]
    for f in last:
        f.start()
    for f in last + [move(project, project_o, 4)] + stores(blocks - 2, blocks % 2) + stores(blocks - 1, (blocks - 1) % 2):
        f.wait()
    g.finish()


def spread_fixed(index, slots, engine, count):
    begin = engine.at
    spread(index, slots, engine, count)
    engine.at = begin


def forward(frames, cot, start, packed, qkv, out, down, up, sizes, collective_id):
    table = bit_table(sizes)
    steps, owners = len(table), 2 ** len(table)
    rows, width = frames.shape
    ff = up.shape[1]
    batches, length = start.shape[0], start.shape[2]
    pairs = width // 128
    two = (2,) * steps
    shards = [packed, qkv, out, down, up]
    pieces = sum(len(u) for u in units_of([a.shape for a in shards]))
    anywhere, vmem = pl.BlockSpec(memory_space=pl.ANY), pl.BlockSpec(memory_space=pltpu.VMEM)
    hbm_out = [(two + a.shape, BF16) for a in shards] + [((rows, 3 * width), BF16), ((rows, width), BF16), ((rows, width), BF16),
               ((rows, width), BF16), ((rows, width), F32), ((rows, width), BF16), (two + (width // owners, ff), BF16), (two + (ff // owners, width), BF16)]
    vmem_out = [((batches, pairs, length // PIECE, 2 * PIECE), F32), ((1, width), F32), ((1, ff), F32), ((1, width), F32), ((1, width), F32)]
    V = pltpu.VMEM
    return pl.pallas_call(
        functools.partial(forward_kernel, table),
        out_shape=[jax.ShapeDtypeStruct(s, d) for s, d in hbm_out + vmem_out],
        in_specs=[vmem, anywhere] + [vmem] * 6,
        out_specs=[anywhere] * len(hbm_out) + [vmem] * len(vmem_out),
        scratch_shapes=[V(up.shape, BF16), V((rows, width), BF16), V((rows, width), BF16), V((rows, 3 * width), BF16), V((rows, width), BF16), V((rows, width), F32),
                        V((rows, width), F32), V((rows, width), F32), V((rows, BLOCK), BF16), V((rows, BLOCK), BF16),
                        V((2,) + two + (width // owners, BLOCK), BF16), V((2,) + two + (ROWS, width), BF16),
                        V((2,) + two + (width // owners, BLOCK), BF16), V((2,) + two + (ROWS, width), BF16), V(two + packed.shape, BF16), V((2, width), F32), V((1, ff), F32),
                        V((sum(h - l for l, _, h in spans(length)), 2 * PIECE), F32),
                        pltpu.SemaphoreType.DMA((5,)), pltpu.SemaphoreType.DMA((pieces, steps)), pltpu.SemaphoreType.DMA((pieces, steps)),
                        pltpu.SemaphoreType.DMA((14,))],
        compiler_params=pltpu.CompilerParams(collective_id=collective_id, has_side_effects=True, vmem_limit_bytes=58 * 2 ** 20),
        name="forward",
    )(frames, cot, start, *shards)


class Scatter:
    def __init__(self, table, bits, where, parts, outs, recv, stage, small, local_sem, send_sem, recv_sem):
        self.table, self.bits, self.steps = table, bits, len(table)
        self.partners = [partner(table, bits, where, k) for k in range(len(table))]
        self.parts, self.outs, self.recv, self.stage = parts, outs, recv, stage
        self.local_sem, self.send_sem, self.recv_sem = local_sem, send_sem, recv_sem
        self.small_recv = small
        self.units, self.chunks = scatter_chunks(table, [p.shape[-2:] for p in parts])
        self.events = timetable(self.units, self.steps, SKEW)
        self.at = 0

    def into(self, c, s):
        if self.chunks[c][0] == len(self.parts) - 1:
            return self.small_recv[s]
        return self.recv[s].at[c]

    def half(self, c, bit):
        i, rows, cols, order = self.chunks[c]
        index = tuple(bit if k == order[0] else slice(None) for k in range(self.steps))
        return self.parts[i].at[index + (rows, cols)]

    def load(self, c):
        return pltpu.make_async_copy(self.half(c, self.bits[self.chunks[c][3][0]]), self.stage.at[c % 4], self.local_sem.at[c % 4])

    def left(self, c, s, last):
        order, out = self.chunks[c][3], []
        for k in range(self.steps):
            if k == order[0]:
                continue
            if k in order[1:s]:
                out.append(self.bits[k])
            elif s < self.steps and k == order[s] and last is not None:
                out.append(last)
            else:
                out.append(slice(None))
        return tuple(out)

    def copy(self, c, s):
        k = self.chunks[c][3][s]
        other = 1 - self.bits[k]
        return pltpu.make_async_remote_copy(
            src_ref=self.half(c, other) if s == 0 else self.into(c, 0).at[self.left(c, s, other)], dst_ref=self.into(c, s),
            send_sem=self.send_sem.at[c, s], recv_sem=self.recv_sem.at[c, s],
            device_id=self.partners[k], device_id_type=pl.DeviceIdType.MESH)

    def add(self, c, s):
        i, rows, cols, order = self.chunks[c]
        small = i == len(self.parts) - 1
        total, got = self.into(c, 0), self.into(c, s)
        free = self.steps - s - 1
        if free == 0:
            own = total[self.left(c, self.steps, None)]
            self.outs[i][rows, cols] = own.astype(F32) + got[...].astype(F32)
            return
        base = self.left(c, s, self.bits[order[s]]) if s else (slice(None),) * free
        mine = self.half(c, self.bits[order[0]]) if small else self.stage.at[c % 4]

        @pl.loop(0, 2 ** free)
        def _(j):
            spot = [(j // 2 ** (free - 1 - b)) % 2 for b in range(free)]
            rest = iter(spot)
            here = tuple(next(rest) if isinstance(e, slice) else e for e in base)
            more = mine[tuple(spot)] if s == 0 else got[tuple(spot)]
            total[here] = (total[here].astype(F32) + more.astype(F32)).astype(total.dtype)

    def event(self, c, s):
        small = self.chunks[c][0] == len(self.parts) - 1
        if s == 0:
            self.copy(c, 0).start()
            if not small:
                self.load(c).start()
            return
        self.copy(c, s - 1).wait_recv()
        if s == 1 and not small:
            self.load(c).wait()
        self.add(c, s - 1)
        if s < self.steps:
            self.copy(c, s).start()

    def run(self, count):
        for c, s in self.events[self.at:self.at + count]:
            self.event(c, s)
        self.at = min(self.at + count, len(self.events))

    def before(self, part):
        return next(n for n, (c, s) in enumerate(self.events) if self.chunks[c][0] == part)

    def finish(self):
        self.run(len(self.events))
        for c in range(len(self.chunks)):
            for s in range(self.steps):
                self.copy(c, s).wait_send()


def scatter_chunks(table, tails):
    two = orders(table)
    units = in_turn(units_of(tails), 0)
    return units, [piece + (two[(h + u) % 2],) for u, unit in enumerate(units) for h, piece in enumerate(unit)]


def attend_back_pair(q_ref, k_ref, v_ref, g_ref, bias, logsum, k_sum, v_sum):
    rows, wide = q_ref.shape
    lanes = lax.broadcasted_iota(jnp.int32, (PIECE, wide), 1) < wide // 2
    at = 0
    k_sum[...] = jnp.zeros_like(k_sum)
    v_sum[...] = jnp.zeros_like(v_sum)
    for i, (low, q, high) in enumerate(spans(rows)):
        n = high - low
        queries = side_by_side(q_ref[q:high, :] * 0.125, lanes)
        grads = side_by_side(g_ref[q:high, :], lanes)
        keys, values = k_ref[low:high, :], v_ref[low:high, :]
        scores = mul(keys, queries, NT) + bias[at:at + n, :]
        full = jnp.exp(scores - logsum[i:i + 1, :])
        grad = mul(values, grads, NT)
        v_sum[low:high, :] += mul(full.astype(BF16), grads)
        total = jnp.sum(full * grad, axis=0, keepdims=True)
        grad_scores = (full * (grad - total)).astype(BF16)
        k_sum[low:high, :] += mul(grad_scores, queries)
        both = mul(grad_scores, keys, TN) * 0.125
        q_ref[q:high, :] = jnp.where(lanes, both[:PIECE], both[PIECE:]).astype(BF16)
        at += n
    k_ref[...] = k_sum[...].astype(BF16)
    v_ref[...] = v_sum[...].astype(BF16)


def by_owner(row, offset, owners):
    total = row.shape[1]
    width = total // owners
    lane = lax.broadcasted_iota(jnp.int32, (128, total), 0)
    col = lax.broadcasted_iota(jnp.int32, (128, total), 1)
    pick = jnp.where(lane == offset + col % width, 1.0, 0.0)
    owner = lax.broadcasted_iota(jnp.int32, (owners, total), 0)
    mine = owner == lax.broadcasted_iota(jnp.int32, (owners, total), 1) // width
    return lax.dot_general(jnp.where(mine, row, 0.0), pick, NT, precision=lax.Precision.HIGHEST, preferred_element_type=F32)


def backward_kernel(table, x_hbm, start, project_hbm, attended_hbm, entered_hbm, middle_hbm, branch_hbm, qkv, out_w, up_g, down_g,
                    logsum, first_row, up_b_g, gain_g, down_b_g,
                    grad_o, out_g, q_g, k_g, v_g, up_o, down_r, out_r, q_r, k_r, v_r, small_r,
                    project, attended, branch, entered, weight, held, back, old, bias, k_sum, v_sum, small, stage,
                    up_r, r0, r1, r2, r3, r4, s0, s1, s2, s3, s4, local_sem, send_sem, recv_sem, sems):
    bits, where = my_bits(table)
    steps, owners = len(table), 2 ** len(table)
    rows, width = attended.shape
    length = start.shape[2]
    pairs = width // 128
    e = Scatter(table, bits, where, [up_g, down_g, out_g, q_g, k_g, v_g, small], [up_r, down_r, out_r, q_r, k_r, v_r, small_r],
                [r0, r1, r2, r3, r4], stage, [s0, s1, s2, s3, s4], local_sem, send_sem, recv_sem)

    def move(src, dst, k):
        return pltpu.make_async_copy(src, dst, sems.at[k])

    for args in ((attended_hbm, attended, 0), (branch_hbm, branch, 1), (out_w, weight.at[0], 2), (project_hbm, project, 3), (entered_hbm, entered, 4)):
        move(*args).start()
    greet(table, bits, where)
    first_q = e.before(3)
    e.run(2)
    move(attended_hbm, attended, 0).wait()
    move(branch_hbm, branch, 1).wait()
    per = rows // TALL
    deep = (width // TALL).bit_length() - 1

    def place(slot, i):
        return held.at[(slot,) + tuple((i // 2 ** (deep - 1 - k)) % 2 for k in range(deep))]

    def put(slot, i, value):
        ref = place(slot, i)
        ref[...] = value.reshape(ref.shape).astype(BF16)

    @pl.loop(0, width // TALL)
    def _(i):
        put(0, i, mul(attended[:, rows_at(i, TALL)], branch[...], TN))
        spread_fixed(i, width // TALL, e, 4)
    e.at += 4
    move(held.at[0], out_g, 5).start()
    move(out_w, weight.at[0], 2).wait()

    @pl.loop(0, per)
    def _(i):
        at = rows_at(i, TALL)
        branch[at, :] = mul(branch[at, :], weight[0].reshape(width, width), NT).astype(BF16)
        spread_fixed(i, per, e, 4)
    e.at += 4
    move(x_hbm, attended, 0).start()
    move(project_hbm, project, 3).wait()
    move(held.at[0], out_g, 5).wait()
    loops = rows // length * pairs
    count = first_q - e.at - 12

    @pl.loop(0, loops)
    def _(i):
        b, h = i // pairs, i % pairs

        @pl.when(h == 0)
        def _():
            fill_bias(bias, start[b], length)
        at = rows_at(b, length)
        lanes = [pl.ds(pl.multiple_of(k * width + h * 128, 128), 128) for k in range(3)]
        q_ref, k_ref, v_ref = [project.at[at, lane] for lane in lanes]
        attend_back_pair(q_ref, k_ref, v_ref, branch.at[at, lanes[0]], bias, logsum.at[b, h], k_sum, v_sum)
        spread_fixed(i, loops, e, count)
    e.at += count
    move(entered_hbm, entered, 4).wait()

    def fetch(u):
        return move(qkv.at[(slice(None),) * (steps + 1) + (slice(u * width, (u + 1) * width),)], weight.at[(u + 1) % 2], 6 + u % 2)

    fetch(0).start()
    fetch(1).start()
    for u, part in enumerate((q_g, k_g, v_g)):
        slot = (u + 1) % 2
        if u == 2:
            move(held.at[slot], q_g, 8).wait()

        @pl.loop(0, width // TALL)
        def _(i):
            put(slot, i, mul(entered[:, rows_at(i, TALL)], project[:, u * width:(u + 1) * width], TN))
            spread_fixed(i, width // TALL, e, 4)
        e.at += 4
        move(held.at[slot], part, 8 + u).start()
    for u, part in enumerate((q_g, k_g, v_g)):
        if u:
            move(held.at[(u + 1) % 2], part, 8 + u).wait()
    mark = e.before(6)
    each = (mark - e.at) // 3
    for u in range(3):
        fetch(u).wait()

        @pl.loop(0, per)
        def _(i):
            at = rows_at(i, TALL)
            more = mul(project[at, u * width:(u + 1) * width], weight[(u + 1) % 2].reshape(width, width), NT)
            if u == 0:
                back[at, :] = more
            else:
                back[at, :] += more
            spread_fixed(i, per, e, each)
        e.at += each
        if u == 0:
            fetch(2).start()
    move(x_hbm, attended, 0).wait()
    part = old.shape[1]
    first_g = jnp.zeros((1, width), F32)

    def older(i):
        return move(middle_hbm.at[rows_at(i, part), :], old.at[i % 2], 11 + i % 2)

    older(0).start()

    @pl.loop(0, rows // part, init_carry=first_g)
    def first_g(i, first_g):
        @pl.when(i + 1 < rows // part)
        def _():
            older(i + 1).start()
        older(i).wait()
        at = rows_at(i, part)
        normal, factor = norm_rows(attended[at, :].astype(F32))
        grad = back[at, :]
        n = grad * first_row[...]
        back[at, :] = old[i % 2] + factor * (n - normal * jnp.mean(n * normal, axis=-1, keepdims=True))
        return first_g + jnp.sum(grad * normal, axis=0, keepdims=True)
    move(back, grad_o, 13).start()
    share = width // owners
    zero = jnp.zeros((owners, 6, 128), F32)
    vectors = by_owner(first_g, 0, owners) + by_owner(gain_g[...], share, owners) + by_owner(down_b_g[...], 2 * share, owners)
    long = sum(by_owner(up_b_g[:, j * BLOCK:(j + 1) * BLOCK], j * ROWS, owners) for j in range(up_b_g.shape[1] // BLOCK))
    packed = jnp.concatenate([long[:, None], vectors[:, None], zero], axis=1)
    small[...] = packed.reshape(small.shape)
    e.finish()
    regroup(up_r, up_o, False)
    move(back, grad_o, 13).wait()


def backward(frames, start, project, attended, entered, middle, branch, qkv, out_w, up_g, down_g, logsum, first_row, up_b_g, gain_g, down_b_g,
             sizes, collective_id):
    table = bit_table(sizes)
    steps, owners = len(table), 2 ** len(table)
    rows, width = frames.shape
    length = start.shape[2]
    two = (2,) * steps
    share = width // owners
    small = (8, 128)
    tails = [up_g.shape[-2:], down_g.shape[-2:]] + [(share, width)] * 4 + [small]
    units, chunks = scatter_chunks(table, tails)
    m = len(chunks)
    piece = (min(ROWS, share), WIDE)
    anywhere, vmem = pl.BlockSpec(memory_space=pl.ANY), pl.BlockSpec(memory_space=pltpu.VMEM)
    V = pltpu.VMEM
    out_shape = [((rows, width), F32)] + [(two + (share, width), BF16)] * 4 + [(t, F32) for t in tails]
    return pl.pallas_call(
        functools.partial(backward_kernel, table),
        out_shape=[jax.ShapeDtypeStruct(s, d) for s, d in out_shape],
        in_specs=[anywhere, vmem] + [anywhere] * 9 + [vmem] * 5,
        out_specs=[anywhere] * 5 + [vmem] * 7,
        scratch_shapes=[V((rows, 3 * width), BF16), V((rows, width), BF16), V((rows, width), BF16), V((rows, width), BF16),
                        V((2,) + two + (share, width), BF16), V((2,) + two + (share, width), BF16), V((rows, width), F32), V((2, 128, width), F32),
                        V((sum(h - l for l, _, h in spans(length)), 2 * PIECE), F32), V((length, 128), F32), V((length, 128), F32),
                        V(two + small, F32), V((4,) + two[1:] + piece, BF16)]
        + [V(tails[0], F32)] + [V((m - 1,) + two[s + 1:] + piece, BF16) for s in range(steps)] + [V(two[s + 1:] + small, F32) for s in range(steps)]
        + [pltpu.SemaphoreType.DMA((4,)), pltpu.SemaphoreType.DMA((m, steps)), pltpu.SemaphoreType.DMA((m, steps)), pltpu.SemaphoreType.DMA((14,))],
        compiler_params=pltpu.CompilerParams(collective_id=collective_id, has_side_effects=True, vmem_limit_bytes=60 * 2 ** 20),
        name="backward",
    )(frames, start, project, attended, entered, middle, branch, qkv, out_w, up_g, down_g, logsum, first_row, up_b_g, gain_g, down_b_g)


def pack(first, second, up_b, down_b):
    rest = jnp.concatenate([first, second, down_b])
    rest = jnp.pad(rest, (0, 128 - rest.shape[0]))
    return jnp.pad(jnp.stack([jnp.pad(up_b, (0, 128 - up_b.shape[0])), rest]), ((0, 14), (0, 0)))


def fits(sizes, shards):
    return all(s & (s - 1) == 0 for s in sizes.values()) and all(a.shape[0] % ROWS == 0 for a in shards) and sizes["dp"] * sizes["fsdp"] * ROWS == BLOCK


def item_starts(lengths, rows):
    slots = jnp.arange(lengths.shape[1], dtype=jnp.int32)
    ends = jnp.sum(jnp.where(slots[None, :, None] <= slots[None, None, :], lengths[:, :, None], 0), axis=1)
    position = jnp.arange(rows, dtype=jnp.int32)[None, None, :]
    return jnp.max(jnp.where(ends[:, :, None] <= position, ends[:, :, None], 0), axis=1, keepdims=True)


def normalize(x_val):
    factor = lax.rsqrt(jnp.mean(x_val * x_val, axis=-1, keepdims=True) + EPS)
    return (x_val * factor, factor)


def norm_back(normal, factor, gain, grad_out):
    gain_grad = jnp.sum(grad_out * normal, axis=0)
    scaled = grad_out * gain
    inner = jnp.mean(scaled * normal, axis=-1, keepdims=True)
    return (factor * (scaled - normal * inner), gain_grad)


def block_pass(frames, lengths, cotangent, params, sum_type):
    first, qkv, out, second, up, up_b, down, down_b = params
    batches, rows, width = frames.shape
    x_val = frames.reshape(batches * rows, width).astype(F32)
    cot = cotangent.reshape(batches * rows, width)
    start = item_starts(lengths, rows)
    normal, factor = normalize(x_val)
    gain = first.astype(F32)
    entered = (normal * gain).astype(BF16)
    project = mul(entered, qkv).astype(BF16)
    attended, logsum = attend(project, start)
    middle = x_val + mul(attended, out)
    output, grad_middle, grad_branch, up_g, down_g, up_b_g, second_g, down_b_g = mlp(middle, cot, second, up, up_b, down, down_b, sum_type)
    out_g = mul(attended, grad_branch, TN)
    grad_attended = mul(grad_branch, out, NT).astype(BF16)
    grads = attend_back(project, grad_attended, start, logsum)
    qkv_g = [mul(entered, grads[j], TN) for j in range(3)]
    grad_entered = sum(mul(grads[j], qkv[:, j * width:(j + 1) * width], NT) for j in range(3))
    back, first_g = norm_back(normal, factor, gain, grad_entered)
    shape = frames.shape
    return (output.reshape(shape), (grad_middle + back).reshape(shape), (down_g, up_g, out_g, *qkv_g),
            (first_g, second_g.reshape(-1), up_b_g.reshape(-1), down_b_g.reshape(-1)))


def body(sizes, frames, lengths, cotangent, *shards):
    weights = [shards[i] for i in (1, 2, 4, 6)]
    vectors = [shards[i] for i in (0, 3, 5, 7)]
    shape = frames.shape
    if fits(sizes, weights):
        qkv_s, out_s, up_s, down_s = weights
        flat = (shape[0] * shape[1], shape[2])
        x_val, cot = frames.reshape(flat), cotangent.reshape(flat)
        start = item_starts(lengths[:, 0], shape[1])
        (_, qkv, out, _, _, project, attended, entered, output, middle, branch, up_g, down_g, logsum, first, up_b_g, second_g, down_b_g) = forward(
            x_val, cot, start, pack(*vectors), qkv_s, out_s, down_s, up_s, sizes, 1)
        frames_grad, _, _, _, _, up_g, down_g, out_g, q_g, k_g, v_g, small = backward(
            x_val, start, project, attended, entered, middle, branch, qkv, out, up_g, down_g, logsum, first, up_b_g, second_g, down_b_g, sizes, 2)
        output, frames_grad = output.reshape(shape), frames_grad.reshape(shape)
        share = vectors[0].shape[0]
        first_g, second_g, down_b_g = [small[1, k * share:(k + 1) * share] for k in range(3)]
        up_b_g, qkv_g = small[0, :vectors[2].shape[0]], [q_g, k_g, v_g]
    else:
        qkv, out, up, down = [lax.all_gather(w, AXES, axis=0, tiled=True) for w in weights]
        first, second, up_b, down_b = [lax.all_gather(v, AXES, axis=0, tiled=True) for v in vectors]
        params = (first, qkv, out, second, up, up_b, down, down_b)
        output, frames_grad, big, small = block_pass(frames, lengths[:, 0], cotangent, params, F32)
        down_g, up_g, out_g, *qkv_g = [lax.psum_scatter(g, AXES, scatter_dimension=0, tiled=True) for g in big]
        first_g, second_g, up_b_g, down_b_g = [lax.psum_scatter(g, AXES, scatter_dimension=0, tiled=True) for g in small]
    return (output, frames_grad, first_g, jnp.concatenate(qkv_g, axis=1), out_g, second_g, up_g, up_b_g, down_g, down_b_g)


def solution(mesh):
    in_specs = (
        P(None, ("dp", "fsdp"), None),
        P(None, ("dp", "fsdp"), None),
        P(None, ("dp", "fsdp"), None),
        P(("dp", "fsdp")),
        P(("dp", "fsdp"), None),
        P(("dp", "fsdp"), None),
        P(("dp", "fsdp")),
        P(("dp", "fsdp"), None),
        P(("dp", "fsdp")),
        P(("dp", "fsdp"), None),
        P(("dp", "fsdp")),
    )
    out_specs = (
        P(None, ("dp", "fsdp"), None),
        P(None, ("dp", "fsdp"), None),
        P(("dp", "fsdp")),
        P(("dp", "fsdp"), None),
        P(("dp", "fsdp"), None),
        P(("dp", "fsdp")),
        P(("dp", "fsdp"), None),
        P(("dp", "fsdp")),
        P(("dp", "fsdp"), None),
        P(("dp", "fsdp")),
    )
    return jax.shard_map(functools.partial(body, dict(mesh.shape)), mesh=mesh, in_specs=in_specs, out_specs=out_specs, check_vma=False)
```

```python
import functools
import jax
import jax.numpy as jnp
from jax import lax
from jax.experimental import pallas as pl
from jax.experimental.pallas import tpu as pltpu
from jax.sharding import PartitionSpec as P

AXES = ("dp", "fsdp")
ROWS, WIDE, SKEW = 32, 512, 1


def bit_table(sizes):
    table = []
    for axis in AXES:
        stride = sizes[axis] // 2
        while stride:
            table.append((axis, stride))
            stride //= 2
    return table


def my_bits(table):
    where = {axis: lax.axis_index(axis) for axis in AXES}
    return [(where[axis] // stride) % 2 for axis, stride in table], where


def partner(table, bits, where, k):
    axis, stride = table[k]
    other = dict(where)
    other[axis] = where[axis] + stride * (1 - 2 * bits[k])
    return tuple(other[a] for a in AXES)


def greet(table, bits, where):
    barrier = pltpu.get_barrier_semaphore()
    for k in range(len(table)):
        pl.semaphore_signal(barrier, inc=1, device_id=partner(table, bits, where, k), device_id_type=pl.DeviceIdType.MESH)
    pl.semaphore_wait(barrier, len(table))


def orders(table):
    dp = [k for k, (axis, _) in enumerate(table) if axis == "dp"]
    rest = [k for k, (axis, _) in enumerate(table) if axis != "dp"]
    core, chips = dp[-1:], dp[:-1]
    return [core + chips + rest, core + chips[::-1] + rest]


def units_of(shapes):
    units = []
    for i, (rows, width) in enumerate(shapes):
        high, wide = min(rows, ROWS), min(width, WIDE)
        for r in range(0, rows, high):
            for c in range(0, width, 2 * wide):
                halves = [c] if c + wide >= width else [c, c + wide]
                units.append([(i, slice(r, r + high), slice(b, b + wide)) for b in halves])
    return units


def timetable(units, steps, skew):
    events, piece = [], 0
    for u, unit in enumerate(units):
        for h in range(len(unit)):
            events += [(u + skew * s, s, piece, h) for s in range(steps + 1)]
            piece += 1
    return [(p, s) for _, s, p, _ in sorted(events)]


EPS = 1e-06
BLOCK = 1024
TALL = 256
NT = (((1,), (1,)), ((), ()))
TN = (((0,), (0,)), ((), ()))
NN = (((1,), (0,)), ((), ()))
F32, BF16 = jnp.float32, jnp.bfloat16


def mul(a, b, dims=NN):
    return lax.dot_general(a, b, dims, preferred_element_type=F32)


def mlp_kernel(middle, cot, gain, up, up_b, down, down_b, out, grad_middle, grad_branch, up_g, down_g, up_b_g, gain_g, down_b_g,
               second, total, back, active, grad_hidden):
    step, last = pl.program_id(0), pl.num_programs(0) - 1
    rows, width = middle.shape
    part = 128

    @pl.when(step == 0)
    def _():
        @pl.loop(0, rows // part)
        def _(i):
            at = pl.ds(pl.multiple_of(i * part, part), part)
            x = middle[at, :]
            normal = x * lax.rsqrt(jnp.mean(x * x, axis=-1, keepdims=True) + EPS)
            second[at, :] = (normal * gain[...]).astype(BF16)

    bias = up_b[...]
    up_b_g[...] = jnp.zeros_like(up_b_g)

    @pl.loop(0, rows // TALL)
    def _(i):
        at = pl.ds(pl.multiple_of(i * TALL, TALL), TALL)
        hidden = mul(second[at, :], up[...]) + bias
        grad = mul(cot[at, :], down[...], NT)
        half = 0.5 + 0.5 * lax.erf(hidden * (0.5 ** 0.5))
        slope = half + hidden * (jnp.exp(hidden * hidden * -0.5) * 0.3989422804014327)
        active[at, :] = (hidden * half).astype(BF16)
        low = (grad * slope).astype(BF16)
        grad_hidden[at, :] = low
        up_b_g[...] += jnp.sum(low.astype(F32), axis=0, keepdims=True)

    @pl.loop(0, rows // TALL)
    def _(i):
        at = pl.ds(pl.multiple_of(i * TALL, TALL), TALL)
        more, less = mul(active[at, :], down[...]), mul(grad_hidden[at, :], up[...], NT)

        @pl.when(step == 0)
        def _():
            total[at, :] = more
            back[at, :] = less

        @pl.when(step > 0)
        def _():
            total[at, :] += more
            back[at, :] += less

    @pl.loop(0, BLOCK // TALL)
    def _(i):
        at = pl.ds(pl.multiple_of(i * TALL, TALL), TALL)
        down_g[at, :] = mul(active[:, at], cot[...], TN).astype(down_g.dtype)

    @pl.loop(0, width // TALL)
    def _(i):
        at = pl.ds(pl.multiple_of(i * TALL, TALL), TALL)
        up_g[at, :] = mul(second[:, at], grad_hidden[...], TN).astype(up_g.dtype)

    @pl.when(step == last)
    def _():
        gain_g[...] = jnp.zeros_like(gain_g)
        down_b_g[...] = jnp.zeros_like(down_b_g)

        @pl.loop(0, rows // part)
        def _(i):
            at = pl.ds(pl.multiple_of(i * part, part), part)
            x = middle[at, :]
            factor = lax.rsqrt(jnp.mean(x * x, axis=-1, keepdims=True) + EPS)
            normal = x * factor
            out[at, :] = (x + (total[at, :] + down_b[...])).astype(BF16)
            g = cot[at, :].astype(F32)
            grad = back[at, :]
            gain_g[...] += jnp.sum(grad * normal, axis=0, keepdims=True)
            down_b_g[...] += jnp.sum(g, axis=0, keepdims=True)
            n = grad * gain[...]
            result = g + factor * (n - normal * jnp.mean(n * normal, axis=-1, keepdims=True))
            grad_middle[at, :] = result
            grad_branch[at, :] = result.astype(BF16)


def mlp(middle, cot, gain, up, up_b, down, down_b, sum_type=BF16):
    rows, width = middle.shape
    ff = up.shape[1]
    whole = lambda *s: pl.BlockSpec(s, lambda j: (0,) * len(s), pipeline_mode=pl.Buffered(1))
    row = whole(1, width)
    return pl.pallas_call(
        mlp_kernel,
        grid=(ff // BLOCK,),
        in_specs=[whole(rows, width), whole(rows, width), row, pl.BlockSpec((width, BLOCK), lambda j: (0, j)),
                  pl.BlockSpec((1, BLOCK), lambda j: (0, j)), pl.BlockSpec((BLOCK, width), lambda j: (j, 0)), row],
        out_specs=[whole(rows, width), whole(rows, width), whole(rows, width), pl.BlockSpec((width, BLOCK), lambda j: (0, j)),
                   pl.BlockSpec((BLOCK, width), lambda j: (j, 0)), pl.BlockSpec((1, BLOCK), lambda j: (0, j)), row, row],
        out_shape=[jax.ShapeDtypeStruct(s, d) for s, d in (
            ((rows, width), BF16), ((rows, width), F32), ((rows, width), BF16), ((width, ff), sum_type), ((ff, width), sum_type),
            ((1, ff), F32), ((1, width), F32), ((1, width), F32))],
        scratch_shapes=[pltpu.VMEM((rows, width), BF16), pltpu.VMEM((rows, width), F32), pltpu.VMEM((rows, width), F32),
                        pltpu.VMEM((rows, BLOCK), BF16), pltpu.VMEM((rows, BLOCK), BF16)],
        compiler_params=pltpu.CompilerParams(vmem_limit_bytes=56 * 2 ** 20, dimension_semantics=("arbitrary",)),
        name="mlp",
    )(middle, cot, gain.reshape(1, -1).astype(F32), up, up_b.reshape(1, -1).astype(F32), down, down_b.reshape(1, -1).astype(F32))


PIECE = 128
REACH = 256


def spans(rows):
    return [(max(0, i * PIECE - REACH), i * PIECE, (i + 1) * PIECE) for i in range(rows // PIECE)]


def side_by_side(x, lanes):
    zero = jnp.zeros_like(x)
    return jnp.concatenate([jnp.where(lanes, x, zero), jnp.where(lanes, zero, x)], axis=0)


def fill_bias(bias, start, rows):
    at = 0
    for low, q, high in spans(rows):
        n = high - low
        key = low + lax.broadcasted_iota(jnp.int32, (n, PIECE), 0)
        query = q + lax.broadcasted_iota(jnp.int32, (n, PIECE), 1)
        seen = jnp.logical_and(key <= query, key >= start[:, q:high])
        b = jnp.where(seen, 0.0, -1e30)
        bias[at:at + n, :] = jnp.concatenate([b, b], axis=1)
        at += n


def attend_kernel(q_ref, k_ref, v_ref, start, out, logsum, bias):
    rows, wide = q_ref.shape

    @pl.when(pl.program_id(1) == 0)
    def _():
        fill_bias(bias, start[0], rows)

    lanes = lax.broadcasted_iota(jnp.int32, (PIECE, wide), 1) < wide // 2
    at = 0
    for i, (low, q, high) in enumerate(spans(rows)):
        n = high - low
        queries = side_by_side(q_ref[q:high, :] * 0.125, lanes)
        scores = mul(k_ref[low:high, :], queries, NT) + bias[at:at + n, :]
        peak = jnp.max(scores, axis=0, keepdims=True)
        expo = jnp.exp(scores - peak)
        total = jnp.sum(expo, axis=0, keepdims=True)
        logsum[0, 0, i:i + 1, :] = peak + jnp.log(total)
        attend = (expo * (1.0 / total)).astype(BF16)
        both = mul(attend, v_ref[low:high, :], TN)
        out[q:high, :] = jnp.where(lanes, both[:PIECE], both[PIECE:]).astype(BF16)
        at += n


def attend_specs(rows, pairs):
    block = lambda off: pl.BlockSpec((rows, 128), lambda b, h: (b, off * pairs + h))
    start = pl.BlockSpec((1, 1, rows), lambda b, h: (b, 0, 0))
    logsum = pl.BlockSpec((1, 1, rows // PIECE, 2 * PIECE), lambda b, h: (b, h, 0, 0))
    return block, start, logsum


def attend(project, start):
    batches, rows = start.shape[0], start.shape[2]
    width = project.shape[1] // 3
    pairs = width // 128
    block, start_spec, logsum = attend_specs(rows, pairs)
    return pl.pallas_call(
        attend_kernel,
        grid=(batches, pairs),
        in_specs=[block(0), block(1), block(2), start_spec],
        out_specs=[block(0), logsum],
        out_shape=[jax.ShapeDtypeStruct((batches * rows, width), BF16),
                   jax.ShapeDtypeStruct((batches, pairs, rows // PIECE, 2 * PIECE), F32)],
        scratch_shapes=[pltpu.VMEM((sum(h - l for l, _, h in spans(rows)), 2 * PIECE), F32)],
        compiler_params=pltpu.CompilerParams(vmem_limit_bytes=40 * 2 ** 20, dimension_semantics=("arbitrary", "arbitrary")),
        name="attend",
    )(project, project, project, start)


def attend_back_kernel(q_ref, k_ref, v_ref, g_ref, start, logsum, out, bias, k_sum, v_sum):
    rows, wide = q_ref.shape

    @pl.when(pl.program_id(1) == 0)
    def _():
        fill_bias(bias, start[0], rows)

    lanes = lax.broadcasted_iota(jnp.int32, (PIECE, wide), 1) < wide // 2
    at = 0
    k_sum[...] = jnp.zeros_like(k_sum)
    v_sum[...] = jnp.zeros_like(v_sum)
    for i, (low, q, high) in enumerate(spans(rows)):
        n = high - low
        queries = side_by_side(q_ref[q:high, :] * 0.125, lanes)
        grads = side_by_side(g_ref[q:high, :], lanes)
        keys, values = k_ref[low:high, :], v_ref[low:high, :]
        scores = mul(keys, queries, NT) + bias[at:at + n, :]
        full = jnp.exp(scores - logsum[0, 0, i:i + 1, :])
        grad = mul(values, grads, NT)
        v_sum[low:high, :] += mul(full.astype(BF16), grads)
        total = jnp.sum(full * grad, axis=0, keepdims=True)
        grad_scores = (full * (grad - total)).astype(BF16)
        k_sum[low:high, :] += mul(grad_scores, queries)
        both = mul(grad_scores, keys, TN) * 0.125
        out[0, q:high, :] = jnp.where(lanes, both[:PIECE], both[PIECE:]).astype(BF16)
        at += n
    out[1] = k_sum[...].astype(BF16)
    out[2] = v_sum[...].astype(BF16)


def attend_back(project, grad, start, logsum):
    batches, rows = start.shape[0], start.shape[2]
    width = project.shape[1] // 3
    pairs = width // 128
    block, start_spec, logsum_spec = attend_specs(rows, pairs)
    return pl.pallas_call(
        attend_back_kernel,
        grid=(batches, pairs),
        in_specs=[block(0), block(1), block(2), block(0), start_spec, logsum_spec],
        out_specs=pl.BlockSpec((3, rows, 128), lambda b, h: (0, b, h)),
        out_shape=jax.ShapeDtypeStruct((3, batches * rows, width), BF16),
        scratch_shapes=[pltpu.VMEM((sum(h - l for l, _, h in spans(rows)), 2 * PIECE), F32),
                        pltpu.VMEM((rows, 128), F32), pltpu.VMEM((rows, 128), F32)],
        compiler_params=pltpu.CompilerParams(vmem_limit_bytes=40 * 2 ** 20, dimension_semantics=("arbitrary", "arbitrary")),
        name="attend_back",
    )(project, project, project, grad, start, logsum)


class Gather:
    def __init__(self, table, bits, where, shards, fulls, local_sem, send_sem, recv_sem):
        self.table, self.bits, self.steps = table, bits, len(table)
        self.partners = [partner(table, bits, where, k) for k in range(len(table))]
        self.shards, self.fulls = shards, fulls
        self.local_sem, self.send_sem, self.recv_sem = local_sem, send_sem, recv_sem
        two = [o[::-1] for o in orders(table)]
        self.units = in_turn(units_of([s.shape for s in shards]), len(shards) - 2)
        self.chunks = [piece + (two[(h + u) % 2],) for u, unit in enumerate(self.units) for h, piece in enumerate(unit)]
        self.events = timetable(self.units, self.steps, SKEW)
        self.at = 0
        pieces = {i: [e for e in self.events if self.chunks[e[0]][0] == i and e[1] == 1] for i in range(len(shards))}
        self.first = {found[0] for found in pieces.values()}

    def own(self, i):
        return pltpu.make_async_copy(self.shards[i], self.fulls[i].at[tuple(self.bits)], self.local_sem.at[i])

    def copy(self, c, s):
        i, rows, cols, order = self.chunks[c]
        index = tuple(slice(None) if k in order[:s] else self.bits[k] for k in range(self.steps))
        there = self.fulls[i].at[index + (rows, cols)]
        return pltpu.make_async_remote_copy(
            src_ref=self.shards[i].at[rows, cols] if s == 0 else there, dst_ref=there,
            send_sem=self.send_sem.at[c, s], recv_sem=self.recv_sem.at[c, s],
            device_id=self.partners[order[s]], device_id_type=pl.DeviceIdType.MESH)

    def event(self, c, s):
        i = self.chunks[c][0]
        if s > 0:
            self.copy(c, s - 1).wait_recv()
            if (c, s) in self.first:
                self.own(i).wait()
        if s < self.steps:
            self.copy(c, s).start()

    def run(self, count):
        self.some(self.at, self.at + count)
        self.at = min(self.at + count, len(self.events))

    def some(self, low, high):
        for c, s in self.events[low:high]:
            self.event(c, s)

    def needed(self, array, unit):
        piece, last = 0, 0
        seen = -1
        for u in self.units:
            seen += u[0][0] == array
            if u[0][0] == array and seen <= unit:
                ends = [self.events.index((piece + h, self.steps)) for h in range(len(u))]
                last = max(last, max(ends) + 1)
            piece += len(u)
        return max(0, last - self.at)

    def until(self, array, unit):
        self.run(self.needed(array, unit))

    def finish(self):
        self.run(len(self.events))
        for c in range(len(self.chunks)):
            for s in range(self.steps):
                self.copy(c, s).wait_send()


def in_turn(units, first):
    one, two = [u for u in units if u[0][0] == first], [u for u in units if u[0][0] == first + 1]
    return [u for u in units if u[0][0] < first] + [u for pair in zip(one, two) for u in pair] + [u for u in units if u[0][0] > first + 1]


def regroup(src, dst, inward):
    width = src.shape[1]
    groups = 128 // ROWS
    part = lax.broadcasted_iota(jnp.int32, (src.shape[0], 128), 1) // ROWS
    tiles = width // 128 // groups
    for k in range(tiles):
        near = [slice((groups * k + m) * 128, (groups * k + m + 1) * 128) for m in range(groups)]
        far = [slice((m * tiles + k) * 128, (m * tiles + k + 1) * 128) for m in range(groups)]
        source, target = (near, far) if inward else (far, near)
        loaded = [src[:, c].astype(F32) for c in source]
        for a in range(groups):
            tile = loaded[a]
            for b in range(groups):
                turned = loaded[b] if a == b else pltpu.roll(loaded[b], (b - a) * ROWS % 128, 1)
                tile = jnp.where(part == b, turned, tile)
            dst[:, target[a]] = tile.astype(dst.dtype)


def spread(index, slots, engine, count):
    done = 0
    for slot in range(slots):
        upto = count * (slot + 1) // slots
        if upto > done:
            pl.when(index == slot)(functools.partial(engine.run, upto - done))
            done = upto


def row_of(table, offset, width, total):
    owners = table.shape[0]
    lane = lax.broadcasted_iota(jnp.int32, (128, total), 0)
    col = lax.broadcasted_iota(jnp.int32, (128, total), 1)
    pick = jnp.where(lane == offset + col % width, 1.0, 0.0).astype(BF16)
    owner = lax.broadcasted_iota(jnp.int32, (owners, total), 0)
    mine = owner == lax.broadcasted_iota(jnp.int32, (owners, total), 1) // width
    return jnp.sum(jnp.where(mine, mul(table, pick), 0.0), axis=0, keepdims=True)


def rows_at(i, size):
    return pl.ds(pl.multiple_of(i * size, size), size)


def norm_rows(x):
    factor = lax.rsqrt(jnp.mean(x * x, axis=-1, keepdims=True) + EPS)
    return x * factor, factor


def attend_pair(q_ref, k_ref, v_ref, bias, out, logsum):
    rows, wide = q_ref.shape
    lanes = lax.broadcasted_iota(jnp.int32, (PIECE, wide), 1) < wide // 2
    at = 0
    for i, (low, q, high) in enumerate(spans(rows)):
        n = high - low
        queries = side_by_side(q_ref[q:high, :] * 0.125, lanes)
        scores = mul(k_ref[low:high, :], queries, NT) + bias[at:at + n, :]
        peak = jnp.max(scores, axis=0, keepdims=True)
        expo = jnp.exp(scores - peak)
        total = jnp.sum(expo, axis=0, keepdims=True)
        logsum[i:i + 1, :] = peak + jnp.log(total)
        attend_low = (expo * (1.0 / total)).astype(BF16)
        both = mul(attend_low, v_ref[low:high, :], TN)
        out[q:high, :] = jnp.where(lanes, both[:PIECE], both[PIECE:]).astype(BF16)
        at += n


def forward_kernel(table, x_ref, cot_hbm, start, small_s, qkv_s, out_s, down_s, up_as_is,
                   small, qkv, out_w, down, up, project_o, attended_o, entered_o, output_o, middle_o, branch_o, up_g, down_g,
                   logsum, first_row, up_b_g, gain_g, down_b_g,
                   up_s, cot, entered, project, attended, middle, total, back, active, grad_hidden, up_v, down_v, up_gv, down_gv, small_v, rows_v, bias_v, bias,
                   local_sem, send_sem, recv_sem, sems):
    bits, where = my_bits(table)
    steps, owners = len(table), 2 ** len(table)
    rows, width = x_ref.shape
    ff = up_s.shape[1]
    regroup(up_as_is, up_s, True)
    length = start.shape[2]
    pairs = width // 128
    g = Gather(table, bits, where, [small_s, qkv_s, out_s, down_s, up_s], [small, qkv, out_w, down, up], local_sem, send_sem, recv_sem)
    SMALL, QKV, OUT, DOWN, UP = range(5)
    greet(table, bits, where)
    for i in range(5):
        g.own(i).start()

    def move(src, dst, k):
        return pltpu.make_async_copy(src, dst, sems.at[k])

    move(cot_hbm, cot, 0).start()
    g.until(SMALL, 0)
    move(small, small_v, 1).start()
    move(small, small_v, 1).wait()
    held = small_v[...].reshape(owners, small_s.shape[0], 128)
    first_row[...] = row_of(held[:, 1], 0, width // owners, width)
    rows_v[0:1, :] = row_of(held[:, 1], width // owners, width // owners, width)
    rows_v[1:2, :] = row_of(held[:, 1], 2 * (width // owners), width // owners, width)
    blocks = ff // BLOCK
    for j in range(blocks):
        bias_v[:, j * BLOCK:(j + 1) * BLOCK] = row_of(held[:, 0], j * ROWS, ROWS, BLOCK)
    part = 128

    @pl.loop(0, rows // part)
    def _(i):
        at = rows_at(i, part)
        normal, _ = norm_rows(x_ref[at, :].astype(F32))
        entered[at, :] = (normal * first_row[...]).astype(BF16)
    move(entered, entered_o, 2).start()

    for u in range(3):
        g.until(QKV, u)
        fetch = move(qkv.at[(slice(None),) * (steps + 1) + (slice(u * width, (u + 1) * width),)], up_v.at[u % 2], 3)
        fetch.start()
        fetch.wait()

        @pl.loop(0, rows // TALL)
        def _(i):
            at = rows_at(i, TALL)
            project[at, u * width:(u + 1) * width] = mul(entered[at, :], up_v[u % 2].reshape(width, width)).astype(BF16)
            spread_fixed(i, rows // TALL, g, 8)
        g.at += 8
    move(project, project_o, 4).start()
    loops = rows // length * pairs
    slot_events = max(0, g.needed(UP, 0) - 8)

    @pl.loop(0, loops)
    def _(i):
        b, h = i // pairs, i % pairs

        @pl.when(h == 0)
        def _():
            fill_bias(bias, start[b], length)
        at = rows_at(b, length)
        lanes = [pl.ds(pl.multiple_of(k * width + h * 128, 128), 128) for k in range(3)]
        q_ref, k_ref, v_ref = [project.at[at, lane] for lane in lanes]
        attend_pair(q_ref, k_ref, v_ref, bias, attended.at[at, lanes[0]], logsum.at[b, h])
        spread_fixed(i, loops, g, slot_events)
    g.at += slot_events
    move(attended, attended_o, 5).start()
    g.until(OUT, 0)
    fetch = move(out_w, up_v.at[1], 3)
    fetch.start()
    fetch.wait()
    move(entered, entered_o, 2).wait()
    second = entered

    @pl.loop(0, rows // TALL)
    def _(i):
        at = rows_at(i, TALL)
        x = x_ref[at, :].astype(F32) + mul(attended[at, :], up_v[1].reshape(width, width))
        middle[at, :] = x
        normal, _ = norm_rows(x)
        second[at, :] = (normal * rows_v[0:1, :]).astype(BF16)
        spread_fixed(i, rows // TALL, g, 8)
    g.at += 8
    g.until(UP, 0)
    move(cot_hbm, cot, 0).wait()

    def block(up_ref, down_ref, j):
        every = (slice(None),) * steps
        return up_ref.at[every + (slice(None), rows_at(j, BLOCK))], down_ref.at[every + (rows_at(j, ROWS),)]

    def fetches(j, slot):
        one, other = block(up, down, j)
        return [move(one, up_v.at[slot], 6 + slot), move(other, down_v.at[slot], 8 + slot)]

    def stores(j, slot):
        one, other = block(up_g, down_g, j)
        return [move(up_gv.at[slot], one, 10 + slot), move(down_gv.at[slot], other, 12 + slot)]

    deep = (BLOCK // TALL).bit_length() - 1

    def put(ref, slot, i, value):
        there = ref.at[(slot,) + tuple((i // 2 ** (deep - 1 - k)) % 2 for k in range(deep))]
        there[...] = value.reshape(there.shape).astype(BF16)

    for f in fetches(0, 0):
        f.start()
    per = rows // TALL
    marks = [g.at] + [g.at + g.needed(UP, j + 1) for j in range(blocks - 1)]

    def between(j, i, loop, loops):
        for k in range(blocks - 1):
            for n in range(per):
                cut = [marks[k] + (marks[k + 1] - marks[k]) * (loop * per + n + e) // (loops * per) for e in (0, 1)]
                if cut[1] > cut[0]:
                    pl.when(jnp.logical_and(j == k, i == n))(functools.partial(g.some, *cut))

    @pl.loop(0, blocks)
    def _(j):
        slot = j % 2
        for f in fetches(j, slot):
            f.wait()

        @pl.when(j >= 2)
        def _():
            for f in stores(j, slot):
                f.wait()
        lane = rows_at(j, BLOCK)
        bias_row = bias_v[:, lane]
        up_b_g[:, lane] = jnp.zeros((1, BLOCK), F32)

        @pl.loop(0, per)
        def _(i):
            at = rows_at(i, TALL)
            hidden = mul(second[at, :], up_v[slot].reshape(width, BLOCK)) + bias_row
            grad = mul(cot[at, :], down_v[slot].reshape(BLOCK, width), NT)
            half = 0.5 + 0.5 * lax.erf(hidden * (0.5 ** 0.5))
            slope = half + hidden * (jnp.exp(hidden * hidden * -0.5) * 0.3989422804014327)
            active[at, :] = (hidden * half).astype(BF16)
            low = (grad * slope).astype(BF16)
            grad_hidden[at, :] = low
            up_b_g[:, lane] += jnp.sum(low.astype(F32), axis=0, keepdims=True)
            between(j, i, 0, 3)

        @pl.loop(0, per)
        def _(i):
            at = rows_at(i, TALL)
            more, less = mul(active[at, :], down_v[slot].reshape(BLOCK, width)), mul(grad_hidden[at, :], up_v[slot].reshape(width, BLOCK), NT)

            @pl.when(j == 0)
            def _():
                total[at, :] = more
                back[at, :] = less

            @pl.when(j > 0)
            def _():
                total[at, :] += more
                back[at, :] += less
            between(j, i, 1, 3)

        @pl.loop(0, BLOCK // TALL)
        def _(i):
            at = rows_at(i, TALL)
            put(down_gv, slot, i, mul(active[:, at], cot[...], TN))
            between(j, i, 2, 3)

        @pl.when(j + 1 < blocks)
        def _():
            for f in fetches(j + 1, 1 - slot):
                f.start()

        @pl.loop(0, width // TALL)
        def _(i):
            at = rows_at(i, TALL)
            put(up_gv, slot, i, mul(second[:, at], grad_hidden[...], TN))
        for f in stores(j, slot):
            f.start()
    g.at = marks[-1]
    move(attended, attended_o, 5).wait()
    output, branch = entered, attended
    gain_g[...] = jnp.zeros_like(gain_g)
    down_b_g[...] = jnp.zeros_like(down_b_g)

    @pl.loop(0, rows // part)
    def _(i):
        at = rows_at(i, part)
        x = middle[at, :]
        normal, factor = norm_rows(x)
        output[at, :] = (x + (total[at, :] + rows_v[1:2, :])).astype(BF16)
        c = cot[at, :].astype(F32)
        grad = back[at, :]
        gain_g[...] += jnp.sum(grad * normal, axis=0, keepdims=True)
        down_b_g[...] += jnp.sum(c, axis=0, keepdims=True)
        n = grad * rows_v[0:1, :]
        result = c + factor * (n - normal * jnp.mean(n * normal, axis=-1, keepdims=True))
        back[at, :] = result
        branch[at, :] = result.astype(BF16)
    last = [move(output, output_o, 2), move(back, middle_o, 3), move(branch, branch_o, 5)]
    for f in last:
        f.start()
    for f in last + [move(project, project_o, 4)] + stores(blocks - 2, blocks % 2) + stores(blocks - 1, (blocks - 1) % 2):
        f.wait()
    g.finish()


def spread_fixed(index, slots, engine, count):
    begin = engine.at
    spread(index, slots, engine, count)
    engine.at = begin


def forward(frames, cot, start, packed, qkv, out, down, up, sizes, collective_id):
    table = bit_table(sizes)
    steps, owners = len(table), 2 ** len(table)
    rows, width = frames.shape
    ff = up.shape[1]
    batches, length = start.shape[0], start.shape[2]
    pairs = width // 128
    two = (2,) * steps
    shards = [packed, qkv, out, down, up]
    pieces = sum(len(u) for u in units_of([a.shape for a in shards]))
    anywhere, vmem = pl.BlockSpec(memory_space=pl.ANY), pl.BlockSpec(memory_space=pltpu.VMEM)
    hbm_out = [(two + a.shape, BF16) for a in shards] + [((rows, 3 * width), BF16), ((rows, width), BF16), ((rows, width), BF16),
               ((rows, width), BF16), ((rows, width), F32), ((rows, width), BF16), (two + (width // owners, ff), BF16), (two + (ff // owners, width), BF16)]
    vmem_out = [((batches, pairs, length // PIECE, 2 * PIECE), F32), ((1, width), F32), ((1, ff), F32), ((1, width), F32), ((1, width), F32)]
    V = pltpu.VMEM
    return pl.pallas_call(
        functools.partial(forward_kernel, table),
        out_shape=[jax.ShapeDtypeStruct(s, d) for s, d in hbm_out + vmem_out],
        in_specs=[vmem, anywhere] + [vmem] * 6,
        out_specs=[anywhere] * len(hbm_out) + [vmem] * len(vmem_out),
        scratch_shapes=[V(up.shape, BF16), V((rows, width), BF16), V((rows, width), BF16), V((rows, 3 * width), BF16), V((rows, width), BF16), V((rows, width), F32),
                        V((rows, width), F32), V((rows, width), F32), V((rows, BLOCK), BF16), V((rows, BLOCK), BF16),
                        V((2,) + two + (width // owners, BLOCK), BF16), V((2,) + two + (ROWS, width), BF16),
                        V((2,) + two + (width // owners, BLOCK), BF16), V((2,) + two + (ROWS, width), BF16), V(two + packed.shape, BF16), V((2, width), F32), V((1, ff), F32),
                        V((sum(h - l for l, _, h in spans(length)), 2 * PIECE), F32),
                        pltpu.SemaphoreType.DMA((5,)), pltpu.SemaphoreType.DMA((pieces, steps)), pltpu.SemaphoreType.DMA((pieces, steps)),
                        pltpu.SemaphoreType.DMA((14,))],
        compiler_params=pltpu.CompilerParams(collective_id=collective_id, has_side_effects=True, vmem_limit_bytes=58 * 2 ** 20),
        name="forward",
    )(frames, cot, start, *shards)


class Scatter:
    def __init__(self, table, bits, where, parts, outs, recv, stage, small, local_sem, send_sem, recv_sem):
        self.table, self.bits, self.steps = table, bits, len(table)
        self.partners = [partner(table, bits, where, k) for k in range(len(table))]
        self.parts, self.outs, self.recv, self.stage = parts, outs, recv, stage
        self.local_sem, self.send_sem, self.recv_sem = local_sem, send_sem, recv_sem
        self.small_recv = small
        self.units, self.chunks = scatter_chunks(table, [p.shape[-2:] for p in parts])
        self.events = timetable(self.units, self.steps, SKEW)
        self.at = 0

    def into(self, c, s):
        if self.chunks[c][0] == len(self.parts) - 1:
            return self.small_recv[s]
        return self.recv[s].at[c]

    def half(self, c, bit):
        i, rows, cols, order = self.chunks[c]
        index = tuple(bit if k == order[0] else slice(None) for k in range(self.steps))
        return self.parts[i].at[index + (rows, cols)]

    def load(self, c):
        return pltpu.make_async_copy(self.half(c, self.bits[self.chunks[c][3][0]]), self.stage.at[c % 4], self.local_sem.at[c % 4])

    def left(self, c, s, last):
        order, out = self.chunks[c][3], []
        for k in range(self.steps):
            if k == order[0]:
                continue
            if k in order[1:s]:
                out.append(self.bits[k])
            elif s < self.steps and k == order[s] and last is not None:
                out.append(last)
            else:
                out.append(slice(None))
        return tuple(out)

    def copy(self, c, s):
        k = self.chunks[c][3][s]
        other = 1 - self.bits[k]
        return pltpu.make_async_remote_copy(
            src_ref=self.half(c, other) if s == 0 else self.into(c, 0).at[self.left(c, s, other)], dst_ref=self.into(c, s),
            send_sem=self.send_sem.at[c, s], recv_sem=self.recv_sem.at[c, s],
            device_id=self.partners[k], device_id_type=pl.DeviceIdType.MESH)

    def add(self, c, s):
        i, rows, cols, order = self.chunks[c]
        small = i == len(self.parts) - 1
        total, got = self.into(c, 0), self.into(c, s)
        free = self.steps - s - 1
        if free == 0:
            own = total[self.left(c, self.steps, None)]
            self.outs[i][rows, cols] = own.astype(F32) + got[...].astype(F32)
            return
        base = self.left(c, s, self.bits[order[s]]) if s else (slice(None),) * free
        mine = self.half(c, self.bits[order[0]]) if small else self.stage.at[c % 4]

        @pl.loop(0, 2 ** free)
        def _(j):
            spot = [(j // 2 ** (free - 1 - b)) % 2 for b in range(free)]
            rest = iter(spot)
            here = tuple(next(rest) if isinstance(e, slice) else e for e in base)
            more = mine[tuple(spot)] if s == 0 else got[tuple(spot)]
            total[here] = (total[here].astype(F32) + more.astype(F32)).astype(total.dtype)

    def event(self, c, s):
        small = self.chunks[c][0] == len(self.parts) - 1
        if s == 0:
            self.copy(c, 0).start()
            if not small:
                self.load(c).start()
            return
        self.copy(c, s - 1).wait_recv()
        if s == 1 and not small:
            self.load(c).wait()
        self.add(c, s - 1)
        if s < self.steps:
            self.copy(c, s).start()

    def run(self, count):
        for c, s in self.events[self.at:self.at + count]:
            self.event(c, s)
        self.at = min(self.at + count, len(self.events))

    def before(self, part):
        return next(n for n, (c, s) in enumerate(self.events) if self.chunks[c][0] == part)

    def finish(self):
        self.run(len(self.events))
        for c in range(len(self.chunks)):
            for s in range(self.steps):
                self.copy(c, s).wait_send()


def scatter_chunks(table, tails):
    two = orders(table)
    units = in_turn(units_of(tails), 0)
    return units, [piece + (two[(h + u) % 2],) for u, unit in enumerate(units) for h, piece in enumerate(unit)]


def attend_back_pair(q_ref, k_ref, v_ref, g_ref, bias, logsum, k_sum, v_sum):
    rows, wide = q_ref.shape
    lanes = lax.broadcasted_iota(jnp.int32, (PIECE, wide), 1) < wide // 2
    at = 0
    k_sum[...] = jnp.zeros_like(k_sum)
    v_sum[...] = jnp.zeros_like(v_sum)
    for i, (low, q, high) in enumerate(spans(rows)):
        n = high - low
        queries = side_by_side(q_ref[q:high, :] * 0.125, lanes)
        grads = side_by_side(g_ref[q:high, :], lanes)
        keys, values = k_ref[low:high, :], v_ref[low:high, :]
        scores = mul(keys, queries, NT) + bias[at:at + n, :]
        full = jnp.exp(scores - logsum[i:i + 1, :])
        grad = mul(values, grads, NT)
        v_sum[low:high, :] += mul(full.astype(BF16), grads)
        total = jnp.sum(full * grad, axis=0, keepdims=True)
        grad_scores = (full * (grad - total)).astype(BF16)
        k_sum[low:high, :] += mul(grad_scores, queries)
        both = mul(grad_scores, keys, TN) * 0.125
        q_ref[q:high, :] = jnp.where(lanes, both[:PIECE], both[PIECE:]).astype(BF16)
        at += n
    k_ref[...] = k_sum[...].astype(BF16)
    v_ref[...] = v_sum[...].astype(BF16)


def by_owner(row, offset, owners):
    total = row.shape[1]
    width = total // owners
    lane = lax.broadcasted_iota(jnp.int32, (128, total), 0)
    col = lax.broadcasted_iota(jnp.int32, (128, total), 1)
    pick = jnp.where(lane == offset + col % width, 1.0, 0.0)
    owner = lax.broadcasted_iota(jnp.int32, (owners, total), 0)
    mine = owner == lax.broadcasted_iota(jnp.int32, (owners, total), 1) // width
    return lax.dot_general(jnp.where(mine, row, 0.0), pick, NT, precision=lax.Precision.HIGHEST, preferred_element_type=F32)


def backward_kernel(table, x_hbm, start, project_hbm, attended_hbm, entered_hbm, middle_hbm, branch_hbm, qkv, out_w, up_g, down_g,
                    logsum, first_row, up_b_g, gain_g, down_b_g,
                    grad_o, out_g, q_g, k_g, v_g, up_o, down_r, out_r, qkv_r, small_r,
                    project, attended, branch, entered, weight, held, back, old, bias, k_sum, v_sum, small, stage,
                    up_r, r0, r1, r2, r3, r4, s0, s1, s2, s3, s4, local_sem, send_sem, recv_sem, sems):
    bits, where = my_bits(table)
    steps, owners = len(table), 2 ** len(table)
    rows, width = attended.shape
    length = start.shape[2]
    pairs = width // 128
    e = Scatter(table, bits, where, [up_g, down_g, out_g, q_g, k_g, v_g, small], [up_r, down_r, out_r, *[qkv_r.at[:, u * width:(u + 1) * width] for u in range(3)], small_r],
                [r0, r1, r2, r3, r4], stage, [s0, s1, s2, s3, s4], local_sem, send_sem, recv_sem)

    def move(src, dst, k):
        return pltpu.make_async_copy(src, dst, sems.at[k])

    for args in ((attended_hbm, attended, 0), (branch_hbm, branch, 1), (out_w, weight.at[0], 2), (project_hbm, project, 3), (entered_hbm, entered, 4)):
        move(*args).start()
    greet(table, bits, where)
    first_q = e.before(3)
    e.run(2)
    move(attended_hbm, attended, 0).wait()
    move(branch_hbm, branch, 1).wait()
    per = rows // TALL
    deep = (width // TALL).bit_length() - 1

    def place(slot, i):
        return held.at[(slot,) + tuple((i // 2 ** (deep - 1 - k)) % 2 for k in range(deep))]

    def put(slot, i, value):
        ref = place(slot, i)
        ref[...] = value.reshape(ref.shape).astype(BF16)

    @pl.loop(0, width // TALL)
    def _(i):
        put(0, i, mul(attended[:, rows_at(i, TALL)], branch[...], TN))
        spread_fixed(i, width // TALL, e, 4)
    e.at += 4
    move(held.at[0], out_g, 5).start()
    move(out_w, weight.at[0], 2).wait()

    @pl.loop(0, per)
    def _(i):
        at = rows_at(i, TALL)
        branch[at, :] = mul(branch[at, :], weight[0].reshape(width, width), NT).astype(BF16)
        spread_fixed(i, per, e, 4)
    e.at += 4
    move(x_hbm, attended, 0).start()
    move(project_hbm, project, 3).wait()
    move(held.at[0], out_g, 5).wait()
    loops = rows // length * pairs
    count = first_q - e.at - 12

    @pl.loop(0, loops)
    def _(i):
        b, h = i // pairs, i % pairs

        @pl.when(h == 0)
        def _():
            fill_bias(bias, start[b], length)
        at = rows_at(b, length)
        lanes = [pl.ds(pl.multiple_of(k * width + h * 128, 128), 128) for k in range(3)]
        q_ref, k_ref, v_ref = [project.at[at, lane] for lane in lanes]
        attend_back_pair(q_ref, k_ref, v_ref, branch.at[at, lanes[0]], bias, logsum.at[b, h], k_sum, v_sum)
        spread_fixed(i, loops, e, count)
    e.at += count
    move(entered_hbm, entered, 4).wait()

    def fetch(u):
        return move(qkv.at[(slice(None),) * (steps + 1) + (slice(u * width, (u + 1) * width),)], weight.at[(u + 1) % 2], 6 + u % 2)

    fetch(0).start()
    fetch(1).start()
    for u, part in enumerate((q_g, k_g, v_g)):
        slot = (u + 1) % 2
        if u == 2:
            move(held.at[slot], q_g, 8).wait()

        @pl.loop(0, width // TALL)
        def _(i):
            put(slot, i, mul(entered[:, rows_at(i, TALL)], project[:, u * width:(u + 1) * width], TN))
            spread_fixed(i, width // TALL, e, 4)
        e.at += 4
        move(held.at[slot], part, 8 + u).start()
    for u, part in enumerate((q_g, k_g, v_g)):
        if u:
            move(held.at[(u + 1) % 2], part, 8 + u).wait()
    mark = e.before(6)
    each = (mark - e.at) // 3
    for u in range(3):
        fetch(u).wait()

        @pl.loop(0, per)
        def _(i):
            at = rows_at(i, TALL)
            more = mul(project[at, u * width:(u + 1) * width], weight[(u + 1) % 2].reshape(width, width), NT)
            if u == 0:
                back[at, :] = more
            else:
                back[at, :] += more
            spread_fixed(i, per, e, each)
        e.at += each
        if u == 0:
            fetch(2).start()
    move(x_hbm, attended, 0).wait()
    part = old.shape[1]
    first_g = jnp.zeros((1, width), F32)

    def older(i):
        return move(middle_hbm.at[rows_at(i, part), :], old.at[i % 2], 11 + i % 2)

    older(0).start()

    @pl.loop(0, rows // part, init_carry=first_g)
    def first_g(i, first_g):
        @pl.when(i + 1 < rows // part)
        def _():
            older(i + 1).start()
        older(i).wait()
        at = rows_at(i, part)
        normal, factor = norm_rows(attended[at, :].astype(F32))
        grad = back[at, :]
        n = grad * first_row[...]
        back[at, :] = old[i % 2] + factor * (n - normal * jnp.mean(n * normal, axis=-1, keepdims=True))
        return first_g + jnp.sum(grad * normal, axis=0, keepdims=True)
    move(back, grad_o, 13).start()
    share = width // owners
    zero = jnp.zeros((owners, 6, 128), F32)
    vectors = by_owner(first_g, 0, owners) + by_owner(gain_g[...], share, owners) + by_owner(down_b_g[...], 2 * share, owners)
    long = sum(by_owner(up_b_g[:, j * BLOCK:(j + 1) * BLOCK], j * ROWS, owners) for j in range(up_b_g.shape[1] // BLOCK))
    packed = jnp.concatenate([long[:, None], vectors[:, None], zero], axis=1)
    small[...] = packed.reshape(small.shape)
    e.finish()
    regroup(up_r, up_o, False)
    move(back, grad_o, 13).wait()


def backward(frames, start, project, attended, entered, middle, branch, qkv, out_w, up_g, down_g, logsum, first_row, up_b_g, gain_g, down_b_g,
             sizes, collective_id):
    table = bit_table(sizes)
    steps, owners = len(table), 2 ** len(table)
    rows, width = frames.shape
    length = start.shape[2]
    two = (2,) * steps
    share = width // owners
    small = (8, 128)
    tails = [up_g.shape[-2:], down_g.shape[-2:]] + [(share, width)] * 4 + [small]
    units, chunks = scatter_chunks(table, tails)
    m = len(chunks)
    piece = (min(ROWS, share), WIDE)
    anywhere, vmem = pl.BlockSpec(memory_space=pl.ANY), pl.BlockSpec(memory_space=pltpu.VMEM)
    V = pltpu.VMEM
    out_shape = [((rows, width), F32)] + [(two + (share, width), BF16)] * 4 + [(t, F32) for t in (*tails[:3], (share, 3 * width), small)]
    return pl.pallas_call(
        functools.partial(backward_kernel, table),
        out_shape=[jax.ShapeDtypeStruct(s, d) for s, d in out_shape],
        in_specs=[anywhere, vmem] + [anywhere] * 9 + [vmem] * 5,
        out_specs=[anywhere] * 5 + [vmem] * 5,
        scratch_shapes=[V((rows, 3 * width), BF16), V((rows, width), BF16), V((rows, width), BF16), V((rows, width), BF16),
                        V((2,) + two + (share, width), BF16), V((2,) + two + (share, width), BF16), V((rows, width), F32), V((2, 128, width), F32),
                        V((sum(h - l for l, _, h in spans(length)), 2 * PIECE), F32), V((length, 128), F32), V((length, 128), F32),
                        V(two + small, F32), V((4,) + two[1:] + piece, BF16)]
        + [V(tails[0], F32)] + [V((m - 1,) + two[s + 1:] + piece, BF16) for s in range(steps)] + [V(two[s + 1:] + small, F32) for s in range(steps)]
        + [pltpu.SemaphoreType.DMA((4,)), pltpu.SemaphoreType.DMA((m, steps)), pltpu.SemaphoreType.DMA((m, steps)), pltpu.SemaphoreType.DMA((14,))],
        compiler_params=pltpu.CompilerParams(collective_id=collective_id, has_side_effects=True, vmem_limit_bytes=60 * 2 ** 20),
        name="backward",
    )(frames, start, project, attended, entered, middle, branch, qkv, out_w, up_g, down_g, logsum, first_row, up_b_g, gain_g, down_b_g)


def pack(first, second, up_b, down_b):
    rest = jnp.concatenate([first, second, down_b])
    rest = jnp.pad(rest, (0, 128 - rest.shape[0]))
    return jnp.pad(jnp.stack([jnp.pad(up_b, (0, 128 - up_b.shape[0])), rest]), ((0, 14), (0, 0)))


def fits(sizes, shards):
    return all(s & (s - 1) == 0 for s in sizes.values()) and all(a.shape[0] % ROWS == 0 for a in shards) and sizes["dp"] * sizes["fsdp"] * ROWS == BLOCK


def item_starts(lengths, rows):
    slots = jnp.arange(lengths.shape[1], dtype=jnp.int32)
    ends = jnp.sum(jnp.where(slots[None, :, None] <= slots[None, None, :], lengths[:, :, None], 0), axis=1)
    position = jnp.arange(rows, dtype=jnp.int32)[None, None, :]
    return jnp.max(jnp.where(ends[:, :, None] <= position, ends[:, :, None], 0), axis=1, keepdims=True)


def normalize(x_val):
    factor = lax.rsqrt(jnp.mean(x_val * x_val, axis=-1, keepdims=True) + EPS)
    return (x_val * factor, factor)


def norm_back(normal, factor, gain, grad_out):
    gain_grad = jnp.sum(grad_out * normal, axis=0)
    scaled = grad_out * gain
    inner = jnp.mean(scaled * normal, axis=-1, keepdims=True)
    return (factor * (scaled - normal * inner), gain_grad)


def block_pass(frames, lengths, cotangent, params, sum_type):
    first, qkv, out, second, up, up_b, down, down_b = params
    batches, rows, width = frames.shape
    x_val = frames.reshape(batches * rows, width).astype(F32)
    cot = cotangent.reshape(batches * rows, width)
    start = item_starts(lengths, rows)
    normal, factor = normalize(x_val)
    gain = first.astype(F32)
    entered = (normal * gain).astype(BF16)
    project = mul(entered, qkv).astype(BF16)
    attended, logsum = attend(project, start)
    middle = x_val + mul(attended, out)
    output, grad_middle, grad_branch, up_g, down_g, up_b_g, second_g, down_b_g = mlp(middle, cot, second, up, up_b, down, down_b, sum_type)
    out_g = mul(attended, grad_branch, TN)
    grad_attended = mul(grad_branch, out, NT).astype(BF16)
    grads = attend_back(project, grad_attended, start, logsum)
    qkv_g = [mul(entered, grads[j], TN) for j in range(3)]
    grad_entered = sum(mul(grads[j], qkv[:, j * width:(j + 1) * width], NT) for j in range(3))
    back, first_g = norm_back(normal, factor, gain, grad_entered)
    shape = frames.shape
    return (output.reshape(shape), (grad_middle + back).reshape(shape), (down_g, up_g, out_g, *qkv_g),
            (first_g, second_g.reshape(-1), up_b_g.reshape(-1), down_b_g.reshape(-1)))


def body(sizes, frames, lengths, cotangent, *shards):
    weights = [shards[i] for i in (1, 2, 4, 6)]
    vectors = [shards[i] for i in (0, 3, 5, 7)]
    shape = frames.shape
    if fits(sizes, weights):
        qkv_s, out_s, up_s, down_s = weights
        flat = (shape[0] * shape[1], shape[2])
        x_val, cot = frames.reshape(flat), cotangent.reshape(flat)
        start = item_starts(lengths[:, 0], shape[1])
        (_, qkv, out, _, _, project, attended, entered, output, middle, branch, up_g, down_g, logsum, first, up_b_g, second_g, down_b_g) = forward(
            x_val, cot, start, pack(*vectors), qkv_s, out_s, down_s, up_s, sizes, 1)
        frames_grad, _, _, _, _, up_g, down_g, out_g, qkv_g, small = backward(
            x_val, start, project, attended, entered, middle, branch, qkv, out, up_g, down_g, logsum, first, up_b_g, second_g, down_b_g, sizes, 2)
        output, frames_grad = output.reshape(shape), frames_grad.reshape(shape)
        share = vectors[0].shape[0]
        first_g, second_g, down_b_g = [small[1, k * share:(k + 1) * share] for k in range(3)]
        up_b_g = small[0, :vectors[2].shape[0]]
    else:
        qkv, out, up, down = [lax.all_gather(w, AXES, axis=0, tiled=True) for w in weights]
        first, second, up_b, down_b = [lax.all_gather(v, AXES, axis=0, tiled=True) for v in vectors]
        params = (first, qkv, out, second, up, up_b, down, down_b)
        output, frames_grad, big, small = block_pass(frames, lengths[:, 0], cotangent, params, F32)
        down_g, up_g, out_g, *qkv_g = [lax.psum_scatter(g, AXES, scatter_dimension=0, tiled=True) for g in big]
        qkv_g = jnp.concatenate(qkv_g, axis=1)
        first_g, second_g, up_b_g, down_b_g = [lax.psum_scatter(g, AXES, scatter_dimension=0, tiled=True) for g in small]
    return (output, frames_grad, first_g, qkv_g, out_g, second_g, up_g, up_b_g, down_g, down_b_g)


def solution(mesh):
    in_specs = (
        P(None, ("dp", "fsdp"), None),
        P(None, ("dp", "fsdp"), None),
        P(None, ("dp", "fsdp"), None),
        P(("dp", "fsdp")),
        P(("dp", "fsdp"), None),
        P(("dp", "fsdp"), None),
        P(("dp", "fsdp")),
        P(("dp", "fsdp"), None),
        P(("dp", "fsdp")),
        P(("dp", "fsdp"), None),
        P(("dp", "fsdp")),
    )
    out_specs = (
        P(None, ("dp", "fsdp"), None),
        P(None, ("dp", "fsdp"), None),
        P(("dp", "fsdp")),
        P(("dp", "fsdp"), None),
        P(("dp", "fsdp"), None),
        P(("dp", "fsdp")),
        P(("dp", "fsdp"), None),
        P(("dp", "fsdp")),
        P(("dp", "fsdp"), None),
        P(("dp", "fsdp")),
    )
    return jax.shard_map(functools.partial(body, dict(mesh.shape)), mesh=mesh, in_specs=in_specs, out_specs=out_specs, check_vma=False)
```
